32 devices in a mesh: rep: 8 (over y, x, core), shard: 4 (over z).
Axes of the slice: x: 2, y: 2, z: 4, core: 2. Of those that a mesh axis runs over, the one named last changes fastest.
Arguments:
- hidden_in: bfloat16 [16384, 960], P(('rep', 'shard')), may hold values from -6 to 6
- cotangent: bfloat16 [16384, 960], P(('rep', 'shard')), may hold values from -6 to 6
- destination: int32 [16384], P(('rep', 'shard')), may hold values from 0 to 16383, as said below
- seq_lengths: int32 [4, 8], P('shard'), may hold values from 1 to 3584, 3840 in all within a row
- gate_mask: int32 [16384], P(('rep', 'shard')), may hold values 0 or 1
- query_weight: bfloat16 [960, 960], P('shard'), may hold values from -0.1875 to 0.1875
- key_matrix: bfloat16 [960, 320], P('shard'), may hold values from -0.1875 to 0.1875
- value_matrix: bfloat16 [960, 320], P('shard'), may hold values from -0.1875 to 0.1875
- out_weight: bfloat16 [960, 960], P('shard'), may hold values from -0.75 to 0.75
- gate_weight: bfloat16 [960, 2560], P('shard'), may hold values from -0.1875 to 0.1875
- up_weight: bfloat16 [960, 2560], P('shard'), may hold values from -0.1875 to 0.1875
- down_weight: bfloat16 [2560, 960], P('shard'), may hold values from -0.125 to 0.125
- attn_gain: bfloat16 [960], P('shard'), may hold values from 0.099609375 to 1.8984375
- ffn_gain: bfloat16 [960], P('shard'), may hold values from 0.099609375 to 1.8984375
- router_weight: bfloat16 [960], P('shard'), may hold values from -0.1875 to 0.1875
Outputs:
- outputs: bfloat16 [16384, 960], P(('rep', 'shard'))
- hidden_grad: bfloat16 [16384, 960], P(('rep', 'shard'))
- query_weight_grad: float32 [960, 960], P('shard')
- key_weight_grad: float32 [960, 320], P('shard')
- value_weight_grad: float32 [960, 320], P('shard')
- out_weight_grad: float32 [960, 960], P('shard')
- gate_weight_grad: float32 [960, 2560], P('shard')
- up_weight_grad: float32 [960, 2560], P('shard')
- down_weight_grad: float32 [2560, 960], P('shard')
- attn_gain_grad: float32 [960], P('shard')
- ffn_gain_grad: float32 [960], P('shard')
- router_weight_grad: float32 [960], P('shard')
The draws below stay inside these ranges and needn't reach their ends.
Inputs may be any that keep to these rules, and one draw needn't show every extreme that they name: Each balanced position is the destination of exactly one token, and each device's 512 initial tokens go exactly 16 to each device's block of 512 balanced positions. `seq_lengths`: each line's lengths sum to 3840; the line's last 256 places are padding; the longest is 3584.
All inputs are finite; a program needn't handle non-finite values. No bound on the sum of `gate_mask` on one device may be relied on, other than what follows from the above.
Results may differ from the reference program's by a relative error of at most 0.023.
Values may be sent and summed in bfloat16 or wider, within the bound.
A program may use at most 192 MiB of HBM per device.

```python
import math
import jax
import jax.numpy as jnp
import numpy as np
from jax import lax

MODEL_DIM = 960
QUERY_HEADS = 15
KEY_VALUE_HEADS = 5
HEAD_DIM = 64
FF = 2560
TOK_DEV = 512
SEQS = 8
LINES = 4
DEVS = 32
PAIR = 16
TOKENS = 16384
LONGEST = 3584
FILLED = 3840
N_REP = 8
N_SHARD = 4


def draw_destination(key, part):
    base_key = jax.random.fold_in(key, 11)
    order_keys = jax.random.split(base_key, 2)
    local_order = jax.vmap(lambda sub_key: jax.random.permutation(sub_key, TOK_DEV))(jax.random.split(order_keys[0], DEVS)).astype(jnp.int32)
    sent_order = jax.vmap(lambda sub_key: jax.random.permutation(sub_key, TOK_DEV))(jax.random.split(order_keys[1], DEVS)).astype(jnp.int32)
    source = local_order // PAIR
    rank_in = local_order % PAIR
    target_dev = jnp.arange(DEVS, dtype=jnp.int32)[:, None]
    column = target_dev * PAIR + rank_in
    anchor = source * TOK_DEV + sent_order[source, column]
    balanced = target_dev * TOK_DEV + jnp.arange(TOK_DEV, dtype=jnp.int32)[None, :]
    return jnp.zeros((TOKENS,), jnp.int32).at[anchor.reshape(-1)].set(balanced.reshape(-1).astype(jnp.int32))


def set_ends(array, rng, smallest, top_value):
    longest = array.shape.index(max(array.shape))
    spots = []
    for shift in (0, 1):
        where = [jax.random.randint(jax.random.fold_in(rng, axis), (), 0, length) for axis, length in enumerate(array.shape)]
        where[longest] = (where[longest] + shift) % array.shape[longest]
        spots.append(tuple(where))
    return array.at[spots[0]].set(smallest).at[spots[1]].set(top_value)


def level_of(key, shape, shards, smallest, top_value):
    gain, own = 1.0, jax.random.fold_in(key, 6)
    for position, shards_of in shards:
        steps = jnp.exp(jax.random.uniform(jax.random.fold_in(own, position), (shards_of,), jnp.float32, smallest / len(shards), top_value / len(shards)))
        gain = gain * jnp.repeat(steps, shape[position] // shards_of).reshape([-1 if axis == position else 1 for axis in range(len(shape))])
    return gain


def length_profile(number_of, total, limit, slope):
    portions = [(1 << 20) // math.isqrt(rank ** slope) + 1 for rank in range(2, number_of + 1)]
    rest, holding = total - limit - (number_of - 1), [1] * (number_of - 1)
    while rest > 0:
        free = [i for i in range(number_of - 1) if holding[i] < limit]
        mass, left = sum([portions[i] for i in free]), rest
        for i in free:
            addition = min(limit - holding[i], max(1, left * portions[i] // mass), rest)
            holding[i] = holding[i] + addition
            rest = rest - addition
    return np.array([limit] + holding)


def ragged(stream_key, number_of, total, limit, lean):
    if number_of == 2:
        one = jax.random.randint(stream_key, (), max(1, total - limit), min(limit, total - 1) + 1)
        return jnp.stack([one, total - one])
    tallies = jnp.asarray(length_profile(number_of, total, limit, lean), jnp.int32)
    couples = (number_of - 1) // 2
    donor, sink = tallies[1:1 + 2 * couples:2], tallies[2:2 + 2 * couples:2]
    slack = jnp.minimum(donor - 1, limit - sink)
    moved = jax.random.randint(jax.random.fold_in(stream_key, 1), (couples,), 0, 1 << 20) % (slack + 1)
    tallies = tallies.at[1:1 + 2 * couples:2].set(donor - moved).at[2:2 + 2 * couples:2].set(sink + moved)
    return tallies[jax.random.permutation(jax.random.fold_in(stream_key, 2), number_of)]


def noise(key, extent, scale, most, shards=(), kind=jnp.bfloat16):
    result = jax.random.normal(key, extent, jnp.float32) * scale
    if len(shards) > 0:
        result = level_of(key, extent, shards, -0.22, 0.18) * result
    return jnp.clip(result, min=-most, max=most).astype(kind)


def setup_inputs(seed: int = 0) -> dict:
    seeds = jax.random.split(jax.random.key(seed), 16)
    hidden_in = noise(seeds[0], (TOKENS, MODEL_DIM), 1.0, 6.0, ((0, 32),))
    cotangent = noise(seeds[1], (TOKENS, MODEL_DIM), 1.0, 6.0, ((0, 32),))
    destination = draw_destination(jax.random.fold_in(seeds[15], 71), 0)
    seq_lengths = jax.vmap(lambda own: ragged(own, SEQS, FILLED, LONGEST, 2))(jax.random.split(seeds[3], LINES)).reshape((LINES, SEQS)).astype(jnp.int32)
    gate_mask = set_ends((jax.random.randint(seeds[4], (TOKENS,), 0, 4) < 3).astype(jnp.int32), jax.random.fold_in(seeds[4], 1), 0, 1)
    query_weight = noise(seeds[5], (MODEL_DIM, MODEL_DIM), MODEL_DIM ** -0.5, 0.1875, ((0, 4),))
    key_matrix = noise(seeds[6], (MODEL_DIM, KEY_VALUE_HEADS * HEAD_DIM), MODEL_DIM ** -0.5, 0.1875, ((0, 4),))
    value_matrix = noise(seeds[7], (MODEL_DIM, KEY_VALUE_HEADS * HEAD_DIM), MODEL_DIM ** -0.5, 0.1875, ((0, 4),))
    out_weight = noise(seeds[8], (MODEL_DIM, MODEL_DIM), (MODEL_DIM // 16) ** -0.5, 0.75, ((0, 4),))
    gate_weight = noise(seeds[9], (MODEL_DIM, FF), MODEL_DIM ** -0.5, 0.1875, ((0, 4),))
    up_weight = noise(seeds[10], (MODEL_DIM, FF), MODEL_DIM ** -0.5, 0.1875, ((0, 4),))
    down_weight = noise(seeds[11], (FF, MODEL_DIM), FF ** -0.5, 0.125, ((0, 4),))
    attn_gain = jnp.clip(1.0 + 0.18 * jax.random.normal(seeds[12], (MODEL_DIM,), jnp.float32), 0.099609375, 1.8984375).astype(jnp.bfloat16)
    ffn_gain = jnp.clip(1.0 + 0.18 * jax.random.normal(seeds[13], (MODEL_DIM,), jnp.float32), 0.099609375, 1.8984375).astype(jnp.bfloat16)
    router_weight = noise(seeds[14], (MODEL_DIM,), MODEL_DIM ** -0.5, 0.1875, ((0, 4),))
    return dict(hidden_in=hidden_in, cotangent=cotangent, destination=destination, seq_lengths=seq_lengths, gate_mask=gate_mask, query_weight=query_weight, key_matrix=key_matrix, value_matrix=value_matrix, out_weight=out_weight, gate_weight=gate_weight, up_weight=up_weight, down_weight=down_weight, attn_gain=attn_gain, ffn_gain=ffn_gain, router_weight=router_weight)


EPSILON = 1e-05
NEGATIVE_HUGE = -1e+30
ROPE_BASE = 10000.0

@jax.custom_vjp
def reduced_float(v):
    return lax.optimization_barrier(v.astype(jnp.bfloat16)).astype(jnp.float32)

@jax.custom_vjp
def reduced_float_back(v):
    return v

def low_keep(v):
    return (reduced_float(v), None)

def low_pass(kept, grad):
    return (grad,)

def back_keep(v):
    return (v, None)

def back_low(kept, grad):
    return (reduced_float(grad),)
reduced_float.defvjp(low_keep, low_pass)
reduced_float_back.defvjp(back_keep, back_low)

def rms_scale(value_rows, gain_vec):
    return value_rows * lax.rsqrt(lax.optimization_barrier(jnp.mean(value_rows * value_rows, axis=-1, keepdims=True)) + EPSILON) * gain_vec

def apply_rotary(value_rows, rotary_angles):
    middle = value_rows.shape[-1] // 2
    leading = value_rows[..., :middle]
    trailing = value_rows[..., middle:]
    cosines = jnp.cos(rotary_angles)[:, None, :]
    sine_part = jnp.sin(rotary_angles)[:, None, :]
    return jnp.concatenate([leading * cosines - trailing * sine_part, trailing * cosines + leading * sine_part], axis=-1)

def rope_angles(within, head_size):
    steps_idx = jnp.arange(head_size // 2).astype(jnp.float32)
    frequency = jnp.power(ROPE_BASE, -2.0 * steps_idx / head_size)
    return within.astype(jnp.float32)[:, None] * frequency[None, :]

def line_layout(lengths_row, positions):
    seq_ends = jnp.cumsum(lengths_row, dtype=jnp.int32)
    reached = seq_ends[None, :] <= positions[:, None]
    segment = lax.optimization_barrier(jnp.sum(reached.astype(jnp.int32), axis=1)).astype(jnp.int32)
    starts = lax.optimization_barrier(jnp.max(jnp.where(reached, seq_ends[None, :], 0), axis=1)).astype(jnp.int32)
    within = (positions - starts).astype(jnp.int32)
    is_valid = positions < seq_ends[-1]
    return (segment, within, is_valid)

def to_lines(value_rows):
    shaped = value_rows.reshape((N_REP, N_SHARD, TOK_DEV) + value_rows.shape[1:])
    return jnp.swapaxes(shaped, 0, 1).reshape((N_SHARD, N_REP * TOK_DEV) + value_rows.shape[1:])

def from_lines(value_rows):
    shaped = value_rows.reshape((N_SHARD, N_REP, TOK_DEV) + value_rows.shape[2:])
    return jnp.swapaxes(shaped, 0, 1).reshape((N_SHARD * N_REP * TOK_DEV,) + value_rows.shape[2:])

def attend(query_batch, key_batch, value_batch, segment, key_code):
    sequence_rows = query_batch.shape[0]
    block_rows = math.gcd(sequence_rows, 512)
    count_blocks = sequence_rows // block_rows
    positions = jnp.arange(sequence_rows, dtype=jnp.int32)
    score_scale = HEAD_DIM ** (-0.5)

    def block_fn(block_items):
        query_block_tile, query_pos, code_blk = block_items
        unscaled_scores = jnp.einsum('bnae,lne->nabl', query_block_tile, key_batch, precision=lax.Precision.HIGHEST)
        scores = reduced_float_back(unscaled_scores) * score_scale
        allowed = (positions[None, :] == query_pos[:, None]) | (key_code[None, :] == code_blk[:, None]) & (positions[None, :] <= query_pos[:, None])
        scores = jnp.where(allowed[None, None], scores, NEGATIVE_HUGE)
        row_max = lax.optimization_barrier(jnp.max(scores, axis=-1, keepdims=True))
        log_sum = row_max + jnp.log(lax.optimization_barrier(jnp.sum(jnp.exp(scores - row_max), axis=-1, keepdims=True)))
        softmax_probabilities = reduced_float(jnp.exp(scores - log_sum))
        return jnp.einsum('impq,qil->piml', softmax_probabilities, value_batch, precision=lax.Precision.HIGHEST)
    block_items = (query_batch.reshape((count_blocks, block_rows) + query_batch.shape[1:]), positions.reshape(count_blocks, block_rows), segment.reshape(count_blocks, block_rows))
    line_outs = lax.map(jax.checkpoint(block_fn), block_items)
    return line_outs.reshape((sequence_rows,) + query_batch.shape[1:])

def line_forward(line_items, weights):
    hidden, active_line, segment_line, code_line, angle_sequence = line_items
    query_w, key_w, value_projection, out_w, gate_w, up_w, down_w, gain_one, gain_two, router_w = weights
    sequence_rows = hidden.shape[0]
    maximum_precision = lax.Precision.HIGHEST
    first_normalized = reduced_float(rms_scale(hidden, gain_one))
    gate_value = jax.nn.sigmoid(jnp.dot(hidden, router_w, precision=maximum_precision))
    branch_scale = active_line.astype(hidden.dtype) * gate_value
    query_before_rotary = reduced_float_back(jnp.dot(first_normalized, query_w, precision=maximum_precision))
    query_batch = reduced_float(apply_rotary(query_before_rotary.reshape(sequence_rows, QUERY_HEADS, HEAD_DIM), angle_sequence)).reshape(sequence_rows, KEY_VALUE_HEADS, QUERY_HEADS // KEY_VALUE_HEADS, HEAD_DIM)
    key_before_rotary = reduced_float_back(jnp.dot(first_normalized, key_w, precision=maximum_precision))
    key_batch = reduced_float(apply_rotary(key_before_rotary.reshape(sequence_rows, KEY_VALUE_HEADS, HEAD_DIM), angle_sequence))
    value_batch = reduced_float_back(reduced_float(jnp.dot(first_normalized, value_projection, precision=maximum_precision))).reshape(sequence_rows, KEY_VALUE_HEADS, HEAD_DIM)
    attention = attend(query_batch, key_batch, value_batch, segment_line, code_line)
    attn_out = reduced_float_back(reduced_float(attention.reshape(sequence_rows, QUERY_HEADS * HEAD_DIM)))
    attn_branch = reduced_float_back(jnp.dot(attn_out, out_w, precision=maximum_precision))
    middle = hidden + attn_branch
    normed_two = reduced_float(rms_scale(middle, gain_two))
    gate_pre = reduced_float_back(jnp.dot(normed_two, gate_w, precision=maximum_precision))
    up_pre = reduced_float_back(jnp.dot(normed_two, up_w, precision=maximum_precision))
    hidden_ffn = reduced_float(jax.nn.silu(gate_pre) * up_pre)
    ffn_branch = reduced_float_back(jnp.dot(hidden_ffn, down_w, precision=maximum_precision))
    return hidden + branch_scale[:, None] * (attn_branch + ffn_branch)

def reference(hidden_in, cotangent, destination, seq_lengths, gate_mask, query_weight, key_matrix, value_matrix, out_weight, gate_weight, up_weight, down_weight, attn_gain, ffn_gain, router_weight):
    sequence_rows = TOK_DEV * N_REP
    positions = jnp.arange(sequence_rows, dtype=jnp.int32)
    segment, within, is_valid = jax.vmap(line_layout, in_axes=(0, None))(seq_lengths, positions)
    active = is_valid & (to_lines(gate_mask) == 1)
    key_code = jnp.where(active, segment, -1).astype(jnp.int32)
    rotary_angles = jax.vmap(lambda within_row: rope_angles(within_row, HEAD_DIM))(within)

    def forward(hidden_all, *weights):
        balanced = jnp.zeros_like(hidden_all).at[destination].set(hidden_all)
        line_data = to_lines(balanced)
        line_outs = lax.map(lambda line_items: line_forward(line_items, weights), (line_data, active, segment, key_code, rotary_angles))
        return from_lines(line_outs)[destination]
    primal, pullback = jax.vjp(forward, hidden_in.astype(jnp.float32), query_weight.astype(jnp.float32), key_matrix.astype(jnp.float32), value_matrix.astype(jnp.float32), out_weight.astype(jnp.float32), gate_weight.astype(jnp.float32), up_weight.astype(jnp.float32), down_weight.astype(jnp.float32), attn_gain.astype(jnp.float32), ffn_gain.astype(jnp.float32), router_weight.astype(jnp.float32))
    gradients = pullback(cotangent.astype(jnp.float32))
    return (primal.astype(jnp.bfloat16), gradients[0].astype(jnp.bfloat16), gradients[1], gradients[2], gradients[3], gradients[4], gradients[5], gradients[6], gradients[7], gradients[8], gradients[9], gradients[10])
```

```python
import functools

import jax
import jax.numpy as jnp
from jax import lax
from jax.experimental import pallas as pl
from jax.experimental.pallas import tpu as pltpu
from jax.sharding import Mesh
from jax.sharding import PartitionSpec as P

QUERY_HEADS = 15
KEY_VALUE_HEADS = 5
HEAD_DIM = 64
GROUP = QUERY_HEADS // KEY_VALUE_HEADS
EPSILON = 1e-05
NEGATIVE_HUGE = -1e30
ROPE_BASE = 10000.0
bf16 = jnp.bfloat16
f32 = jnp.float32
MESH = pl.DeviceIdType.MESH
REP = ("chip", "core")
ALL = ("chip", "core", "shard")
VMEM_SPEC = pl.BlockSpec(memory_space=pltpu.VMEM)


def dot(a, b, ca=1, cb=0):
    return lax.dot_general(a, b, (((ca,), (cb,)), ((), ())), preferred_element_type=f32)


def peer_coords(index, axes, sizes):
    coords = {}
    for name in reversed(axes):
        coords[name] = lax.rem(index, sizes[name])
        index = index // sizes[name]
    return coords


def exchange_kernel(specs, sizes, *refs):
    n = len(specs)
    ins, outs, sems = refs[:n], refs[n : 2 * n], refs[2 * n :]
    barrier = pltpu.get_barrier_semaphore()
    widest = max((axes for axes, _ in specs), key=lambda axes: len(axes))
    total = 1
    for name in widest:
        total *= sizes[name]
    me_all = lax.axis_index(widest)

    def greet(k, carry):
        peer = lax.rem(me_all + k, total)
        pl.semaphore_signal(
            barrier, inc=1, device_id=peer_coords(peer, widest, sizes), device_id_type=MESH
        )
        return carry

    lax.fori_loop(1, total, greet, 0)
    pl.semaphore_wait(barrier, total - 1)

    def copy_to(i, k):
        axes, spread = specs[i]
        count = 1
        for name in axes:
            count *= sizes[name]
        me = lax.axis_index(axes)
        peer = lax.rem(me + k, count)
        return pltpu.make_async_remote_copy(
            src_ref=ins[i] if spread else ins[i].at[peer],
            dst_ref=outs[i].at[me],
            send_sem=sems[2 * i].at[k],
            recv_sem=sems[2 * i + 1].at[k],
            device_id=peer_coords(peer, axes, sizes),
            device_id_type=MESH,
        )

    counts = []
    for i, (axes, spread) in enumerate(specs):
        count = 1
        for name in axes:
            count *= sizes[name]
        counts.append(count)

        def send(k, carry, i=i):
            copy_to(i, k).start()
            return carry

        lax.fori_loop(1, count, send, 0)
    for i, (axes, spread) in enumerate(specs):
        me = lax.axis_index(axes)
        outs[i][me] = ins[i][...] if spread else ins[i][me]
    for i in range(n):

        def finish(k, carry, i=i):
            copy_to(i, k).wait()
            return carry

        lax.fori_loop(1, counts[i], finish, 0)


def exchange(collective_id, sizes, items):
    specs = tuple((axes, spread) for _, axes, spread in items)
    out_shape, scratch = [], []
    for array, axes, spread in items:
        count = 1
        for name in axes:
            count *= sizes[name]
        shape = (count,) + array.shape if spread else array.shape
        out_shape.append(jax.ShapeDtypeStruct(shape, array.dtype))
        scratch += [pltpu.SemaphoreType.DMA((count,)), pltpu.SemaphoreType.DMA((count,))]
    return pl.pallas_call(
        functools.partial(exchange_kernel, specs, sizes),
        out_shape=out_shape,
        in_specs=[VMEM_SPEC] * len(items),
        out_specs=[VMEM_SPEC] * len(items),
        scratch_shapes=scratch,
        compiler_params=pltpu.CompilerParams(collective_id=collective_id, has_side_effects=True),
        name="exchange_%d" % collective_id,
    )(*[array for array, _, _ in items])


def mask_rows(code_row):
    index = lax.broadcasted_iota(jnp.int32, (16, code_row.shape[1]), 0)
    return jnp.where(index == code_row, 0.0, NEGATIVE_HUGE).astype(bf16)


def segment_rows(segment_row):
    index = lax.broadcasted_iota(jnp.int32, (16, segment_row.shape[1]), 0)
    return jnp.where(index == segment_row, 1.0, 0.0).astype(bf16)


def as_column(row):
    return jnp.transpose(jnp.broadcast_to(row, (128, row.shape[1])))[:, :1]


def diagonal_bias(info):
    code, place = as_column(info[0:1]), as_column(info[2:3])
    allowed = (place == info[2:3]) | ((code == info[1:2]) & (place <= info[2:3]))
    return jnp.where(allowed, 0.0, NEGATIVE_HUGE)


def forward_kernel(qkv_ref, info_ref, out_ref, keep_ref, lse_ref, bias, acc, stat):
    slots = qkv_ref.shape[2]
    i = pl.program_id(0)
    bias[...] = diagonal_bias(info_ref[i])
    seg = segment_rows(info_ref[i, 1:2])
    qa = [jnp.concatenate([qkv_ref[i, 0, m], seg], axis=0) for m in range(slots)]
    for m in range(slots):
        s = dot(jnp.transpose(qkv_ref[i, 1, m]), qkv_ref[i, 0, m]) + bias[...]
        top = jnp.max(s, axis=0, keepdims=True)
        p = jnp.exp(s - top)
        stat[2 * m : 2 * m + 1] = top
        stat[2 * m + 1 : 2 * m + 2] = jnp.sum(p, axis=0, keepdims=True)
        acc[m] = dot(qkv_ref[i, 2, m], p.astype(bf16))

    @pl.loop(0, i)
    def _(j):
        mask = mask_rows(info_ref[j, 0:1])
        for m in range(slots):
            ka = jnp.transpose(jnp.concatenate([qkv_ref[j, 1, m], mask], axis=0))
            s = dot(ka, qa[m])
            old = stat[2 * m : 2 * m + 1]
            top = jnp.maximum(old, jnp.max(s, axis=0, keepdims=True))
            p = jnp.exp(s - top)
            factor = jnp.exp(old - top)
            stat[2 * m : 2 * m + 1] = top
            stat[2 * m + 1 : 2 * m + 2] = stat[2 * m + 1 : 2 * m + 2] * factor + jnp.sum(
                p, axis=0, keepdims=True
            )
            acc[m] = acc[m] * factor + dot(qkv_ref[j, 2, m], p.astype(bf16))

    for m in range(slots):
        total = stat[2 * m + 1 : 2 * m + 2]
        result = acc[m] / total
        out_ref[i, m] = result.astype(bf16)
        keep_ref[i, m] = result
        lse_ref[i, m : m + 1] = stat[2 * m : 2 * m + 1] + jnp.log(total)


def attention_forward(qkv, info):
    blocks, _, slots, width, rows = qkv.shape
    return pl.pallas_call(
        forward_kernel,
        grid=(blocks,),
        in_specs=[VMEM_SPEC, VMEM_SPEC],
        out_specs=[VMEM_SPEC] * 3,
        out_shape=[
            jax.ShapeDtypeStruct((blocks, slots, width, rows), bf16),
            jax.ShapeDtypeStruct((blocks, slots, width, rows), f32),
            jax.ShapeDtypeStruct((blocks, 8, rows), f32),
        ],
        scratch_shapes=[
            pltpu.VMEM((rows, rows), f32),
            pltpu.VMEM((slots, width, rows), f32),
            pltpu.VMEM((8, rows), f32),
        ],
        name="attention_forward",
    )(qkv, info)


def backward_kernel(qkv_ref, do_ref, keep_ref, lse_ref, info_ref, out_ref, bias, dq, qn, don, delta):
    blocks, _, slots = qkv_ref.shape[:3]
    j = pl.program_id(0)

    @pl.when(j == 0)
    def _():
        @pl.loop(0, blocks)
        def _(i):
            for m in range(slots):
                qn[i, m] = jnp.transpose(qkv_ref[i, 0, m])
                don[i, m] = jnp.transpose(do_ref[i, m])
                delta[i, m : m + 1] = jnp.sum(
                    do_ref[i, m].astype(f32) * keep_ref[i, m], axis=0, keepdims=True
                )
                dq[i, m] = jnp.zeros_like(dq[i, m])

    bias[...] = diagonal_bias(info_ref[j])
    mask = mask_rows(info_ref[j, 0:1])
    kn = [jnp.transpose(qkv_ref[j, 1, m]) for m in range(slots)]
    ka = [
        jnp.transpose(jnp.concatenate([qkv_ref[j, 1, m], mask], axis=0)) for m in range(slots)
    ]
    vn = [jnp.transpose(qkv_ref[j, 2, m]) for m in range(slots)]

    def tile(i, m, s):
        p = jnp.exp(s - lse_ref[i, m : m + 1])
        dp = dot(vn[m], do_ref[i, m])
        ds = (p * (dp - delta[i, m : m + 1])).astype(bf16)
        dq[i, m] += dot(qkv_ref[j, 1, m], ds)
        return dot(ds, qn[i, m]), dot(p.astype(bf16), don[i, m])

    start = []
    for m in range(slots):
        start += list(tile(j, m, dot(kn[m], qkv_ref[j, 0, m]) + bias[...]))

    def later(i, carry):
        seg = segment_rows(info_ref[i, 1:2])
        new = []
        for m in range(slots):
            qa = jnp.concatenate([qkv_ref[i, 0, m], seg], axis=0)
            a, b = tile(i, m, dot(ka[m], qa))
            new += [carry[2 * m] + a, carry[2 * m + 1] + b]
        return tuple(new)

    done = lax.fori_loop(j + 1, blocks, later, tuple(start))
    for m in range(slots):
        out_ref[j, 1, m] = jnp.transpose(done[2 * m]).astype(bf16)
        out_ref[j, 2, m] = jnp.transpose(done[2 * m + 1]).astype(bf16)

    @pl.when(j == blocks - 1)
    def _():
        @pl.loop(0, blocks)
        def _(i):
            for m in range(slots):
                out_ref[i, 0, m] = (dq[i, m] * HEAD_DIM ** (-0.5)).astype(bf16)


def attention_backward(qkv, grad, keep, lse, info):
    blocks, _, slots, width, rows = qkv.shape
    return pl.pallas_call(
        backward_kernel,
        grid=(blocks,),
        in_specs=[VMEM_SPEC] * 5,
        out_specs=VMEM_SPEC,
        out_shape=jax.ShapeDtypeStruct(qkv.shape, bf16),
        scratch_shapes=[
            pltpu.VMEM((rows, rows), f32),
            pltpu.VMEM((blocks, slots, width, rows), f32),
            pltpu.VMEM((blocks, slots, rows, width), bf16),
            pltpu.VMEM((blocks, slots, rows, width), bf16),
            pltpu.VMEM((blocks, 8, rows), f32),
        ],
        name="attention_backward",
    )(qkv, grad, keep, lse, info)


def ffn_kernel(x_ref, gf_ref, gu_ref, down_ref, part_ref, gu_grad_ref, down_grad_ref, ffn, dx):
    k = pl.program_id(0)
    half = gu_ref.shape[1] // 2
    x, gf = x_ref[...], gf_ref[...]
    both = dot(x, gu_ref[...])
    gate, up = both[:, :half], both[:, half:]
    sig = 1.0 / (1.0 + jnp.exp(-gate))
    act = gate * sig
    hidden = (act * up).astype(bf16)
    grad_hidden = dot(gf, down_ref[...], 1, 1)
    grad_gate = (grad_hidden * up * (sig * (1.0 + gate * (1.0 - sig)))).astype(bf16)
    grad_up = (grad_hidden * act).astype(bf16)
    grads = jnp.concatenate([grad_gate, grad_up], axis=1)
    ffn_now = dot(hidden, down_ref[...])
    dx_now = dot(grads, gu_ref[...], 1, 1)

    @pl.when(k == 0)
    def _():
        ffn[...] = ffn_now
        dx[...] = dx_now

    @pl.when(k > 0)
    def _():
        ffn[...] += ffn_now
        dx[...] += dx_now

    gu_grad_ref[...] = dot(x, grads, 0, 0).astype(bf16)
    down_grad_ref[...] = dot(hidden, gf, 0, 0).astype(bf16)

    @pl.when(k == pl.num_programs(0) - 1)
    def _():
        rows = part_ref.shape[2]
        for c in range(2):
            part_ref[c, 0] = dx[c * rows : (c + 1) * rows].astype(bf16)
            part_ref[c, 1] = ffn[c * rows : (c + 1) * rows].astype(bf16)


def feed_forward(x, gf, gate_up, down):
    tokens, width = x.shape
    chunks, _, columns = gate_up.shape
    hidden = columns // 2
    return pl.pallas_call(
        ffn_kernel,
        grid=(chunks,),
        in_specs=[
            pl.BlockSpec((tokens, width), lambda k: (0, 0)),
            pl.BlockSpec((tokens, width), lambda k: (0, 0)),
            pl.BlockSpec((None, width, columns), lambda k: (k, 0, 0)),
            pl.BlockSpec((None, hidden, width), lambda k: (k, 0, 0)),
        ],
        out_specs=[
            pl.BlockSpec((2, 2, tokens // 2, width), lambda k: (0, 0, 0, 0)),
            pl.BlockSpec((None, width, columns), lambda k: (k, 0, 0)),
            pl.BlockSpec((None, hidden, width), lambda k: (k, 0, 0)),
        ],
        out_shape=[
            jax.ShapeDtypeStruct((2, 2, tokens // 2, width), bf16),
            jax.ShapeDtypeStruct((chunks, width, columns), bf16),
            jax.ShapeDtypeStruct((chunks, hidden, width), bf16),
        ],
        scratch_shapes=[pltpu.VMEM((tokens, width), f32), pltpu.VMEM((tokens, width), f32)],
        name="feed_forward",
    )(x, gf, gate_up, down)


def rms_scale(rows, gain):
    return rows * lax.rsqrt(jnp.mean(rows * rows, axis=-1, keepdims=True) + EPSILON) * gain


def norm_back(rows, gain, grad):
    r = lax.rsqrt(jnp.mean(rows * rows, axis=-1, keepdims=True) + EPSILON)
    scaled = gain * grad
    back = r * scaled - rows * (r * r * r) * jnp.mean(scaled * rows, axis=-1, keepdims=True)
    return back, jnp.sum(grad * rows * r, axis=0)


def line_layout(lengths_row, positions):
    seq_ends = jnp.cumsum(lengths_row, dtype=jnp.int32)
    reached = seq_ends[None, :] <= positions[:, None]
    segment = jnp.sum(reached.astype(jnp.int32), axis=1)
    starts = jnp.max(jnp.where(reached, seq_ends[None, :], 0), axis=1)
    return segment, positions - starts, positions < seq_ends[-1]


def rotate(heads, cosines, sines):
    half = HEAD_DIM // 2
    a, b = heads[:, :half], heads[:, half:]
    return jnp.concatenate([a * cosines - b * sines, b * cosines + a * sines], axis=1)


def local(
    sizes,
    hidden_in,
    cotangent,
    destination,
    seq_lengths,
    gate_mask,
    query_weight,
    key_matrix,
    value_matrix,
    out_weight,
    gate_weight,
    up_weight,
    down_weight,
    attn_gain,
    ffn_gain,
    router_weight,
):
    rows, width = hidden_in.shape
    chips, shards = sizes["chip"], sizes["shard"]
    reps = 2 * chips
    devices = reps * shards
    per_pair = rows // devices
    slots = -(-QUERY_HEADS // reps)
    padded_heads = slots * reps
    chip, core = lax.axis_index("chip"), lax.axis_index("core")
    rep = lax.axis_index(REP)
    shard_rows = query_weight.shape[0]

    def column_slice(weight, index, count):
        size = weight.shape[1] // count
        return lax.dynamic_slice_in_dim(weight, index * size, size, 1)

    qkv_shard = jnp.concatenate([query_weight, key_matrix, value_matrix], axis=1)
    vectors = jnp.stack([attn_gain, ffn_gain, router_weight], axis=1)
    qkv_piece = jnp.concatenate(
        [column_slice(qkv_shard, rep, reps), jnp.pad(vectors, ((0, 0), (0, 5)))], axis=1
    )
    qkv_all = lax.all_gather(qkv_piece, ALL, axis=0, tiled=True)
    qkv_columns = qkv_piece.shape[1] - 8
    qkv_all = qkv_all.reshape(reps, width, qkv_columns + 8)
    full_qkv = jnp.transpose(qkv_all[:, :, :qkv_columns], (1, 0, 2)).reshape(width, -1)
    vector_rows = jnp.transpose(qkv_all[0, :, qkv_columns : qkv_columns + 3]).astype(f32)
    gain_one, gain_two, full_router = vector_rows[0], vector_rows[1], vector_rows[2]

    out_piece = column_slice(out_weight, rep, reps)
    out_all = lax.all_gather(out_piece, ALL, axis=0, tiled=True)
    out_columns = out_piece.shape[1]
    full_out = jnp.transpose(out_all.reshape(reps, width, out_columns), (1, 0, 2)).reshape(
        width, -1
    )
    gate_up_piece = jnp.concatenate(
        [column_slice(gate_weight, rep, reps), column_slice(up_weight, rep, reps)], axis=1
    )
    ff_chunk = gate_up_piece.shape[1] // 2
    gate_up = lax.all_gather(gate_up_piece, ("chip", "shard"), axis=0, tiled=True)
    gate_up = gate_up.reshape(chips, width, 2 * ff_chunk)
    down_rows = down_weight.shape[0] // reps
    down_piece = lax.dynamic_slice_in_dim(down_weight, (core * chips + chip) * down_rows, down_rows, 0)
    down = lax.all_gather(down_piece, ("shard", "chip"), axis=0, tiled=True)
    down = down.reshape(shards, ff_chunk, width)

    row_index = jnp.arange(rows, dtype=jnp.int32)
    target = destination // rows
    earlier = (target[None, :] == target[:, None]) & (row_index[None, :] < row_index[:, None])
    slot_of_row = target * per_pair + jnp.sum(earlier.astype(jnp.int32), axis=1)
    to_slot = slot_of_row[None, :] == row_index[:, None]
    to_slot_b = to_slot.astype(bf16)
    place_sent = jnp.sum(jnp.where(to_slot, (destination % rows)[None, :], 0), axis=1)
    place_sent = jnp.pad(place_sent.reshape(devices, 1, per_pair), ((0, 0), (0, 0), (0, 128 - per_pair)))
    sent_hidden = jnp.dot(to_slot_b, hidden_in, preferred_element_type=f32).astype(bf16)
    sent_grad = jnp.dot(to_slot_b, cotangent, preferred_element_type=f32).astype(bf16)
    got_hidden, got_place = exchange(
        1,
        sizes,
        [
            (sent_hidden.reshape(devices, per_pair, width), ALL, False),
            (place_sent, ALL, False),
        ],
    )
    got_grad = lax.all_to_all(
        sent_grad.reshape(devices, per_pair, width), ALL, split_axis=0, concat_axis=0, tiled=True
    )
    hidden = got_hidden.reshape(rows, width)
    place = got_place[:, 0, :per_pair].reshape(rows)

    positions = rep * rows + place
    segment, within, is_valid = line_layout(seq_lengths[0], positions)
    gate_here = jnp.sum(jnp.where(place[:, None] == row_index[None, :], gate_mask[None, :], 0), axis=1)
    active = is_valid & (gate_here == 1)
    key_code = jnp.where(active, segment, -1)
    active_f = active.astype(f32)

    hidden_f = hidden.astype(f32)
    first_normalized = rms_scale(hidden_f, gain_one).astype(bf16)
    router_logit = jnp.sum(hidden_f * full_router, axis=1)
    gate_value = jax.nn.sigmoid(router_logit)
    branch_scale = active_f * gate_value

    steps = jnp.arange(HEAD_DIM // 2).astype(f32)
    frequency = jnp.power(ROPE_BASE, -2.0 * steps / HEAD_DIM)
    angles = frequency[:, None] * within.astype(f32)[None, :]
    cosines, sines = jnp.cos(angles), jnp.sin(angles)
    qkv_t = jnp.einsum("te,ed->dt", first_normalized, full_qkv, preferred_element_type=f32)
    qkv_t = qkv_t.reshape(QUERY_HEADS + 2 * KEY_VALUE_HEADS, HEAD_DIM, rows)
    rotated = rotate(qkv_t[: QUERY_HEADS + KEY_VALUE_HEADS], cosines, sines).astype(bf16)
    query = rotated[:QUERY_HEADS] * jnp.asarray(HEAD_DIM ** (-0.5), bf16)
    key_t = jnp.repeat(rotated[QUERY_HEADS:], GROUP, axis=0)
    value_t = jnp.repeat(qkv_t[QUERY_HEADS + KEY_VALUE_HEADS :].astype(bf16), GROUP, axis=0)

    def by_owner(heads):
        heads = jnp.pad(heads, ((0, padded_heads - QUERY_HEADS), (0, 0), (0, 0)))
        return heads.reshape(reps, slots, HEAD_DIM, rows)

    qkv_sent = jnp.stack([by_owner(query), by_owner(key_t), by_owner(value_t)], axis=1)
    info = jnp.pad(jnp.stack([key_code, segment, place]), ((0, 5), (0, 0)))
    qkv_got, info_got = exchange(2, sizes, [(qkv_sent, REP, False), (info, REP, True)])
    att_out, att_keep, lse = attention_forward(qkv_got, info_got)
    (att_home,) = exchange(3, sizes, [(att_out, REP, False)])
    attn_out_t = att_home.reshape(padded_heads * HEAD_DIM, rows)[:width]

    attn_branch = jnp.einsum("dt,de->te", attn_out_t, full_out, preferred_element_type=f32)
    middle = hidden_f + attn_branch
    normed_two = rms_scale(middle, gain_two).astype(bf16)
    grad_out = got_grad.reshape(rows, width).astype(f32)
    grad_branch = branch_scale[:, None] * grad_out
    grad_ffn = grad_branch.astype(bf16)
    x_pair, gf_pair = exchange(
        4, sizes, [(normed_two, ("core",), True), (grad_ffn, ("core",), True)]
    )
    parts, gate_up_grad, down_grad = feed_forward(
        x_pair.reshape(2 * rows, width), gf_pair.reshape(2 * rows, width), gate_up, down
    )
    (parts_got,) = exchange(5, sizes, [(parts, ("core",), False)])
    grad_normed_two = parts_got[0, 0].astype(f32) + parts_got[1, 0].astype(f32)
    ffn_branch = parts_got[0, 1].astype(f32) + parts_got[1, 1].astype(f32)

    gate_up_sum = lax.psum_scatter(
        gate_up_grad.reshape(chips * shards, shard_rows, 2 * ff_chunk),
        ("chip", "shard"),
        scatter_dimension=0,
        tiled=True,
    )
    down_sum = lax.psum_scatter(
        down_grad.reshape(shards * chips, down_rows, width),
        ("shard", "chip"),
        scatter_dimension=0,
        tiled=True,
    )
    gate_up_total = lax.all_gather(gate_up_sum, REP, axis=0, tiled=True)
    down_total = lax.all_gather(down_sum, ("core", "chip"), axis=0, tiled=True)

    branch_sum = attn_branch + ffn_branch
    result = (hidden_f + branch_scale[:, None] * branch_sum).astype(bf16)
    home_out = lax.all_to_all(
        result.reshape(devices, per_pair, width), ALL, split_axis=0, concat_axis=0, tiled=True
    )
    grad_logit = active_f * jnp.sum(grad_out * branch_sum, axis=1) * gate_value * (1.0 - gate_value)
    grad_middle, grad_gain_ffn = norm_back(middle, gain_two, grad_normed_two)
    grad_attn = (grad_branch + grad_middle).astype(bf16)
    grad_attention_t = jnp.einsum("te,de->dt", grad_attn, full_out, preferred_element_type=f32)
    grad_attention_t = grad_attention_t.astype(bf16).reshape(QUERY_HEADS, HEAD_DIM, rows)
    (grad_got,) = exchange(6, sizes, [(by_owner(grad_attention_t), REP, False)])
    grads_sent = attention_backward(qkv_got, grad_got, att_keep, lse, info_got)
    (grads_home,) = exchange(7, sizes, [(grads_sent, REP, False)])
    grads_home = jnp.transpose(grads_home, (1, 0, 2, 3, 4)).reshape(3, padded_heads, HEAD_DIM, rows)
    grads_home = grads_home[:, :QUERY_HEADS].astype(f32)
    grouped = grads_home[1:].reshape(2, KEY_VALUE_HEADS, GROUP, HEAD_DIM, rows).sum(axis=2)
    back = rotate(jnp.concatenate([grads_home[0], grouped[0]], axis=0), cosines, -sines)
    qkv_grad_t = jnp.concatenate([back, grouped[1]], axis=0).astype(bf16).reshape(-1, rows)
    grad_normed_one = jnp.einsum("ct,ec->te", qkv_grad_t, full_qkv, preferred_element_type=f32)
    grad_norm_x, grad_gain_attn = norm_back(hidden_f, gain_one, grad_normed_one)
    grad_hidden = grad_out + grad_middle + grad_norm_x + grad_logit[:, None] * full_router
    home_grad = lax.all_to_all(
        grad_hidden.astype(bf16).reshape(devices, per_pair, width),
        ALL,
        split_axis=0,
        concat_axis=0,
        tiled=True,
    )

    qkv_grad = jnp.einsum("te,ct->ec", first_normalized, qkv_grad_t, preferred_element_type=f32)
    out_grad = jnp.einsum("dt,te->de", attn_out_t, grad_attn, preferred_element_type=f32)
    router_grad = jnp.sum(grad_logit[:, None] * hidden_f, axis=0)

    def by_columns(grad, columns):
        return jnp.transpose(grad.astype(bf16).reshape(width, reps, columns), (1, 0, 2))

    vector_grads = jnp.stack([grad_gain_attn, grad_gain_ffn, router_grad], axis=1).astype(bf16)
    vector_grads = jnp.pad(vector_grads[None], ((0, reps - 1), (0, 0), (0, 5)))
    proj_grad = jnp.concatenate(
        [by_columns(qkv_grad, qkv_columns), by_columns(out_grad, out_columns), vector_grads], axis=2
    )
    proj_sum = lax.psum_scatter(
        proj_grad.reshape(devices, shard_rows, -1), ALL, scatter_dimension=0, tiled=True
    )
    proj_total = lax.all_gather(proj_sum, REP, axis=0, tiled=True)
    proj_total = proj_total.reshape(reps, shard_rows, -1).astype(f32)

    def joined(piece):
        return jnp.transpose(piece, (1, 0, 2)).reshape(shard_rows, -1)

    qkv_total = joined(proj_total[:, :, :qkv_columns])
    out_total = joined(proj_total[:, :, qkv_columns : qkv_columns + out_columns])
    vector_total = jnp.transpose(proj_total[0, :, qkv_columns + out_columns :])
    gate_up_total = gate_up_total.reshape(reps, shard_rows, 2 * ff_chunk).astype(f32)
    q_end, k_end = query_weight.shape[1], query_weight.shape[1] + key_matrix.shape[1]

    def home_rows(home):
        return jnp.dot(
            to_slot_b.T, home.reshape(rows, width), preferred_element_type=f32
        ).astype(bf16)

    return (
        home_rows(home_out),
        home_rows(home_grad),
        qkv_total[:, :q_end],
        qkv_total[:, q_end:k_end],
        qkv_total[:, k_end:],
        out_total,
        joined(gate_up_total[:, :, :ff_chunk]),
        joined(gate_up_total[:, :, ff_chunk:]),
        down_total.reshape(-1, width).astype(f32),
        vector_total[0],
        vector_total[1],
        vector_total[2],
    )


def solution(mesh):
    reps, shards = mesh.shape["rep"], mesh.shape["shard"]
    sizes = {"chip": reps // 2, "core": 2, "shard": shards}
    split_mesh = Mesh(mesh.devices.reshape(reps // 2, 2, shards), ALL)
    tokens, tokens_1d = P(ALL, None), P(ALL)
    weight, vector = P("shard", None), P("shard")
    return jax.shard_map(
        functools.partial(local, sizes),
        mesh=split_mesh,
        in_specs=(tokens, tokens, tokens_1d, weight, tokens_1d) + (weight,) * 7 + (vector,) * 3,
        out_specs=(tokens, tokens) + (weight,) * 7 + (vector,) * 3,
        check_vma=False,
    )
```

```python
import functools

import jax
import jax.numpy as jnp
from jax import lax
from jax.experimental import pallas as pl
from jax.experimental.pallas import tpu as pltpu
from jax.sharding import Mesh
from jax.sharding import PartitionSpec as P

QUERY_HEADS = 15
KEY_VALUE_HEADS = 5
HEAD_DIM = 64
GROUP = QUERY_HEADS // KEY_VALUE_HEADS
EPSILON = 1e-05
NEGATIVE_HUGE = -1e30
ROPE_BASE = 10000.0
FF_CHUNK = 256
bf16 = jnp.bfloat16
f32 = jnp.float32
MESH = pl.DeviceIdType.MESH
REP = ("chip", "core")
ALL = ("chip", "core", "shard")
VMEM_SPEC = pl.BlockSpec(memory_space=pltpu.VMEM)
HBM_SPEC = pl.BlockSpec(memory_space=pl.ANY)


def dot(a, b, ca=1, cb=0):
    return lax.dot_general(a, b, (((ca,), (cb,)), ((), ())), preferred_element_type=f32)


def axes_size(sizes, axes):
    total = 1
    for name in axes:
        total *= sizes[name]
    return total


def peer_coords(index, axes, sizes):
    coords = {}
    for name in reversed(axes):
        coords[name] = lax.rem(index, sizes[name])
        index = index // sizes[name]
    return coords


def remote(src, dst, send_sem, recv_sem, coords):
    return pltpu.make_async_remote_copy(
        src_ref=src,
        dst_ref=dst,
        send_sem=send_sem,
        recv_sem=recv_sem,
        device_id=coords,
        device_id_type=MESH,
    )


def each(start, stop, body):
    def step(k, carry):
        body(k)
        return carry

    lax.fori_loop(start, stop, step, 0)


class Item:
    late = False
    aliased = False

    def start(self, ins, outs, scratch):
        pass

    def middle(self, ins, outs, scratch):
        pass

    def finish(self, ins, outs, scratch):
        pass


class AllToAll(Item):
    def __init__(self, sizes, array, axes, spread=False, late=False, source=None):
        self.sizes, self.axes, self.spread, self.late = sizes, axes, spread, late
        self.count = axes_size(sizes, axes)
        self.source = source
        self.inputs = [] if source is not None else [array]
        shape = (self.count,) + tuple(array.shape) if spread else tuple(array.shape)
        self.in_specs = [VMEM_SPEC] * len(self.inputs)
        self.out_shapes = [jax.ShapeDtypeStruct(shape, array.dtype)]
        self.out_specs = [VMEM_SPEC]
        self.scratch = [
            pltpu.SemaphoreType.DMA((self.count,)),
            pltpu.SemaphoreType.DMA((self.count,)),
        ]

    def copy(self, k, ins, outs, scratch):
        me = lax.axis_index(self.axes)
        peer = lax.rem(me + k, self.count)
        return remote(
            ins[0] if self.spread else ins[0].at[peer],
            outs[0].at[me],
            scratch[0].at[k],
            scratch[1].at[k],
            peer_coords(peer, self.axes, self.sizes),
        )

    def start(self, ins, outs, scratch):
        each(1, self.count, lambda k: self.copy(k, ins, outs, scratch).start())
        me = lax.axis_index(self.axes)
        outs[0][me] = ins[0][...] if self.spread else ins[0][me]

    def finish(self, ins, outs, scratch):
        each(1, self.count, lambda k: self.copy(k, ins, outs, scratch).wait())


class Scatter(Item):
    def __init__(self, sizes, array, axes, dim, half=False, late=False, source=None):
        self.sizes, self.axes, self.dim = sizes, axes, dim
        self.half, self.late, self.source = half, late, source
        self.count = axes_size(sizes, axes)
        self.slots = self.count // 2
        piece = tuple(array.shape[:dim]) + tuple(array.shape[dim + 1 :])
        self.inputs = [] if source is not None else [array]
        self.in_specs = [HBM_SPEC] * len(self.inputs)
        self.out_shapes = [jax.ShapeDtypeStruct((self.count - 1,) + piece, array.dtype)]
        self.out_specs = [HBM_SPEC]
        self.scratch = [
            pltpu.SemaphoreType.DMA((self.count,)),
            pltpu.SemaphoreType.DMA((self.count,)),
        ]

    def guarded(self, index, body):
        if self.half:
            pl.when(index // self.slots == lax.axis_index("core"))(body)
        else:
            body()

    def copy(self, k, ins, outs, scratch):
        me = lax.axis_index(self.axes)
        peer = lax.rem(me + k, self.count)
        index = lax.rem(peer, self.slots) if self.half else peer
        src = ins[0].at[index] if self.dim == 0 else ins[0].at[:, index]
        return peer, remote(
            src,
            outs[0].at[k - 1],
            scratch[0].at[k],
            scratch[1].at[k],
            peer_coords(peer, self.axes, self.sizes),
        )

    def start(self, ins, outs, scratch):
        def send(k):
            peer, copy = self.copy(k, ins, outs, scratch)
            self.guarded(peer, copy.start)

        each(1, self.count, send)

    def finish(self, ins, outs, scratch):
        def receive(k):
            self.copy(k, ins, outs, scratch)[1].wait_recv()

        def sent(k):
            peer, copy = self.copy(k, ins, outs, scratch)
            self.guarded(peer, copy.wait_send)

        me = lax.axis_index(self.axes)
        self.guarded(me, lambda: each(1, self.count, receive))
        each(1, self.count, sent)


class SpreadHalf(Item):
    def __init__(self, sizes, array):
        self.sizes, self.count = sizes, axes_size(sizes, REP)
        self.slots = sizes["shard"] // 2
        self.inputs, self.in_specs = [array], [VMEM_SPEC]
        shape = (sizes["chip"],) + tuple(array.shape)
        self.out_shapes = [jax.ShapeDtypeStruct(shape, array.dtype)]
        self.out_specs = [VMEM_SPEC]
        self.scratch = [
            pltpu.SemaphoreType.DMA((self.count,)),
            pltpu.SemaphoreType.DMA((self.count,)),
        ]

    def owner(self):
        return lax.axis_index("shard") // self.slots

    def copy(self, k, ins, outs, scratch, sending):
        me = lax.axis_index(REP)
        peer = lax.rem(me + k, self.count) if sending else lax.rem(me + self.count - k, self.count)
        chip = lax.axis_index("chip") if sending else peer // 2
        return peer, remote(
            ins[0],
            outs[0].at[chip],
            scratch[0].at[k],
            scratch[1].at[k],
            peer_coords(peer, REP, self.sizes),
        )

    def start(self, ins, outs, scratch):
        @pl.when(lax.axis_index("core") == self.owner())
        def _():
            each(1, self.count, lambda k: self.copy(k, ins, outs, scratch, True)[1].start())
            outs[0][lax.axis_index("chip")] = ins[0][...]

    def finish(self, ins, outs, scratch):
        def receive(k):
            peer, copy = self.copy(k, ins, outs, scratch, False)
            pl.when(lax.rem(peer, 2) == self.owner())(copy.wait_recv)

        each(1, self.count, receive)

        @pl.when(lax.axis_index("core") == self.owner())
        def _():
            each(1, self.count, lambda k: self.copy(k, ins, outs, scratch, True)[1].wait_send())


class Gather(Item):
    def __init__(self, sizes, array, split_axes, stages, half=False):
        self.sizes, self.split_axes, self.stages, self.half = sizes, split_axes, stages, half
        self.shards = sizes["shard"]
        self.slots = self.shards // 2 if half else self.shards
        self.split = axes_size(sizes, split_axes)
        both = stages == "both"
        self.inputs = [array]
        self.in_specs = [VMEM_SPEC if both else HBM_SPEC]
        if stages == "plane":
            shape, self.aliased = tuple(array.shape), True
        else:
            shape = (self.slots,) + tuple(array.shape)
        self.out_shapes = [jax.ShapeDtypeStruct(shape, array.dtype)]
        self.out_specs = [VMEM_SPEC if both else HBM_SPEC]
        dma = pltpu.SemaphoreType.DMA
        self.scratch = []
        if stages != "plane":
            self.scratch += [dma((self.shards,)), dma((self.shards,))]
        if stages == "z":
            self.scratch += [pltpu.VMEM(array.shape, array.dtype), dma((2,))]
        if stages != "z":
            self.scratch += [dma((self.split, self.shards)), dma((self.split, self.shards))]

    def valid(self, z):
        if not self.half:
            return None
        return z // self.slots == lax.axis_index("core")

    def guarded(self, z, body):
        ok = self.valid(z)
        if ok is None:
            body()
        else:
            pl.when(ok)(body)

    def slot(self, z):
        return lax.rem(z, self.slots) if self.half else z

    def z_copy(self, k, src, full, scratch, sending):
        me = lax.axis_index("shard")
        mine = lax.axis_index(self.split_axes)
        peer = lax.rem(me + k, self.shards) if sending else lax.rem(me + self.shards - k, self.shards)
        source = me if sending else peer
        dst = full.at[self.slot(source), mine]
        return remote(
            src.at[mine] if sending else dst,
            dst,
            scratch[0].at[k],
            scratch[1].at[k],
            {"shard": peer},
        )

    def start(self, ins, outs, scratch):
        me = lax.axis_index("shard")
        if self.stages == "plane":
            self.plane_start(outs[0], scratch)
            return
        src, full = ins[0], outs[0]

        def send():
            each(1, self.shards, lambda k: self.z_copy(k, src, full, scratch, True).start())

        self.guarded(me, send)
        if self.stages == "both":
            full[me] = src[...]
        else:

            def load():
                pltpu.make_async_copy(src, scratch[2], scratch[3].at[0]).start()

            self.guarded(me, load)

    def z_finish(self, src, full, scratch):
        me = lax.axis_index("shard")

        def receive(k):
            peer = lax.rem(me + self.shards - k, self.shards)
            self.guarded(
                peer, lambda: self.z_copy(k, src, full, scratch, False).wait_recv()
            )

        each(1, self.shards, receive)

        def sent():
            each(1, self.shards, lambda k: self.z_copy(k, src, full, scratch, True).wait_send())

        self.guarded(me, sent)

    def plane_copy(self, k, d, full, scratch, sending):
        me, mine = lax.axis_index("shard"), lax.axis_index(self.split_axes)
        z = lax.rem(me + d, self.shards)
        if sending:
            peer, owner = lax.rem(mine + k, self.split), mine
        else:
            peer = owner = lax.rem(mine + self.split - k, self.split)
        region = full.at[self.slot(z), owner]
        return z, remote(
            region,
            region,
            scratch[-2].at[k, d],
            scratch[-1].at[k, d],
            peer_coords(peer, self.split_axes, self.sizes),
        )

    def plane_each(self, full, scratch, sending, act):
        def peers(k):
            def shards(d):
                z, copy = self.plane_copy(k, d, full, scratch, sending)
                self.guarded(z, lambda: act(copy))

            each(1, self.shards, shards)

        each(1, self.split, peers)

    def plane_start(self, full, scratch):
        self.plane_each(full, scratch, True, lambda copy: copy.start())

    def middle(self, ins, outs, scratch):
        if self.stages == "both":
            self.z_finish(ins[0], outs[0], scratch)
            self.plane_start(outs[0], scratch)
        elif self.stages == "z":
            me = lax.axis_index("shard")

            def store():
                pltpu.make_async_copy(ins[0], scratch[2], scratch[3].at[0]).wait()
                pltpu.make_async_copy(
                    scratch[2], outs[0].at[self.slot(me)], scratch[3].at[1]
                ).start()

            self.guarded(me, store)

    def finish(self, ins, outs, scratch):
        if self.stages == "z":
            me = lax.axis_index("shard")

            def stored():
                pltpu.make_async_copy(
                    scratch[2], outs[0].at[self.slot(me)], scratch[3].at[1]
                ).wait()

            self.guarded(me, stored)
            self.z_finish(ins[0], outs[0], scratch)
        else:
            self.plane_each(outs[0], scratch, False, lambda copy: copy.wait_recv())
            self.plane_each(outs[0], scratch, True, lambda copy: copy.wait_send())


class Compute:
    def __init__(self, body, inputs, out_shapes, scratch=()):
        self.body, self.inputs, self.out_shapes = body, list(inputs), list(out_shapes)
        self.scratch = list(scratch)


def greet_all(sizes, wide):
    barrier = pltpu.get_barrier_semaphore()
    groups = [ALL] if wide else [REP, ("shard",)]
    total = 0
    for axes in groups:
        count, me = axes_size(sizes, axes), lax.axis_index(axes)
        total += count - 1

        def greet(k):
            peer = peer_coords(lax.rem(me + k, count), axes, sizes)
            pl.semaphore_signal(barrier, inc=1, device_id=peer, device_id_type=MESH)

        each(1, count, greet)
    pl.semaphore_wait(barrier, total)


def run(collective_id, name, sizes, items, compute=None):
    wide = any(getattr(item, "axes", ()) == ALL for item in items)
    compute = compute or Compute(None, [], [])
    inputs, in_specs, out_shapes, out_specs, scratch, aliases = [], [], [], [], [], {}
    spans = []
    for item in items:
        if item.aliased:
            aliases[len(inputs)] = len(out_shapes)
        spans.append((len(inputs), len(out_shapes), len(scratch)))
        inputs += item.inputs
        in_specs += item.in_specs
        out_shapes += item.out_shapes
        out_specs += item.out_specs
        scratch += item.scratch
    own = (len(inputs), len(out_shapes), len(scratch))
    inputs += compute.inputs
    in_specs += [VMEM_SPEC] * len(compute.inputs)
    out_shapes += compute.out_shapes
    out_specs += [VMEM_SPEC] * len(compute.out_shapes)
    scratch += compute.scratch
    n_in, n_out = len(inputs), len(out_shapes)

    def kernel(*refs):
        ins, outs, tmp = refs[:n_in], refs[n_in : n_in + n_out], refs[n_in + n_out :]

        def parts(index):
            item, (a, b, c) = items[index], spans[index]
            item_ins = ins[a : a + len(item.inputs)]
            if getattr(item, "source", None) is not None:
                item_ins = [outs[own[1] + item.source]]
            return (
                item_ins,
                outs[b : b + len(item.out_shapes)],
                tmp[c : c + len(item.scratch)],
            )

        greet_all(sizes, wide)
        for index, item in enumerate(items):
            if not item.late:
                item.start(*parts(index))
        for index, item in enumerate(items):
            item.middle(*parts(index))
        if compute.body is not None:
            compute.body(ins[own[0] :], outs[own[1] :], tmp[own[2] :])
        for index, item in enumerate(items):
            if item.late:
                item.start(*parts(index))
        for index, item in enumerate(items):
            item.finish(*parts(index))

    return pl.pallas_call(
        kernel,
        out_shape=out_shapes,
        in_specs=in_specs,
        out_specs=out_specs,
        scratch_shapes=scratch,
        input_output_aliases=aliases,
        compiler_params=pltpu.CompilerParams(collective_id=collective_id, has_side_effects=True),
        name=name,
    )(*inputs)


def mask_rows(code_row):
    index = lax.broadcasted_iota(jnp.int32, (16, code_row.shape[1]), 0)
    return jnp.where(index == code_row, 0.0, NEGATIVE_HUGE).astype(bf16)


def segment_rows(segment_row):
    index = lax.broadcasted_iota(jnp.int32, (16, segment_row.shape[1]), 0)
    return jnp.where(index == segment_row, 1.0, 0.0).astype(bf16)


def as_column(row):
    return jnp.transpose(jnp.broadcast_to(row, (128, row.shape[1])))[:, :1]


def diagonal_bias(info):
    code, place = as_column(info[0:1]), as_column(info[2:3])
    allowed = (place == info[2:3]) | ((code == info[1:2]) & (place <= info[2:3]))
    return jnp.where(allowed, 0.0, NEGATIVE_HUGE)


def forward_body(ins, outs, tmp):
    qkv_ref, info_ref = ins
    out_ref, keep_ref, lse_ref = outs
    bias, acc, stat = tmp
    blocks, _, slots = qkv_ref.shape[:3]

    @pl.loop(0, blocks)
    def _(i):
        bias[...] = diagonal_bias(info_ref[i])
        seg = segment_rows(info_ref[i, 1:2])
        qa = [jnp.concatenate([qkv_ref[i, 0, m], seg], axis=0) for m in range(slots)]
        for m in range(slots):
            s = dot(jnp.transpose(qkv_ref[i, 1, m]), qkv_ref[i, 0, m]) + bias[...]
            top = jnp.max(s, axis=0, keepdims=True)
            p = jnp.exp(s - top)
            stat[2 * m : 2 * m + 1] = top
            stat[2 * m + 1 : 2 * m + 2] = jnp.sum(p, axis=0, keepdims=True)
            acc[m] = dot(qkv_ref[i, 2, m], p.astype(bf16))

        @pl.loop(0, i)
        def _(j):
            mask = mask_rows(info_ref[j, 0:1])
            for m in range(slots):
                ka = jnp.transpose(jnp.concatenate([qkv_ref[j, 1, m], mask], axis=0))
                s = dot(ka, qa[m])
                old = stat[2 * m : 2 * m + 1]
                top = jnp.maximum(old, jnp.max(s, axis=0, keepdims=True))
                p = jnp.exp(s - top)
                factor = jnp.exp(old - top)
                stat[2 * m : 2 * m + 1] = top
                stat[2 * m + 1 : 2 * m + 2] = stat[2 * m + 1 : 2 * m + 2] * factor + jnp.sum(
                    p, axis=0, keepdims=True
                )
                acc[m] = acc[m] * factor + dot(qkv_ref[j, 2, m], p.astype(bf16))

        for m in range(slots):
            total = stat[2 * m + 1 : 2 * m + 2]
            result = acc[m] / total
            out_ref[i, m] = result.astype(bf16)
            keep_ref[i, m] = result
            lse_ref[i, m : m + 1] = stat[2 * m : 2 * m + 1] + jnp.log(total)


def backward_body(ins, outs, tmp):
    qkv_ref, do_ref, keep_ref, lse_ref, info_ref = ins
    (out_ref,) = outs
    bias, dq, qn, don, delta = tmp
    blocks, _, slots = qkv_ref.shape[:3]

    @pl.loop(0, blocks)
    def _(i):
        for m in range(slots):
            qn[i, m] = jnp.transpose(qkv_ref[i, 0, m])
            don[i, m] = jnp.transpose(do_ref[i, m])
            delta[i, m : m + 1] = jnp.sum(
                do_ref[i, m].astype(f32) * keep_ref[i, m], axis=0, keepdims=True
            )
            dq[i, m] = jnp.zeros_like(dq[i, m])

    @pl.loop(0, blocks)
    def _(j):
        bias[...] = diagonal_bias(info_ref[j])
        mask = mask_rows(info_ref[j, 0:1])
        kn = [jnp.transpose(qkv_ref[j, 1, m]) for m in range(slots)]
        ka = [
            jnp.transpose(jnp.concatenate([qkv_ref[j, 1, m], mask], axis=0)) for m in range(slots)
        ]
        vn = [jnp.transpose(qkv_ref[j, 2, m]) for m in range(slots)]

        def tile(i, m, s):
            p = jnp.exp(s - lse_ref[i, m : m + 1])
            dp = dot(vn[m], do_ref[i, m])
            ds = (p * (dp - delta[i, m : m + 1])).astype(bf16)
            dq[i, m] += dot(qkv_ref[j, 1, m], ds)
            return dot(ds, qn[i, m]), dot(p.astype(bf16), don[i, m])

        start = []
        for m in range(slots):
            start += list(tile(j, m, dot(kn[m], qkv_ref[j, 0, m]) + bias[...]))

        def later(i, carry):
            seg = segment_rows(info_ref[i, 1:2])
            new = []
            for m in range(slots):
                qa = jnp.concatenate([qkv_ref[i, 0, m], seg], axis=0)
                a, b = tile(i, m, dot(ka[m], qa))
                new += [carry[2 * m] + a, carry[2 * m + 1] + b]
            return tuple(new)

        done = lax.fori_loop(j + 1, blocks, later, tuple(start))
        for m in range(slots):
            out_ref[j, 1, m] = jnp.transpose(done[2 * m]).astype(bf16)
            out_ref[j, 2, m] = jnp.transpose(done[2 * m + 1]).astype(bf16)


    @pl.loop(0, blocks)
    def _(i):
        for m in range(slots):
            out_ref[i, 0, m] = (dq[i, m] * HEAD_DIM ** (-0.5)).astype(bf16)


def ffn_kernel(x_ref, gf_ref, gu_ref, down_ref, part_ref, gu_grad_ref, down_grad_ref, ffn, dx):
    k = pl.program_id(0)
    half = gu_ref.shape[1] // 2
    x, gf = x_ref[...], gf_ref[...]
    both = dot(x, gu_ref[...])
    gate, up = both[:, :half], both[:, half:]
    sig = 1.0 / (1.0 + jnp.exp(-gate))
    act = gate * sig
    hidden = (act * up).astype(bf16)
    grad_hidden = dot(gf, down_ref[...], 1, 1)
    grad_gate = (grad_hidden * up * (sig * (1.0 + gate * (1.0 - sig)))).astype(bf16)
    grad_up = (grad_hidden * act).astype(bf16)
    grads = jnp.concatenate([grad_gate, grad_up], axis=1)
    ffn_now = dot(hidden, down_ref[...])
    dx_now = dot(grads, gu_ref[...], 1, 1)

    @pl.when(k == 0)
    def _():
        ffn[...] = ffn_now
        dx[...] = dx_now

    @pl.when(k > 0)
    def _():
        ffn[...] += ffn_now
        dx[...] += dx_now

    gu_grad = dot(x, grads, 0, 0)
    shards, padded = gu_grad_ref.shape[:2]
    filled = x.shape[1] // shards
    for z in range(shards):
        gu_grad_ref[z, :filled] = gu_grad[z * filled : (z + 1) * filled].astype(bf16)
        if padded > filled:
            gu_grad_ref[z, filled:] = jnp.zeros((padded - filled, gu_grad.shape[1]), bf16)
    down_grad_ref[...] = dot(hidden, gf, 0, 0).astype(bf16)

    @pl.when(k == pl.num_programs(0) - 1)
    def _():
        rows = part_ref.shape[2]
        for c in range(2):
            part_ref[c, 0] = dx[c * rows : (c + 1) * rows].astype(bf16)
            part_ref[c, 1] = ffn[c * rows : (c + 1) * rows].astype(bf16)


def feed_forward(x, gf, gate_up, down, shards, padded):
    tokens, width = x.shape
    hidden, columns = FF_CHUNK, 2 * FF_CHUNK
    chunks = gate_up.shape[1] // columns
    return pl.pallas_call(
        ffn_kernel,
        grid=(chunks,),
        in_specs=[
            pl.BlockSpec((tokens, width), lambda k: (0, 0)),
            pl.BlockSpec((tokens, width), lambda k: (0, 0)),
            pl.BlockSpec((width, columns), lambda k: (0, k)),
            pl.BlockSpec((hidden, width), lambda k: (k, 0)),
        ],
        out_specs=[
            pl.BlockSpec((2, 2, tokens // 2, width), lambda k: (0, 0, 0, 0)),
            pl.BlockSpec((shards, padded, columns), lambda k: (0, 0, k)),
            pl.BlockSpec((hidden, width), lambda k: (k, 0)),
        ],
        out_shape=[
            jax.ShapeDtypeStruct((2, 2, tokens // 2, width), bf16),
            jax.ShapeDtypeStruct((shards, padded, chunks * columns), bf16),
            jax.ShapeDtypeStruct(down.shape, bf16),
        ],
        scratch_shapes=[pltpu.VMEM((tokens, width), f32), pltpu.VMEM((tokens, width), f32)],
        name="feed_forward",
    )(x, gf, gate_up, down)


def rms_scale(rows, gain):
    return rows * lax.rsqrt(jnp.mean(rows * rows, axis=-1, keepdims=True) + EPSILON) * gain


def norm_back(rows, gain, grad):
    r = lax.rsqrt(jnp.mean(rows * rows, axis=-1, keepdims=True) + EPSILON)
    scaled = gain * grad
    back = r * scaled - rows * (r * r * r) * jnp.mean(scaled * rows, axis=-1, keepdims=True)
    return back, jnp.sum(grad * rows * r, axis=0)


def line_layout(lengths_row, positions):
    seq_ends = jnp.cumsum(lengths_row, dtype=jnp.int32)
    reached = seq_ends[None, :] <= positions[:, None]
    segment = jnp.sum(reached.astype(jnp.int32), axis=1)
    starts = jnp.max(jnp.where(reached, seq_ends[None, :], 0), axis=1)
    return segment, positions - starts, positions < seq_ends[-1]


def project_body(ins, outs, tmp):
    hidden_ref, weight_ref, gain_ref, cos_ref, sin_ref = ins
    sent_ref, normed_ref = outs
    reps, _, slots, _, rows = sent_ref.shape
    hidden = hidden_ref[...].astype(f32)
    normed = rms_scale(hidden, gain_ref[...]).astype(bf16)
    normed_ref[...] = normed
    cosines, sines = cos_ref[...], sin_ref[...]
    half, columns = HEAD_DIM // 2, weight_ref.shape[1]

    def put(kind, head, value):
        sent_ref[head // slots, kind, head % slots] = value

    for start in range(0, columns, 256):
        stop = min(start + 256, columns)
        block = jnp.transpose(dot(normed, weight_ref[:, start:stop]))
        for head in range(start // HEAD_DIM, stop // HEAD_DIM):
            at = head * HEAD_DIM - start
            a, b = block[at : at + half], block[at + half : at + HEAD_DIM]
            if head < QUERY_HEADS:
                scale = HEAD_DIM ** (-0.5)
                put(
                    0,
                    head,
                    (
                        jnp.concatenate(
                            [a * cosines - b * sines, b * cosines + a * sines], axis=0
                        )
                        * scale
                    ).astype(bf16),
                )
            elif head < QUERY_HEADS + KEY_VALUE_HEADS:
                value = jnp.concatenate(
                    [a * cosines - b * sines, b * cosines + a * sines], axis=0
                ).astype(bf16)
                for m in range(GROUP):
                    put(1, (head - QUERY_HEADS) * GROUP + m, value)
            else:
                value = block[at : at + HEAD_DIM].astype(bf16)
                for m in range(GROUP):
                    put(2, (head - QUERY_HEADS - KEY_VALUE_HEADS) * GROUP + m, value)
    for head in range(QUERY_HEADS, reps * slots):
        for kind in range(3):
            put(kind, head, jnp.zeros((HEAD_DIM, rows), bf16))


def project_back_body(ins, outs, tmp):
    grads_ref, cos_ref, sin_ref, weight_ref, hidden_ref, normed_ref, gain_ref, base_ref = ins
    sent_ref, weight_grad_ref, gain_grad_ref = outs
    (dt,) = tmp
    slots, half = grads_ref.shape[2], HEAD_DIM // 2
    cosines, sines = cos_ref[...], sin_ref[...]

    def get(kind, head):
        return grads_ref[head // slots, kind, head % slots].astype(f32)

    def back(value):
        a, b = value[:half], value[half:]
        return jnp.concatenate([a * cosines + b * sines, b * cosines - a * sines], axis=0)

    for head in range(QUERY_HEADS):
        dt[head * HEAD_DIM : (head + 1) * HEAD_DIM] = back(get(0, head)).astype(bf16)
    for group in range(KEY_VALUE_HEADS):
        for kind in (1, 2):
            value = get(kind, group * GROUP)
            for m in range(1, GROUP):
                value = value + get(kind, group * GROUP + m)
            if kind == 1:
                value = back(value)
            at = (QUERY_HEADS + (kind - 1) * KEY_VALUE_HEADS + group) * HEAD_DIM
            dt[at : at + HEAD_DIM] = value.astype(bf16)
    grad = dot(dt[...], weight_ref[...], 0, 1)
    norm_grad, gain_grad = norm_back(hidden_ref[...].astype(f32), gain_ref[...], grad)
    gain_grad_ref[...] = jnp.broadcast_to(gain_grad[None], gain_grad_ref.shape)
    total = (base_ref[...] + norm_grad).astype(bf16)
    devices, per_pair = sent_ref.shape[:2]
    sent_ref[...] = total.reshape(sent_ref.shape)
    shards, reps, unit, columns = weight_grad_ref.shape
    filled = normed_ref.shape[1] // shards
    for start in range(0, columns, 256):
        stop = min(start + 256, columns)
        block = dot(normed_ref[...], dt[start:stop], 0, 1)
        for z in range(shards):
            for r in range(reps):
                size = max(0, min(unit, filled - r * unit))
                at = z * filled + r * unit
                if size:
                    weight_grad_ref[z, r, :size, start:stop] = block[at : at + size].astype(bf16)
                if size < unit:
                    weight_grad_ref[z, r, size:, start:stop] = jnp.zeros(
                        (unit - size, stop - start), bf16
                    )


def rounded_up(value, unit):
    return -(-value // unit) * unit


def local(
    sizes,
    hidden_in,
    cotangent,
    destination,
    seq_lengths,
    gate_mask,
    query_weight,
    key_matrix,
    value_matrix,
    out_weight,
    gate_weight,
    up_weight,
    down_weight,
    attn_gain,
    ffn_gain,
    router_weight,
):
    rows, width = hidden_in.shape
    chips, shards = sizes["chip"], sizes["shard"]
    reps = 2 * chips
    devices = reps * shards
    per_pair = rows // devices
    slots = -(-QUERY_HEADS // reps)
    padded_heads = slots * reps
    chip, core, shard = lax.axis_index("chip"), lax.axis_index("core"), lax.axis_index("shard")
    rep = lax.axis_index(REP)
    shard_rows = query_weight.shape[0]
    rep_unit = rounded_up(-(-shard_rows // reps), 8)
    padded = rep_unit * reps
    chip_unit = padded // chips
    ff_half = gate_weight.shape[1] // 2
    chunks = ff_half // FF_CHUNK

    def padded_rows(array):
        return jnp.pad(array, ((0, padded - shard_rows), (0, 0)))

    qkv_shard = padded_rows(jnp.concatenate([query_weight, key_matrix, value_matrix], axis=1))
    qkv_shard = qkv_shard.reshape(reps, rep_unit, -1)
    out_shard = padded_rows(out_weight).reshape(reps, rep_unit, width)
    halves = [
        lax.dynamic_slice_in_dim(w, core * ff_half, ff_half, 1).reshape(
            shard_rows, chunks, 1, FF_CHUNK
        )
        for w in (gate_weight, up_weight)
    ]
    gate_up_shard = jnp.concatenate(halves, axis=2).reshape(shard_rows, 2 * ff_half)
    gate_up_shard = padded_rows(gate_up_shard).reshape(chips, chip_unit, 2 * ff_half)
    down_unit = down_weight.shape[0] // chips
    down_shard = down_weight.reshape(chips, down_unit, width)
    vectors = jnp.stack([attn_gain, ffn_gain, router_weight]).astype(f32)
    vectors = jnp.pad(vectors, ((0, 5), (0, 0)))

    def full_rows(full):
        full = full.reshape(shards, padded, full.shape[-1])
        return full[:, :shard_rows].reshape(width, full.shape[-1])

    row_index = jnp.arange(rows, dtype=jnp.int32)
    target = destination // rows
    earlier = (target[None, :] == target[:, None]) & (row_index[None, :] < row_index[:, None])
    slot_of_row = target * per_pair + jnp.sum(earlier.astype(jnp.int32), axis=1)
    to_slot = slot_of_row[None, :] == row_index[:, None]
    to_slot_b = to_slot.astype(bf16)
    place_sent = jnp.sum(jnp.where(to_slot, (destination % rows)[None, :], 0), axis=1)
    place_sent = place_sent.reshape(devices, 1, per_pair)
    place_sent = jnp.pad(place_sent, ((0, 0), (0, 0), (0, 128 - per_pair)))

    def by_slot(tokens):
        tokens = jnp.dot(to_slot_b, tokens, preferred_element_type=f32).astype(bf16)
        return tokens.reshape(devices, per_pair, width)

    got_hidden, got_place, vectors_got, qkv_full = run(
        1,
        "first",
        sizes,
        [
            AllToAll(sizes, by_slot(hidden_in), ALL),
            AllToAll(sizes, place_sent, ALL),
            AllToAll(sizes, vectors, ("shard",), spread=True),
            Gather(sizes, qkv_shard, REP, "both"),
        ],
    )
    hidden = got_hidden.reshape(rows, width)
    place = got_place[:, 0, :per_pair].reshape(rows)
    qkv_full = full_rows(qkv_full)
    vectors_full = jnp.transpose(vectors_got[:, :3], (1, 0, 2)).reshape(3, width)
    gain_one, gain_two, full_router = vectors_full[0], vectors_full[1], vectors_full[2]

    positions = rep * rows + place
    segment, within, is_valid = line_layout(seq_lengths[0], positions)
    here = place[:, None] == row_index[None, :]
    gate_here = jnp.sum(jnp.where(here, gate_mask[None, :], 0), axis=1)
    active = is_valid & (gate_here == 1)
    key_code = jnp.where(active, segment, -1)
    active_f = active.astype(f32)
    info = jnp.pad(jnp.stack([key_code, segment, place]), ((0, 5), (0, 0)))
    steps = jnp.arange(HEAD_DIM // 2).astype(f32)
    frequency = jnp.power(ROPE_BASE, -2.0 * steps / HEAD_DIM)
    angles = frequency[:, None] * within.astype(f32)[None, :]
    cosines, sines = jnp.cos(angles), jnp.sin(angles)

    heads_shape = (reps, 3, slots, HEAD_DIM, rows)
    heads_type = jax.ShapeDtypeStruct(heads_shape, bf16)
    gate_up_z, down_z, out_z, info_got, qkv_got, _, first_normalized = run(
        2,
        "project",
        sizes,
        [
            Gather(sizes, gate_up_shard, ("chip",), "z"),
            Gather(sizes, down_shard, ("chip",), "z", half=True),
            Gather(sizes, out_shard, REP, "z"),
            AllToAll(sizes, info, REP, spread=True),
            AllToAll(sizes, heads_type, REP, late=True, source=0),
        ],
        Compute(
            project_body,
            [hidden, qkv_full, gain_one[None], cosines, sines],
            [heads_type, jax.ShapeDtypeStruct((rows, width), bf16)],
        ),
    )
    slot_type = jax.ShapeDtypeStruct((reps, slots, HEAD_DIM, rows), bf16)
    gate_up_full, down_full, out_full, got_grad, att_home, _, att_keep, lse = run(
        3,
        "attend",
        sizes,
        [
            Gather(sizes, gate_up_z, ("chip",), "plane"),
            Gather(sizes, down_z, ("chip",), "plane", half=True),
            Gather(sizes, out_z, REP, "plane"),
            AllToAll(sizes, by_slot(cotangent), ALL),
            AllToAll(sizes, slot_type, REP, late=True, source=0),
        ],
        Compute(
            forward_body,
            [qkv_got, info_got],
            [
                slot_type,
                jax.ShapeDtypeStruct(slot_type.shape, f32),
                jax.ShapeDtypeStruct((reps, 8, rows), f32),
            ],
            [
                pltpu.VMEM((rows, rows), f32),
                pltpu.VMEM((slots, HEAD_DIM, rows), f32),
                pltpu.VMEM((8, rows), f32),
            ],
        ),
    )
    attn_out_t = att_home.reshape(padded_heads * HEAD_DIM, rows)[:width]
    full_out = full_rows(out_full)
    gate_up = full_rows(gate_up_full)
    down = down_full.reshape(ff_half, width)

    hidden_f = hidden.astype(f32)
    router_logit = jnp.sum(hidden_f * full_router, axis=1)
    gate_value = jax.nn.sigmoid(router_logit)
    branch_scale = active_f * gate_value
    attn_branch = jnp.einsum("dt,de->te", attn_out_t, full_out, preferred_element_type=f32)
    middle = hidden_f + attn_branch
    normed_two = rms_scale(middle, gain_two).astype(bf16)
    grad_out = got_grad.reshape(rows, width).astype(f32)
    grad_branch = branch_scale[:, None] * grad_out
    grad_ffn = grad_branch.astype(bf16)
    x_pair, gf_pair = run(
        4,
        "pair",
        sizes,
        [
            AllToAll(sizes, normed_two, ("core",), spread=True),
            AllToAll(sizes, grad_ffn, ("core",), spread=True),
        ],
    )
    parts, gate_up_grad, down_grad = feed_forward(
        x_pair.reshape(2 * rows, width),
        gf_pair.reshape(2 * rows, width),
        gate_up,
        down,
        shards,
        padded,
    )
    (parts_got,) = run(5, "parts", sizes, [AllToAll(sizes, parts, ("core",))])
    grad_normed_two = parts_got[0, 0].astype(f32) + parts_got[1, 0].astype(f32)
    ffn_branch = parts_got[0, 1].astype(f32) + parts_got[1, 1].astype(f32)
    branch_sum = attn_branch + ffn_branch
    result = (hidden_f + branch_scale[:, None] * branch_sum).astype(bf16)
    grad_logit = active_f * jnp.sum(grad_out * branch_sum, axis=1) * gate_value * (1.0 - gate_value)
    grad_middle, grad_gain_ffn = norm_back(middle, gain_two, grad_normed_two)
    grad_attn = (grad_branch + grad_middle).astype(bf16)
    grad_attention_t = jnp.einsum("te,de->dt", grad_attn, full_out, preferred_element_type=f32)
    grad_attention_t = jnp.pad(
        grad_attention_t.astype(bf16), ((0, padded_heads * HEAD_DIM - width), (0, 0))
    ).reshape(slot_type.shape)
    (grad_got,) = run(6, "grads", sizes, [AllToAll(sizes, grad_attention_t, REP)])

    out_grad = jnp.einsum("dt,te->de", attn_out_t, grad_attn, preferred_element_type=f32)
    out_grad = jnp.pad(
        out_grad.astype(bf16).reshape(shards, shard_rows, width),
        ((0, 0), (0, padded - shard_rows), (0, 0)),
    ).reshape(shards, reps, rep_unit, width)
    gate_up_grad = gate_up_grad.reshape(shards, chips, chip_unit, 2 * ff_half)
    down_grad = down_grad.reshape(shards // 2, chips, down_unit, width)
    gate_up_recv, down_recv, out_recv, home_out, heads_home, _ = run(
        7,
        "attend_back",
        sizes,
        [
            Scatter(sizes, gate_up_grad, ("chip",), 1),
            Scatter(sizes, down_grad, ("chip",), 1),
            Scatter(sizes, out_grad, REP, 1),
            AllToAll(sizes, result.reshape(devices, per_pair, width), ALL),
            AllToAll(sizes, heads_type, REP, late=True, source=0),
        ],
        Compute(
            backward_body,
            [qkv_got, grad_got, att_keep, lse, info_got],
            [heads_type],
            [
                pltpu.VMEM((rows, rows), f32),
                pltpu.VMEM((reps, slots, HEAD_DIM, rows), f32),
                pltpu.VMEM((reps, slots, rows, HEAD_DIM), bf16),
                pltpu.VMEM((reps, slots, rows, HEAD_DIM), bf16),
                pltpu.VMEM((reps, 8, rows), f32),
            ],
        ),
    )

    def summed(own, got):
        total = own.astype(f32)
        for index in range(got.shape[0]):
            total = total + got[index].astype(f32)
        return total.astype(bf16)

    def taken(array, index, dim):
        return lax.dynamic_index_in_dim(array, index, dim, keepdims=False)

    gate_up_sum = summed(taken(gate_up_grad, chip, 1), gate_up_recv)
    down_sum = summed(taken(down_grad, chip, 1), down_recv)
    out_sum = summed(taken(out_grad, rep, 1), out_recv)

    base = grad_out + grad_middle + grad_logit[:, None] * full_router
    tokens_type = jax.ShapeDtypeStruct((devices, per_pair, width), bf16)
    qkv_grad_type = jax.ShapeDtypeStruct((shards, reps, rep_unit, qkv_full.shape[1]), bf16)
    gate_up_recv, down_recv, out_recv, home_grad, qkv_recv, _, qkv_grad, gain_grad = run(
        8,
        "project_back",
        sizes,
        [
            Scatter(sizes, gate_up_sum, ("shard",), 0),
            Scatter(sizes, down_sum, ("shard",), 0, half=True),
            Scatter(sizes, out_sum, ("shard",), 0),
            AllToAll(sizes, tokens_type, ALL, late=True, source=0),
            Scatter(sizes, qkv_grad_type, REP, 1, late=True, source=1),
        ],
        Compute(
            project_back_body,
            [
                heads_home,
                cosines,
                sines,
                qkv_full,
                hidden,
                first_normalized,
                gain_one[None],
                base,
            ],
            [tokens_type, qkv_grad_type, jax.ShapeDtypeStruct((8, width), f32)],
            [pltpu.VMEM((qkv_full.shape[1], rows), bf16)],
        ),
    )
    gate_up_sum = summed(taken(gate_up_sum, shard, 0), gate_up_recv)
    down_sum = summed(taken(down_sum, lax.rem(shard, shards // 2), 0), down_recv)
    out_sum = summed(taken(out_sum, shard, 0), out_recv)
    qkv_sum = summed(taken(qkv_grad, rep, 1), qkv_recv)
    router_grad = jnp.sum(grad_logit[:, None] * hidden_f, axis=0)
    vector_grads = jnp.stack([gain_grad[0], grad_gain_ffn, router_grad])
    vector_grads = jnp.pad(vector_grads, ((0, 5), (0, 0))).reshape(8, shards, shard_rows)
    vector_grads = jnp.broadcast_to(
        jnp.transpose(vector_grads, (1, 0, 2))[None], (reps, shards, 8, shard_rows)
    ).reshape(devices, 8, shard_rows)
    gate_up_home, down_home, out_home, vectors_home, qkv_recv = run(
        9,
        "totals",
        sizes,
        [
            AllToAll(sizes, gate_up_sum, REP, spread=True),
            SpreadHalf(sizes, down_sum),
            AllToAll(sizes, out_sum, REP, spread=True),
            AllToAll(sizes, vector_grads, ALL),
            Scatter(sizes, qkv_sum, ("shard",), 0),
        ],
    )
    qkv_sum = summed(taken(qkv_sum, shard, 0), qkv_recv)
    (qkv_home,) = run(10, "last", sizes, [AllToAll(sizes, qkv_sum, REP, spread=True)])

    qkv_total = qkv_home.reshape(padded, -1)[:shard_rows].astype(f32)
    out_total = out_home.reshape(padded, width)[:shard_rows].astype(f32)
    gate_up_total = gate_up_home.reshape(chips, 2, chip_unit, chunks, 2, FF_CHUNK)

    def half_total(which):
        total = jnp.transpose(gate_up_total[:, :, :, :, which], (0, 2, 1, 3, 4))
        return total.reshape(padded, 2 * ff_half)[:shard_rows].astype(f32)

    vector_total = jnp.sum(vectors_home, axis=0)
    q_end, k_end = query_weight.shape[1], query_weight.shape[1] + key_matrix.shape[1]

    def home_rows(home):
        home = home.reshape(rows, width)
        return jnp.einsum("sr,sw->rw", to_slot_b, home, preferred_element_type=f32).astype(bf16)

    return (
        home_rows(home_out),
        home_rows(home_grad),
        qkv_total[:, :q_end],
        qkv_total[:, q_end:k_end],
        qkv_total[:, k_end:],
        out_total,
        half_total(0),
        half_total(1),
        down_home.reshape(-1, width).astype(f32),
        vector_total[0],
        vector_total[1],
        vector_total[2],
    )


def solution(mesh):
    reps, shards = mesh.shape["rep"], mesh.shape["shard"]
    sizes = {"chip": reps // 2, "core": 2, "shard": shards}
    split_mesh = Mesh(mesh.devices.reshape(reps // 2, 2, shards), ALL)
    tokens, tokens_1d = P(ALL, None), P(ALL)
    weight, vector = P("shard", None), P("shard")
    return jax.shard_map(
        functools.partial(local, sizes),
        mesh=split_mesh,
        in_specs=(tokens, tokens, tokens_1d, weight, tokens_1d) + (weight,) * 7 + (vector,) * 3,
        out_specs=(tokens, tokens) + (weight,) * 7 + (vector,) * 3,
        check_vma=False,
    )
```

```python
import functools

import jax
import jax.numpy as jnp
from jax import lax
from jax.experimental import pallas as pl
from jax.experimental.pallas import tpu as pltpu
from jax.sharding import Mesh
from jax.sharding import PartitionSpec as P

QUERY_HEADS = 15
KEY_VALUE_HEADS = 5
HEAD_DIM = 64
GROUP = QUERY_HEADS // KEY_VALUE_HEADS
EPSILON = 1e-05
NEGATIVE_HUGE = -1e30
ROPE_BASE = 10000.0
FF_CHUNK = 256
bf16 = jnp.bfloat16
f32 = jnp.float32
MESH = pl.DeviceIdType.MESH
REP = ("chip", "core")
ALL = ("chip", "core", "shard")
VMEM_SPEC = pl.BlockSpec(memory_space=pltpu.VMEM)
HBM_SPEC = pl.BlockSpec(memory_space=pl.ANY)


def dot(a, b, ca=1, cb=0):
    return lax.dot_general(a, b, (((ca,), (cb,)), ((), ())), preferred_element_type=f32)


def axes_size(sizes, axes):
    total = 1
    for name in axes:
        total *= sizes[name]
    return total


def peer_coords(index, axes, sizes):
    coords = {}
    for name in reversed(axes):
        coords[name] = lax.rem(index, sizes[name])
        index = index // sizes[name]
    return coords


def remote(src, dst, send_sem, recv_sem, coords):
    return pltpu.make_async_remote_copy(
        src_ref=src,
        dst_ref=dst,
        send_sem=send_sem,
        recv_sem=recv_sem,
        device_id=coords,
        device_id_type=MESH,
    )


def each(start, stop, body):
    def step(k, carry):
        body(k)
        return carry

    lax.fori_loop(start, stop, step, 0)


class Item:
    late = False
    final = False
    aliased = False
    pre = 0

    def steps(self, ins, outs, scratch):
        yield


class AllToAll(Item):
    final = True

    def __init__(self, sizes, array, axes, spread=False, by_shard=False, late=False, source=None):
        self.sizes, self.axes, self.spread, self.late = sizes, axes, spread, late
        self.by_shard = by_shard
        self.count = axes_size(sizes, axes)
        self.source = source
        self.inputs = [] if source is not None else [array]
        piece = tuple(array.shape) if spread else tuple(array.shape[1:])
        self.in_specs = [VMEM_SPEC] * len(self.inputs)
        self.out_shapes = [jax.ShapeDtypeStruct((self.count,) + piece, array.dtype)]
        self.out_specs = [VMEM_SPEC]
        self.scratch = [
            pltpu.SemaphoreType.DMA((self.count,)),
            pltpu.SemaphoreType.DMA((self.count,)),
        ]

    def index(self, peer):
        return lax.rem(peer, self.sizes["shard"]) if self.by_shard else peer

    def copy(self, k, ins, outs, scratch):
        me = lax.axis_index(self.axes)
        peer = lax.rem(me + k, self.count)
        return remote(
            ins[0] if self.spread else ins[0].at[self.index(peer)],
            outs[0].at[me],
            scratch[0].at[k],
            scratch[1].at[k],
            peer_coords(peer, self.axes, self.sizes),
        )

    def steps(self, ins, outs, scratch):
        each(1, self.count, lambda k: self.copy(k, ins, outs, scratch).start())
        me = lax.axis_index(self.axes)
        outs[0][me] = ins[0][...] if self.spread else ins[0][self.index(me)]
        yield
        each(1, self.count, lambda k: self.copy(k, ins, outs, scratch).wait())


class Heads(Item):
    final = True
    late = True

    def __init__(self, sizes, array, to, source):
        self.sizes, self.to, self.source = sizes, to, source
        self.count = axes_size(sizes, REP)
        self.slots = array.shape[1] // 3
        self.main = array.shape[1] if self.slots != 2 else 4
        self.units = array.shape[1]
        self.inputs, self.in_specs = [], []
        self.out_shapes = [jax.ShapeDtypeStruct(array.shape, array.dtype)]
        self.out_specs = [VMEM_SPEC]
        dma = pltpu.SemaphoreType.DMA
        self.scratch = [dma((2, self.count)), dma((2, self.count))]

    def copy(self, k, ins, outs, scratch, extra, sending):
        me = lax.axis_index(REP)
        peer = lax.rem(me + (k if sending else self.count - k), self.count)
        units = pl.ds(self.main, self.units - self.main) if extra else pl.ds(0, self.main)
        return peer, remote(
            ins[0].at[peer, units],
            outs[0].at[me if sending else peer, units],
            scratch[0].at[int(extra), k],
            scratch[1].at[int(extra), k],
            peer_coords(peer, REP, self.sizes),
        )

    def every(self, ins, outs, scratch, sending, act):
        def main(k):
            act(self.copy(k, ins, outs, scratch, False, sending)[1])

        def extra(k):
            peer, copy = self.copy(k, ins, outs, scratch, True, sending)
            owner = peer if sending == self.to else lax.axis_index(REP)
            pl.when(apart(owner) == 1)(lambda: act(copy))

        each(1, self.count, main)
        if self.units > self.main:
            each(1, self.count, extra)

    def steps(self, ins, outs, scratch):
        self.every(ins, outs, scratch, True, lambda copy: copy.start())
        me = lax.axis_index(REP)
        outs[0][me] = ins[0][me]
        yield
        self.every(ins, outs, scratch, False, lambda copy: copy.wait_recv())
        self.every(ins, outs, scratch, True, lambda copy: copy.wait_send())


def apart(rep):
    last = KEY_VALUE_HEADS - 1
    return jnp.minimum((2 * rep + 1) // GROUP, last) - jnp.minimum((2 * rep) // GROUP, last)


def key_slots(slots):
    return [0, apart(lax.axis_index(REP))] if slots == 2 else list(range(slots))


def key_unit(slots, slot):
    return slots + 2 * slot


def value_unit(slots, slot):
    return slots + 2 * slot + 1


def flipped(chip, k):
    x, y = lax.rem(chip, 2), chip // 2
    x = 1 - x if k in (1, 3) else x
    y = 1 - y if k in (2, 3) else y
    return 2 * y + x


class Plane:
    def __init__(self, sizes, pair, lo, hi):
        self.pair, self.lo, self.hi, self.chips = pair, lo, hi, sizes["chip"]
        self.relay = self.chips == 4
        self.near = (1, 2) if self.relay else tuple(range(1, self.chips))
        self.scratch = [pltpu.SemaphoreType.DMA((self.chips, hi))] * (4 if pair else 2)

    def bind(self, region, path, guard, other, sems):
        self.region, self.path, self.guard, self.other, self.sems = region, path, guard, other, sems
        self.chip, self.core = lax.axis_index("chip"), lax.axis_index("core")

    def peer(self, k):
        return flipped(self.chip, k) if self.relay else lax.rem(self.chip + k, self.chips)

    def owner(self, k):
        if self.relay:
            return flipped(self.chip, k)
        return lax.rem(self.chip + self.chips - k, self.chips)

    def copy(self, t, k, owner, to):
        ref = self.region(t, owner, self.core)
        return remote(ref, ref, self.sems[0].at[k, t], self.sems[1].at[k, t], {"chip": to})

    def relayed(self, t, k):
        return self.copy(t, 3, self.owner(k), self.peer(3 - k))

    def pass_on(self, t, owner, core=None):
        ref = self.region(t, owner, self.core if core is None else core)
        return remote(
            ref, ref, self.sems[2].at[owner, t], self.sems[3].at[owner, t], {"core": 1 - self.core}
        )

    def parts(self, body, guard=None):
        each(self.lo, self.hi, lambda t: (guard or self.guard)(t, lambda: body(t)))

    def start(self):
        def part(t):
            for k in self.near:
                self.copy(t, k, self.chip, self.peer(k)).start()
            if self.pair:
                self.pass_on(t, self.chip).start()

        self.parts(part)

    def forward(self):
        def arrived(t, k):
            self.copy(t, k, self.owner(k), self.chip).wait_recv()
            if self.pair:
                self.pass_on(t, self.owner(k)).start()

        def part(t):
            for k in self.near:
                arrived(t, k)
                if self.relay:
                    pl.when(self.path(t) == k - 1)(lambda: self.relayed(t, k).start())

        self.parts(part)
        if self.relay:
            self.parts(lambda t: arrived(t, 3))

    def finish(self):
        def sent(t):
            for k in self.near:
                self.copy(t, k, self.chip, self.peer(k)).wait_send()
                if self.relay:
                    pl.when(self.path(t) == k - 1)(lambda: self.relayed(t, k).wait_send())
            if self.pair:
                each(0, self.chips, lambda c: self.pass_on(t, c).wait_send())

        self.parts(sent)
        if self.pair:
            self.parts(
                lambda t: each(
                    0, self.chips, lambda c: self.pass_on(t, c, 1 - self.core).wait_recv()
                ),
                self.other,
            )


def always(t, body):
    body()


class Gather(Item):
    def __init__(self, sizes, array, split_axes, stages, half=False):
        self.sizes, self.split_axes, self.stages, self.half = sizes, split_axes, stages, half
        self.shards = sizes["shard"]
        self.slots = self.shards // 2 if half else self.shards
        self.pair = len(split_axes) == 2
        both = stages == "both"
        self.pre = 0 if stages == "plane" else 1
        self.inputs = [array]
        self.in_specs = [VMEM_SPEC if both else HBM_SPEC]
        if stages == "plane":
            shape, self.aliased = tuple(array.shape), True
        else:
            shape = (self.slots,) + tuple(array.shape)
        self.out_shapes = [jax.ShapeDtypeStruct(shape, array.dtype)]
        self.out_specs = [VMEM_SPEC if both else HBM_SPEC]
        dma = pltpu.SemaphoreType.DMA
        self.scratch = []
        if stages != "plane":
            self.scratch += [dma((self.shards,)), dma((self.shards,))]
        if stages == "z":
            self.scratch += [pltpu.VMEM(array.shape, array.dtype), dma((2,))]
        else:
            self.plane = Plane(sizes, self.pair, 1, self.shards)
            self.scratch += self.plane.scratch

    def guarded(self, z, body):
        if self.half:
            pl.when(z // self.slots == lax.axis_index("core"))(body)
        else:
            body()

    def slot(self, z):
        return lax.rem(z, self.slots) if self.half else z

    def z_copy(self, k, src, full, scratch, sending):
        me = lax.axis_index("shard")
        mine = lax.axis_index(self.split_axes)
        peer = lax.rem(me + k, self.shards) if sending else lax.rem(me + self.shards - k, self.shards)
        source = me if sending else peer
        dst = full.at[self.slot(source), mine]
        return remote(
            src.at[mine] if sending else dst,
            dst,
            scratch[0].at[k],
            scratch[1].at[k],
            {"shard": peer},
        )

    def z_start(self, src, full, scratch):
        self.guarded(
            lax.axis_index("shard"),
            lambda: each(1, self.shards, lambda k: self.z_copy(k, src, full, scratch, True).start()),
        )

    def z_finish(self, src, full, scratch):
        me = lax.axis_index("shard")

        def receive(k):
            peer = lax.rem(me + self.shards - k, self.shards)
            self.guarded(
                peer, lambda: self.z_copy(k, src, full, scratch, False).wait_recv()
            )

        each(1, self.shards, receive)

        def sent():
            each(1, self.shards, lambda k: self.z_copy(k, src, full, scratch, True).wait_send())

        self.guarded(me, sent)

    def steps(self, ins, outs, scratch):
        me = lax.axis_index("shard")
        src, full = ins[0], outs[0]
        if self.stages == "z":
            self.z_start(src, full, scratch)
            load = pltpu.make_async_copy(src, scratch[2], scratch[3].at[0])
            store = pltpu.make_async_copy(scratch[2], full.at[self.slot(me)], scratch[3].at[1])
            self.guarded(me, load.start)
            yield

            def both():
                load.wait()
                store.start()

            self.guarded(me, both)
            yield
            self.guarded(me, store.wait)
            self.z_finish(src, full, scratch)
            return

        def shard_of(t):
            return lax.rem(me + t, self.shards)

        def region(t, chip, core):
            return full.at[self.slot(shard_of(t)), 2 * chip + core if self.pair else chip]

        guard = (lambda t, body: self.guarded(shard_of(t), body)) if self.half else always
        if self.stages == "both":
            self.z_start(src, full, scratch)
            full[me] = src[...]
            yield
            self.z_finish(src, full, scratch)
        self.plane.bind(
            region, lambda t: lax.rem(shard_of(t), 2), guard, always, scratch[-len(self.plane.scratch) :]
        )
        self.plane.start()
        yield
        self.plane.forward()
        yield
        self.plane.finish()


class Reduce(Item):
    def __init__(self, sizes, array, stages, half=False, late=False, source=None):
        self.stages, self.half, self.late, self.source = stages, half, late, source
        self.pre = int(stages[0] == "pair" and not late)
        self.chips, self.shards = sizes["chip"], sizes["shard"]
        self.slots = self.shards // 2
        lead = {"pair": 3, "plane": 2, "shard": 1, "spread": 0}[stages[0]]
        unit = tuple(array.shape[lead:])
        self.zs = array.shape[0]
        zs, chips, dtype = self.zs, self.chips, array.dtype
        self.inputs = [] if source is not None else [array]
        self.from_hbm = source is None and stages[0] == "plane"
        self.in_specs = [HBM_SPEC if self.from_hbm else VMEM_SPEC] * len(self.inputs)
        self.names, self.scratch = [], []

        def add(name, buffer):
            self.names.append(name)
            self.scratch.append(buffer)

        dma = pltpu.SemaphoreType.DMA
        if "pair" in stages:
            add("pair_got", pltpu.VMEM((zs, chips) + unit, dtype))
            add("pair_sum", pltpu.VMEM((zs, chips) + unit, dtype))
            add("pair_sems", dma((2,)))
        if "plane" in stages:
            add("plane_got", pltpu.VMEM((chips - 1, zs) + unit, dtype))
            add("plane_sent", dma((chips,)))
            add("plane_arrived", dma((chips,)))
            if self.from_hbm:
                add("plane_own", pltpu.VMEM((zs,) + unit, dtype))
                add("own_sems", dma((1,)))
            if stages[-1] != "plane":
                add("plane_sum", pltpu.VMEM((zs,) + unit, dtype))
        if "shard" in stages:
            add("shard_got", pltpu.VMEM((self.shards - 1,) + unit, dtype))
            add("shard_sent", dma((self.shards,)))
            add("shard_arrived", dma((self.shards,)))
        shape = (zs,) + unit if stages[-1] == "plane" else unit
        if stages[-1] == "spread":
            shape = (chips,) + (() if half else (2,)) + unit
            self.plane = Plane(sizes, True, 0, unit[0])
            for index, buffer in enumerate(self.plane.scratch):
                add("spread%d" % index, buffer)
        self.out_shapes = [jax.ShapeDtypeStruct(shape, dtype)]
        self.out_specs = [VMEM_SPEC]

    def steps(self, ins, outs, scratch):
        buf = dict(zip(self.names, scratch))
        chip, core, shard = (lax.axis_index(name) for name in ALL)
        now, out, last, sent = ins[0], outs[0], self.stages[-1], []
        mine = out.at[chip] if self.half else out.at[chip, core]

        def carrying(index):
            return index // self.slots == core

        def guard(t, body):
            if self.half:
                pl.when(carrying(shard))(body)
            else:
                body()

        def other(t, body):
            if self.half:
                pl.when(jnp.logical_not(carrying(shard)))(body)
            else:
                body()

        if "pair" in self.stages:
            pair = remote(
                now.at[:, :, 1 - core],
                buf["pair_got"],
                buf["pair_sems"].at[0],
                buf["pair_sems"].at[1],
                {"core": 1 - core},
            )
            pair.start()
            yield
            pair.wait()
            given = now

            def add_pair(index):
                z, c = index // self.chips, lax.rem(index, self.chips)
                total = given[z, c, core].astype(f32) + buf["pair_got"][z, c].astype(f32)
                buf["pair_sum"][z, c] = total.astype(bf16)

            each(0, self.zs * self.chips, add_pair)
            now = buf["pair_sum"]
        if "plane" in self.stages:
            partial = now

            def plane_copy(k):
                peer = lax.rem(chip + k, self.chips)
                return remote(
                    partial.at[:, peer],
                    buf["plane_got"].at[k - 1],
                    buf["plane_sent"].at[k],
                    buf["plane_arrived"].at[k],
                    {"chip": peer},
                )

            each(1, self.chips, lambda k: plane_copy(k).start())
            if self.from_hbm:
                own = pltpu.make_async_copy(
                    partial.at[:, chip], buf["plane_own"], buf["own_sems"].at[0]
                )
                own.start()
            yield
            each(1, self.chips, lambda k: plane_copy(k).wait_recv())
            if self.from_hbm:
                own.wait()
            target = out if last == "plane" else buf["plane_sum"]

            def add_plane(z):
                total = (buf["plane_own"][z] if self.from_hbm else partial[z, chip]).astype(f32)
                for k in range(self.chips - 1):
                    total = total + buf["plane_got"][k, z].astype(f32)
                target[z] = total.astype(bf16)

            each(0, self.zs, add_plane)
            sent.append(lambda: each(1, self.chips, lambda k: plane_copy(k).wait_send()))
            now = target
        if "shard" in self.stages:
            summed = now

            def slot(index):
                return lax.rem(index, self.slots) if self.half else index

            def shard_copy(k):
                peer = lax.rem(shard + k, self.shards)
                return peer, remote(
                    summed.at[slot(peer)],
                    buf["shard_got"].at[k - 1],
                    buf["shard_sent"].at[k],
                    buf["shard_arrived"].at[k],
                    {"shard": peer},
                )

            def shard_each(act):
                def one(k):
                    peer, copy = shard_copy(k)
                    if self.half:
                        pl.when(carrying(peer))(lambda: act(copy))
                    else:
                        act(copy)

                each(1, self.shards, one)

            shard_each(lambda copy: copy.start())
            yield

            def add_shard():
                each(1, self.shards, lambda k: shard_copy(k)[1].wait_recv())
                target = mine if last == "spread" else out
                for part in range(target.shape[0]):
                    total = summed[slot(shard), part].astype(f32)
                    for k in range(self.shards - 1):
                        total = total + buf["shard_got"][k, part].astype(f32)
                    target[part] = total.astype(bf16)

            guard(0, add_shard)
            sent.append(lambda: shard_each(lambda copy: copy.wait_send()))
        if last == "spread":
            if "shard" not in self.stages:
                mine[...] = now[...]
            self.plane.bind(
                lambda t, c, k: out.at[c, t] if self.half else out.at[c, k, t],
                lambda t: lax.rem(t, 2),
                guard,
                other,
                [buf["spread%d" % index] for index in range(4)],
            )
            self.plane.start()
            yield
            self.plane.forward()
            yield
            self.plane.finish()
        for wait in sent:
            wait()


class Compute:
    def __init__(self, body, inputs, out_shapes, scratch=()):
        self.body, self.inputs, self.out_shapes = body, list(inputs), list(out_shapes)
        self.scratch = list(scratch)


def greet_all(sizes, wide):
    barrier = pltpu.get_barrier_semaphore()
    groups = [ALL] if wide else [REP, ("shard",)]
    total = 0
    for axes in groups:
        count, me = axes_size(sizes, axes), lax.axis_index(axes)
        total += count - 1

        def greet(k):
            peer = peer_coords(lax.rem(me + k, count), axes, sizes)
            pl.semaphore_signal(barrier, inc=1, device_id=peer, device_id_type=MESH)

        each(1, count, greet)
    pl.semaphore_wait(barrier, total)


DONE = object()


def run(collective_id, name, sizes, items, compute=None):
    wide = any(getattr(item, "axes", ()) == ALL for item in items)
    compute = compute or Compute(None, [], [])
    inputs, in_specs, out_shapes, out_specs, scratch, aliases = [], [], [], [], [], {}
    spans = []
    for item in items:
        if item.aliased:
            aliases[len(inputs)] = len(out_shapes)
        spans.append((len(inputs), len(out_shapes), len(scratch)))
        inputs += item.inputs
        in_specs += item.in_specs
        out_shapes += item.out_shapes
        out_specs += item.out_specs
        scratch += item.scratch
    own = (len(inputs), len(out_shapes), len(scratch))
    inputs += compute.inputs
    in_specs += [VMEM_SPEC] * len(compute.inputs)
    out_shapes += compute.out_shapes
    out_specs += [VMEM_SPEC] * len(compute.out_shapes)
    scratch += compute.scratch
    n_in, n_out = len(inputs), len(out_shapes)

    def kernel(*refs):
        ins, outs, tmp = refs[:n_in], refs[n_in : n_in + n_out], refs[n_in + n_out :]

        def parts(index):
            item, (a, b, c) = items[index], spans[index]
            item_ins = ins[a : a + len(item.inputs)]
            if getattr(item, "source", None) is not None:
                item_ins = [outs[own[1] + item.source]]
            return (
                item_ins,
                outs[b : b + len(item.out_shapes)],
                tmp[c : c + len(item.scratch)],
            )

        greet_all(sizes, wide)
        going = {}
        for index, item in enumerate(items):
            if not item.late:
                going[index] = item.steps(*parts(index))
                next(going[index])
        for index, item in enumerate(items):
            if not item.late:
                for _ in range(item.pre):
                    next(going[index])
        if compute.body is not None:
            compute.body(ins[own[0] :], outs[own[1] :], tmp[own[2] :])
        for index, item in enumerate(items):
            if item.late:
                going[index] = item.steps(*parts(index))
                next(going[index])
        for final in (False, True):
            left = [index for index, item in enumerate(items) if item.final == final]
            while left:
                left = [index for index in left if next(going[index], DONE) is not DONE]

    return pl.pallas_call(
        kernel,
        out_shape=out_shapes,
        in_specs=in_specs,
        out_specs=out_specs,
        scratch_shapes=scratch,
        input_output_aliases=aliases,
        compiler_params=pltpu.CompilerParams(collective_id=collective_id, has_side_effects=True),
        name=name,
    )(*inputs)


def mask_rows(code_row):
    index = lax.broadcasted_iota(jnp.int32, (16, code_row.shape[1]), 0)
    return jnp.where(index == code_row, 0.0, NEGATIVE_HUGE).astype(bf16)


def segment_rows(segment_row):
    index = lax.broadcasted_iota(jnp.int32, (16, segment_row.shape[1]), 0)
    return jnp.where(index == segment_row, 1.0, 0.0).astype(bf16)


def as_column(row):
    return jnp.transpose(jnp.broadcast_to(row, (128, row.shape[1])))[:, :1]


def diagonal_bias(info):
    code, place = as_column(info[0:1]), as_column(info[2:3])
    allowed = (place == info[2:3]) | ((code == info[1:2]) & (place <= info[2:3]))
    return jnp.where(allowed, 0.0, NEGATIVE_HUGE)


def forward_body(ins, outs, tmp):
    qkv_ref, info_ref = ins
    out_ref, keep_ref, lse_ref = outs
    bias, acc, stat = tmp
    blocks, slots = qkv_ref.shape[0], qkv_ref.shape[1] // 3
    source = key_slots(slots)
    key = [key_unit(slots, source[m]) for m in range(slots)]
    value = [value_unit(slots, source[m]) for m in range(slots)]

    @pl.loop(0, blocks)
    def _(i):
        bias[...] = diagonal_bias(info_ref[i])
        seg = segment_rows(info_ref[i, 1:2])
        qa = [jnp.concatenate([qkv_ref[i, m], seg], axis=0) for m in range(slots)]
        for m in range(slots):
            s = dot(jnp.transpose(qkv_ref[i, key[m]]), qkv_ref[i, m]) + bias[...]
            top = jnp.max(s, axis=0, keepdims=True)
            p = jnp.exp(s - top)
            stat[2 * m : 2 * m + 1] = top
            stat[2 * m + 1 : 2 * m + 2] = jnp.sum(p, axis=0, keepdims=True)
            acc[m] = dot(qkv_ref[i, value[m]], p.astype(bf16))

        @pl.loop(0, i)
        def _(j):
            mask = mask_rows(info_ref[j, 0:1])
            for m in range(slots):
                ka = jnp.transpose(jnp.concatenate([qkv_ref[j, key[m]], mask], axis=0))
                s = dot(ka, qa[m])
                old = stat[2 * m : 2 * m + 1]
                top = jnp.maximum(old, jnp.max(s, axis=0, keepdims=True))
                p = jnp.exp(s - top)
                factor = jnp.exp(old - top)
                stat[2 * m : 2 * m + 1] = top
                stat[2 * m + 1 : 2 * m + 2] = stat[2 * m + 1 : 2 * m + 2] * factor + jnp.sum(
                    p, axis=0, keepdims=True
                )
                acc[m] = acc[m] * factor + dot(qkv_ref[j, value[m]], p.astype(bf16))

        for m in range(slots):
            total = stat[2 * m + 1 : 2 * m + 2]
            result = acc[m] / total
            out_ref[i, m] = result.astype(bf16)
            keep_ref[i, m] = result
            lse_ref[i, m : m + 1] = stat[2 * m : 2 * m + 1] + jnp.log(total)


def backward_body(ins, outs, tmp):
    qkv_ref, do_ref, keep_ref, lse_ref, info_ref = ins
    (out_ref,) = outs
    bias, dq, qn, don, delta = tmp
    blocks, slots = qkv_ref.shape[0], qkv_ref.shape[1] // 3
    source = key_slots(slots)
    key = [key_unit(slots, source[m]) for m in range(slots)]
    value = [value_unit(slots, source[m]) for m in range(slots)]

    @pl.loop(0, blocks)
    def _(i):
        for m in range(slots):
            qn[i, m] = jnp.transpose(qkv_ref[i, m])
            don[i, m] = jnp.transpose(do_ref[i, m])
            delta[i, m : m + 1] = jnp.sum(
                do_ref[i, m].astype(f32) * keep_ref[i, m], axis=0, keepdims=True
            )
            dq[i, m] = jnp.zeros_like(dq[i, m])

    @pl.loop(0, blocks)
    def _(j):
        bias[...] = diagonal_bias(info_ref[j])
        mask = mask_rows(info_ref[j, 0:1])
        kn = [jnp.transpose(qkv_ref[j, key[m]]) for m in range(slots)]
        ka = [
            jnp.transpose(jnp.concatenate([qkv_ref[j, key[m]], mask], axis=0)) for m in range(slots)
        ]
        vn = [jnp.transpose(qkv_ref[j, value[m]]) for m in range(slots)]

        def tile(i, m, s):
            p = jnp.exp(s - lse_ref[i, m : m + 1])
            dp = dot(vn[m], do_ref[i, m])
            ds = (p * (dp - delta[i, m : m + 1])).astype(bf16)
            dq[i, m] += dot(qkv_ref[j, key[m]], ds)
            return dot(ds, qn[i, m]), dot(p.astype(bf16), don[i, m])

        start = []
        for m in range(slots):
            start += list(tile(j, m, dot(kn[m], qkv_ref[j, m]) + bias[...]))

        def later(i, carry):
            seg = segment_rows(info_ref[i, 1:2])
            new = []
            for m in range(slots):
                qa = jnp.concatenate([qkv_ref[i, m], seg], axis=0)
                a, b = tile(i, m, dot(ka[m], qa))
                new += [carry[2 * m] + a, carry[2 * m + 1] + b]
            return tuple(new)

        done = lax.fori_loop(j + 1, blocks, later, tuple(start))
        done = [jnp.transpose(value) for value in done]
        if slots == 2:
            shared = (1 - source[1]).astype(f32)
            done[0] = done[0] + done[2] * shared
            done[1] = done[1] + done[3] * shared
        for m in range(slots):
            out_ref[j, key_unit(slots, m)] = done[2 * m].astype(bf16)
            out_ref[j, value_unit(slots, m)] = done[2 * m + 1].astype(bf16)

    @pl.loop(0, blocks)
    def _(i):
        for m in range(slots):
            out_ref[i, m] = (dq[i, m] * HEAD_DIM ** (-0.5)).astype(bf16)


def ffn_kernel(x_ref, gf_ref, gu_ref, down_ref, part_ref, gu_grad_ref, down_grad_ref, ffn, dx):
    k = pl.program_id(0)
    half = gu_ref.shape[2] // 2
    x, gf = x_ref[...], gf_ref[...]
    filled = x.shape[1] // gu_ref.shape[0]
    weight = jnp.concatenate([gu_ref[z, :filled] for z in range(gu_ref.shape[0])], axis=0)
    both = dot(x, weight)
    gate, up = both[:, :half], both[:, half:]
    sig = 1.0 / (1.0 + jnp.exp(-gate))
    act = gate * sig
    hidden = (act * up).astype(bf16)
    grad_hidden = dot(gf, down_ref[...], 1, 1)
    grad_gate = (grad_hidden * up * (sig * (1.0 + gate * (1.0 - sig)))).astype(bf16)
    grad_up = (grad_hidden * act).astype(bf16)
    grads = jnp.concatenate([grad_gate, grad_up], axis=1)
    ffn_now = dot(hidden, down_ref[...])
    dx_now = dot(grads, weight, 1, 1)

    @pl.when(k == 0)
    def _():
        ffn[...] = ffn_now
        dx[...] = dx_now

    @pl.when(k > 0)
    def _():
        ffn[...] += ffn_now
        dx[...] += dx_now

    gu_grad = dot(x, grads, 0, 0)
    shards, padded = gu_grad_ref.shape[:2]
    for z in range(shards):
        gu_grad_ref[z, :filled] = gu_grad[z * filled : (z + 1) * filled].astype(bf16)
        if padded > filled:
            gu_grad_ref[z, filled:] = jnp.zeros((padded - filled, gu_grad.shape[1]), bf16)
    down_grad_ref[...] = dot(hidden, gf, 0, 0).astype(bf16)

    @pl.when(k == pl.num_programs(0) - 1)
    def _():
        rows = part_ref.shape[2]
        for c in range(2):
            part_ref[c, 0] = dx[c * rows : (c + 1) * rows].astype(bf16)
            part_ref[c, 1] = ffn[c * rows : (c + 1) * rows].astype(bf16)


def feed_forward(x, gf, gate_up, down):
    tokens, width = x.shape
    hidden, columns = FF_CHUNK, 2 * FF_CHUNK
    shards, padded = gate_up.shape[:2]
    chunks = gate_up.shape[2] // columns
    return pl.pallas_call(
        ffn_kernel,
        grid=(chunks,),
        in_specs=[
            pl.BlockSpec((tokens, width), lambda k: (0, 0)),
            pl.BlockSpec((tokens, width), lambda k: (0, 0)),
            pl.BlockSpec((shards, padded, columns), lambda k: (0, 0, k)),
            pl.BlockSpec((hidden, width), lambda k: (k, 0)),
        ],
        out_specs=[
            pl.BlockSpec((2, 2, tokens // 2, width), lambda k: (0, 0, 0, 0)),
            pl.BlockSpec((shards, padded, columns), lambda k: (0, 0, k)),
            pl.BlockSpec((hidden, width), lambda k: (k, 0)),
        ],
        out_shape=[
            jax.ShapeDtypeStruct((2, 2, tokens // 2, width), bf16),
            jax.ShapeDtypeStruct((shards, padded, chunks * columns), bf16),
            jax.ShapeDtypeStruct(down.shape, bf16),
        ],
        scratch_shapes=[pltpu.VMEM((tokens, width), f32), pltpu.VMEM((tokens, width), f32)],
        name="feed_forward",
    )(x, gf, gate_up, down)


def rms_scale(rows, gain):
    return rows * lax.rsqrt(jnp.mean(rows * rows, axis=-1, keepdims=True) + EPSILON) * gain


def norm_back(rows, gain, grad):
    r = lax.rsqrt(jnp.mean(rows * rows, axis=-1, keepdims=True) + EPSILON)
    scaled = gain * grad
    back = r * scaled - rows * (r * r * r) * jnp.mean(scaled * rows, axis=-1, keepdims=True)
    return back, jnp.sum(grad * rows * r, axis=0)


def line_layout(lengths_row, positions):
    seq_ends = jnp.cumsum(lengths_row, dtype=jnp.int32)
    reached = seq_ends[None, :] <= positions[:, None]
    segment = jnp.sum(reached.astype(jnp.int32), axis=1)
    starts = jnp.max(jnp.where(reached, seq_ends[None, :], 0), axis=1)
    return segment, positions - starts, positions < seq_ends[-1]


def project_body(ins, outs, tmp):
    hidden_ref, weight_ref, gain_ref, cos_ref, sin_ref = ins
    sent_ref, normed_ref, full_ref = outs
    reps, units, _, rows = sent_ref.shape
    slots, filled = units // 3, full_ref.shape[0] // weight_ref.shape[0]
    for z in range(weight_ref.shape[0]):
        full_ref[z * filled : (z + 1) * filled] = weight_ref[z, :filled]
    hidden = hidden_ref[...].astype(f32)
    normed = rms_scale(hidden, gain_ref[...]).astype(bf16)
    normed_ref[...] = normed
    cosines, sines = cos_ref[...], sin_ref[...]
    half, columns = HEAD_DIM // 2, full_ref.shape[1]

    def put(kind, head, value):
        slot = head % slots
        unit = (slot, key_unit(slots, slot), value_unit(slots, slot))[kind]
        sent_ref[head // slots, unit] = value

    for start in range(0, columns, 256):
        stop = min(start + 256, columns)
        block = jnp.transpose(dot(normed, full_ref[:, start:stop]))
        for head in range(start // HEAD_DIM, stop // HEAD_DIM):
            at = head * HEAD_DIM - start
            a, b = block[at : at + half], block[at + half : at + HEAD_DIM]
            if head < QUERY_HEADS:
                scale = HEAD_DIM ** (-0.5)
                put(
                    0,
                    head,
                    (
                        jnp.concatenate(
                            [a * cosines - b * sines, b * cosines + a * sines], axis=0
                        )
                        * scale
                    ).astype(bf16),
                )
            elif head < QUERY_HEADS + KEY_VALUE_HEADS:
                value = jnp.concatenate(
                    [a * cosines - b * sines, b * cosines + a * sines], axis=0
                ).astype(bf16)
                for m in range(GROUP):
                    put(1, (head - QUERY_HEADS) * GROUP + m, value)
            else:
                value = block[at : at + HEAD_DIM].astype(bf16)
                for m in range(GROUP):
                    put(2, (head - QUERY_HEADS - KEY_VALUE_HEADS) * GROUP + m, value)
    for head in range(QUERY_HEADS, reps * slots):
        for kind in range(3):
            put(kind, head, jnp.zeros((HEAD_DIM, rows), bf16))


def project_back_body(ins, outs, tmp):
    (grads_ref, cos_ref, sin_ref, weight_ref, hidden_ref, normed_ref, gain_ref, base_ref) = ins[:8]
    vectors_ref = ins[8]
    sent_ref, weight_grad_ref, vectors_grad_ref = outs
    (dt,) = tmp
    slots, half = grads_ref.shape[1] // 3, HEAD_DIM // 2
    cosines, sines = cos_ref[...], sin_ref[...]

    def get(kind, head):
        slot = head % slots
        unit = (slot, key_unit(slots, slot), value_unit(slots, slot))[kind]
        return grads_ref[head // slots, unit].astype(f32)

    def back(value):
        a, b = value[:half], value[half:]
        return jnp.concatenate([a * cosines + b * sines, b * cosines - a * sines], axis=0)

    for head in range(QUERY_HEADS):
        dt[head * HEAD_DIM : (head + 1) * HEAD_DIM] = back(get(0, head)).astype(bf16)
    for group in range(KEY_VALUE_HEADS):
        for kind in (1, 2):
            value = get(kind, group * GROUP)
            for head in range(group * GROUP + 1, (group + 1) * GROUP):
                if slots != 2 or head % 2 == 0:
                    value = value + get(kind, head)
            if kind == 1:
                value = back(value)
            at = (QUERY_HEADS + (kind - 1) * KEY_VALUE_HEADS + group) * HEAD_DIM
            dt[at : at + HEAD_DIM] = value.astype(bf16)
    grad = dot(dt[...], weight_ref[...], 0, 1)
    norm_grad, gain_grad = norm_back(hidden_ref[...].astype(f32), gain_ref[...], grad)
    index = lax.broadcasted_iota(jnp.int32, vectors_ref.shape, 0)
    vectors = jnp.where(index == 0, gain_grad[None], vectors_ref[...])
    piece = vectors_grad_ref.shape[2]
    for z in range(vectors_grad_ref.shape[0]):
        vectors_grad_ref[z] = vectors[:, z * piece : (z + 1) * piece]
    total = (base_ref[...] + norm_grad).astype(bf16)
    devices, per_pair = sent_ref.shape[:2]
    sent_ref[...] = total.reshape(sent_ref.shape)
    shards, chips, cores, parts, unit, columns = weight_grad_ref.shape
    filled = normed_ref.shape[1] // shards
    places = [(c, k, p) for c in range(chips) for k in range(cores) for p in range(parts)]
    for start in range(0, columns, 256):
        stop = min(start + 256, columns)
        block = dot(normed_ref[...], dt[start:stop], 0, 1)
        for z in range(shards):
            for r, place in enumerate(places):
                size = max(0, min(unit, filled - r * unit))
                at = z * filled + r * unit
                here = weight_grad_ref.at[z, *place]
                if size:
                    here[:size, start:stop] = block[at : at + size].astype(bf16)
                if size < unit:
                    here[size:, start:stop] = jnp.zeros((unit - size, stop - start), bf16)


def finalize_kernel(gate_up_ref, down_ref, out_ref, qkv_ref, gate, up, down, out, query, key, value):
    cores, rows, columns = gate_up_ref.shape[1:]
    half = columns // 2
    for core in range(cores):
        for start in range(0, columns, 2 * FF_CHUNK):
            at = core * half + start // 2
            middle = start + FF_CHUNK
            gate[:, at : at + FF_CHUNK] = gate_up_ref[0, core, :, start:middle].astype(f32)
            up[:, at : at + FF_CHUNK] = gate_up_ref[0, core, :, middle : middle + FF_CHUNK].astype(f32)
    down[...] = down_ref[0].astype(f32)
    out[...] = out_ref[0].astype(f32)
    ends = (query.shape[1], query.shape[1] + key.shape[1])
    qkv = qkv_ref[0].astype(f32)
    query[...] = qkv[:, : ends[0]]
    key[...] = qkv[:, ends[0] : ends[1]]
    value[...] = qkv[:, ends[1] :]


def finalize(gate_up, down, out, qkv, shard_rows, key_width):
    chips, rows = gate_up.shape[0], gate_up.shape[2]
    width, hidden = out.shape[2], gate_up.shape[3]
    columns = (hidden, hidden, None, width, width, key_width, key_width)

    def out_spec(array_columns):
        shape = tuple(down.shape[1:]) if array_columns is None else (rows, array_columns)
        return pl.BlockSpec(shape, lambda c: (c, 0))

    def out_type(array_columns):
        shape = (chips * down.shape[1], down.shape[2])
        shape = shape if array_columns is None else (shard_rows, array_columns)
        return jax.ShapeDtypeStruct(shape, f32)

    return pl.pallas_call(
        finalize_kernel,
        grid=(chips,),
        in_specs=[pl.BlockSpec((1, 2, rows, hidden), lambda c: (c, 0, 0, 0))]
        + [pl.BlockSpec((1,) + tuple(a.shape[1:]), lambda c: (c, 0, 0)) for a in (down, out, qkv)],
        out_specs=[out_spec(c) for c in columns],
        out_shape=[out_type(c) for c in columns],
        name="finalize",
    )(gate_up, down, out, qkv)


def rounded_up(value, unit):
    return -(-value // unit) * unit


def local(
    sizes,
    hidden_in,
    cotangent,
    destination,
    seq_lengths,
    gate_mask,
    query_weight,
    key_matrix,
    value_matrix,
    out_weight,
    gate_weight,
    up_weight,
    down_weight,
    attn_gain,
    ffn_gain,
    router_weight,
):
    rows, width = hidden_in.shape
    chips, shards = sizes["chip"], sizes["shard"]
    reps = 2 * chips
    devices = reps * shards
    per_pair = rows // devices
    slots = -(-QUERY_HEADS // reps)
    padded_heads = slots * reps
    chip, core, shard = lax.axis_index("chip"), lax.axis_index("core"), lax.axis_index("shard")
    rep = lax.axis_index(REP)
    shard_rows = query_weight.shape[0]
    rep_unit = rounded_up(-(-shard_rows // reps), 8)
    padded = rep_unit * reps
    chip_unit = padded // chips
    ff_half = gate_weight.shape[1] // 2
    chunks = ff_half // FF_CHUNK

    def padded_rows(array):
        return jnp.pad(array, ((0, padded - shard_rows), (0, 0)))

    qkv_shard = padded_rows(jnp.concatenate([query_weight, key_matrix, value_matrix], axis=1))
    qkv_shard = qkv_shard.reshape(reps, rep_unit, -1)
    out_shard = padded_rows(out_weight).reshape(reps, rep_unit, width)
    halves = [
        lax.dynamic_slice_in_dim(w, core * ff_half, ff_half, 1).reshape(
            shard_rows, chunks, 1, FF_CHUNK
        )
        for w in (gate_weight, up_weight)
    ]
    gate_up_shard = jnp.concatenate(halves, axis=2).reshape(shard_rows, 2 * ff_half)
    gate_up_shard = padded_rows(gate_up_shard).reshape(chips, chip_unit, 2 * ff_half)
    down_unit = down_weight.shape[0] // chips
    down_shard = down_weight.reshape(chips, down_unit, width)
    vectors = jnp.stack([attn_gain, ffn_gain, router_weight]).astype(f32)
    vectors = jnp.pad(vectors, ((0, 5), (0, 0)))

    def full_rows(full):
        full = full.reshape(shards, padded, full.shape[-1])
        return full[:, :shard_rows].reshape(width, full.shape[-1])

    row_index = jnp.arange(rows, dtype=jnp.int32)
    target = destination // rows
    earlier = (target[None, :] == target[:, None]) & (row_index[None, :] < row_index[:, None])
    slot_of_row = target * per_pair + jnp.sum(earlier.astype(jnp.int32), axis=1)
    to_slot = slot_of_row[None, :] == row_index[:, None]
    to_slot_b = to_slot.astype(bf16)
    place_sent = jnp.sum(jnp.where(to_slot, (destination % rows)[None, :], 0), axis=1)
    place_sent = place_sent.reshape(devices, 1, per_pair)
    place_sent = jnp.pad(place_sent, ((0, 0), (0, 0), (0, 128 - per_pair)))

    def by_slot(tokens):
        tokens = jnp.dot(to_slot_b, tokens, preferred_element_type=f32).astype(bf16)
        return tokens.reshape(devices, per_pair, width)

    got_hidden, got_place, vectors_got, qkv_full = run(
        1,
        "first",
        sizes,
        [
            AllToAll(sizes, by_slot(hidden_in), ALL, late=True),
            AllToAll(sizes, place_sent, ALL, late=True),
            AllToAll(sizes, vectors, ("shard",), spread=True),
            Gather(sizes, qkv_shard, REP, "both"),
        ],
    )
    hidden = got_hidden.reshape(rows, width)
    place = got_place[:, 0, :per_pair].reshape(rows)
    qkv_full = qkv_full.reshape(shards, padded, -1)
    vectors_full = jnp.transpose(vectors_got[:, :3], (1, 0, 2)).reshape(3, width)
    gain_one, gain_two, full_router = vectors_full[0], vectors_full[1], vectors_full[2]

    positions = rep * rows + place
    segment, within, is_valid = line_layout(seq_lengths[0], positions)
    here = place[:, None] == row_index[None, :]
    gate_here = jnp.sum(jnp.where(here, gate_mask[None, :], 0), axis=1)
    active = is_valid & (gate_here == 1)
    key_code = jnp.where(active, segment, -1)
    active_f = active.astype(f32)
    info = jnp.pad(jnp.stack([key_code, segment, place]), ((0, 5), (0, 0)))
    steps = jnp.arange(HEAD_DIM // 2).astype(f32)
    frequency = jnp.power(ROPE_BASE, -2.0 * steps / HEAD_DIM)
    angles = frequency[:, None] * within.astype(f32)[None, :]
    cosines, sines = jnp.cos(angles), jnp.sin(angles)

    heads_shape = (reps, 3 * slots, HEAD_DIM, rows)
    heads_type = jax.ShapeDtypeStruct(heads_shape, bf16)
    gate_up_z, down_z, out_z, info_got, qkv_got, _, first_normalized, qkv_weights = run(
        2,
        "project",
        sizes,
        [
            Gather(sizes, gate_up_shard, ("chip",), "z"),
            Gather(sizes, down_shard, ("chip",), "z", half=True),
            Gather(sizes, out_shard, REP, "z"),
            AllToAll(sizes, info, REP, spread=True),
            Heads(sizes, heads_type, True, 0),
        ],
        Compute(
            project_body,
            [hidden, qkv_full, gain_one[None], cosines, sines],
            [
                heads_type,
                jax.ShapeDtypeStruct((rows, width), bf16),
                jax.ShapeDtypeStruct((width, qkv_full.shape[2]), bf16),
            ],
        ),
    )
    slot_type = jax.ShapeDtypeStruct((reps, slots, HEAD_DIM, rows), bf16)
    gate_up_full, down_full, out_full, got_grad, att_home, _, att_keep, lse = run(
        3,
        "attend",
        sizes,
        [
            Gather(sizes, gate_up_z, ("chip",), "plane"),
            Gather(sizes, down_z, ("chip",), "plane", half=True),
            Gather(sizes, out_z, REP, "plane"),
            AllToAll(sizes, by_slot(cotangent), ALL),
            AllToAll(sizes, slot_type, REP, late=True, source=0),
        ],
        Compute(
            forward_body,
            [qkv_got, info_got],
            [
                slot_type,
                jax.ShapeDtypeStruct(slot_type.shape, f32),
                jax.ShapeDtypeStruct((reps, 8, rows), f32),
            ],
            [
                pltpu.VMEM((rows, rows), f32),
                pltpu.VMEM((slots, HEAD_DIM, rows), f32),
                pltpu.VMEM((8, rows), f32),
            ],
        ),
    )
    attn_out_t = att_home.reshape(padded_heads * HEAD_DIM, rows)[:width]
    full_out = full_rows(out_full)
    gate_up = gate_up_full.reshape(shards, padded, 2 * ff_half)
    down = down_full.reshape(ff_half, width)

    hidden_f = hidden.astype(f32)
    router_logit = jnp.sum(hidden_f * full_router, axis=1)
    gate_value = jax.nn.sigmoid(router_logit)
    branch_scale = active_f * gate_value
    attn_branch = jnp.einsum("dt,de->te", attn_out_t, full_out, preferred_element_type=f32)
    middle = hidden_f + attn_branch
    normed_two = rms_scale(middle, gain_two).astype(bf16)
    grad_out = got_grad.reshape(rows, width).astype(f32)
    grad_branch = branch_scale[:, None] * grad_out
    grad_ffn = grad_branch.astype(bf16)
    x_pair, gf_pair = run(
        4,
        "pair",
        sizes,
        [
            AllToAll(sizes, normed_two, ("core",), spread=True),
            AllToAll(sizes, grad_ffn, ("core",), spread=True),
        ],
    )
    parts, gate_up_grad, down_grad = feed_forward(
        x_pair.reshape(2 * rows, width),
        gf_pair.reshape(2 * rows, width),
        gate_up,
        down,
    )
    (parts_got,) = run(5, "parts", sizes, [AllToAll(sizes, parts, ("core",))])
    grad_normed_two = parts_got[0, 0].astype(f32) + parts_got[1, 0].astype(f32)
    ffn_branch = parts_got[0, 1].astype(f32) + parts_got[1, 1].astype(f32)
    branch_sum = attn_branch + ffn_branch
    result = (hidden_f + branch_scale[:, None] * branch_sum).astype(bf16)
    grad_logit = active_f * jnp.sum(grad_out * branch_sum, axis=1) * gate_value * (1.0 - gate_value)
    grad_middle, grad_gain_ffn = norm_back(middle, gain_two, grad_normed_two)
    grad_attn = (grad_branch + grad_middle).astype(bf16)
    grad_attention_t = jnp.einsum("te,de->dt", grad_attn, full_out, preferred_element_type=f32)
    grad_attention_t = jnp.pad(
        grad_attention_t.astype(bf16), ((0, padded_heads * HEAD_DIM - width), (0, 0))
    ).reshape(slot_type.shape)
    (grad_got,) = run(6, "grads", sizes, [AllToAll(sizes, grad_attention_t, REP)])

    out_grad = jnp.einsum("dt,te->de", attn_out_t, grad_attn, preferred_element_type=f32)
    parts = 2 if chips == 4 else 1
    out_grad = jnp.pad(
        out_grad.astype(bf16).reshape(shards, shard_rows, width),
        ((0, 0), (0, padded - shard_rows), (0, 0)),
    ).reshape(shards, chips, 2, parts, rep_unit // parts, width)
    gate_up_grad = gate_up_grad.reshape(shards, chips, parts, chip_unit // parts, 2 * ff_half)
    down_grad = down_grad.reshape(shards // 2, chips, parts, down_unit // parts, width)
    gate_up_sum, down_sum, out_sum, home_out, heads_home, _ = run(
        7,
        "attend_back",
        sizes,
        [
            Reduce(sizes, gate_up_grad, ("plane", "shard")),
            Reduce(sizes, down_grad, ("plane",)),
            Reduce(sizes, out_grad, ("pair", "plane")),
            AllToAll(sizes, result.reshape(devices, per_pair, width), ALL),
            Heads(sizes, heads_type, False, 0),
        ],
        Compute(
            backward_body,
            [qkv_got, grad_got, att_keep, lse, info_got],
            [heads_type],
            [
                pltpu.VMEM((rows, rows), f32),
                pltpu.VMEM((reps, slots, HEAD_DIM, rows), f32),
                pltpu.VMEM((reps, slots, rows, HEAD_DIM), bf16),
                pltpu.VMEM((reps, slots, rows, HEAD_DIM), bf16),
                pltpu.VMEM((reps, 8, rows), f32),
            ],
        ),
    )

    base = grad_out + grad_middle + grad_logit[:, None] * full_router
    router_grad = jnp.sum(grad_logit[:, None] * hidden_f, axis=0)
    vector_grads = jnp.pad(jnp.stack([grad_gain_ffn, router_grad]), ((1, 5), (0, 0)))
    tokens_type = jax.ShapeDtypeStruct((devices, per_pair, width), bf16)
    qkv_columns = qkv_weights.shape[1]
    qkv_grad_type = jax.ShapeDtypeStruct(
        (shards, chips, 2, parts, rep_unit // parts, qkv_columns), bf16
    )
    vectors_type = jax.ShapeDtypeStruct((shards, 8, shard_rows), f32)
    qkv_home, gate_up_home, down_home, out_home, home_grad, vectors_home = run(
        8,
        "project_back",
        sizes,
        [
            Reduce(sizes, qkv_grad_type, ("pair", "plane", "shard", "spread"), late=True, source=1),
            Reduce(sizes, gate_up_sum, ("spread",)),
            Reduce(sizes, down_sum, ("shard", "spread"), half=True),
            Reduce(sizes, out_sum, ("shard", "spread")),
            AllToAll(sizes, tokens_type, ALL, late=True, source=0),
            AllToAll(sizes, vectors_type, ALL, by_shard=True, late=True, source=2),
        ],
        Compute(
            project_back_body,
            [
                heads_home,
                cosines,
                sines,
                qkv_weights,
                hidden,
                first_normalized,
                gain_one[None],
                base,
                vector_grads,
            ],
            [tokens_type, qkv_grad_type, vectors_type],
            [pltpu.VMEM((qkv_columns, rows), bf16)],
        ),
    )[:6]
    weight_grads = finalize(
        gate_up_home.reshape(chips, 2, chip_unit, 2 * ff_half),
        down_home.reshape(chips, down_unit, width),
        out_home.reshape(chips, chip_unit, width),
        qkv_home.reshape(chips, chip_unit, qkv_columns),
        shard_rows,
        key_matrix.shape[1],
    )
    gate_total, up_total, down_total, out_total, query_total, key_total, value_total = weight_grads
    vector_total = jnp.sum(vectors_home, axis=0)

    def home_rows(home):
        home = home.reshape(rows, width)
        return jnp.einsum("sr,sw->rw", to_slot_b, home, preferred_element_type=f32).astype(bf16)

    return (
        home_rows(home_out),
        home_rows(home_grad),
        query_total,
        key_total,
        value_total,
        out_total,
        gate_total,
        up_total,
        down_total,
        vector_total[0],
        vector_total[1],
        vector_total[2],
    )


def solution(mesh):
    reps, shards = mesh.shape["rep"], mesh.shape["shard"]
    sizes = {"chip": reps // 2, "core": 2, "shard": shards}
    split_mesh = Mesh(mesh.devices.reshape(reps // 2, 2, shards), ALL)
    tokens, tokens_1d = P(ALL, None), P(ALL)
    weight, vector = P("shard", None), P("shard")
    return jax.shard_map(
        functools.partial(local, sizes),
        mesh=split_mesh,
        in_specs=(tokens, tokens, tokens_1d, weight, tokens_1d) + (weight,) * 7 + (vector,) * 3,
        out_specs=(tokens, tokens) + (weight,) * 7 + (vector,) * 3,
        check_vma=False,
    )
```

```python
import functools
import types

import jax
import jax.numpy as jnp
from jax import lax
from jax.experimental import pallas as pl
from jax.experimental.pallas import tpu as pltpu
from jax.sharding import Mesh
from jax.sharding import PartitionSpec as P

QUERY_HEADS = 15
KEY_VALUE_HEADS = 5
HEAD_DIM = 64
GROUP = QUERY_HEADS // KEY_VALUE_HEADS
EPSILON = 1e-05
NEGATIVE_HUGE = -1e30
ROPE_BASE = 10000.0
FF_CHUNK = 256
bf16 = jnp.bfloat16
f32 = jnp.float32
MESH = pl.DeviceIdType.MESH
REP = ("chip", "core")
ALL = ("chip", "core", "shard")
VMEM_SPEC = pl.BlockSpec(memory_space=pltpu.VMEM)
HBM_SPEC = pl.BlockSpec(memory_space=pl.ANY)


def dot(a, b, ca=1, cb=0):
    return lax.dot_general(a, b, (((ca,), (cb,)), ((), ())), preferred_element_type=f32)


def axes_size(sizes, axes):
    total = 1
    for name in axes:
        total *= sizes[name]
    return total


def peer_coords(index, axes, sizes):
    coords = {}
    for name in reversed(axes):
        coords[name] = lax.rem(index, sizes[name])
        index = index // sizes[name]
    return coords


def partner(k, axes, sizes, back=False):
    if axes == ALL:
        reps = axes_size(sizes, REP)
        offsets = {"chip": lax.rem(k, reps) // 2, "core": lax.rem(k, 2), "shard": k // reps}
    elif axes == REP:
        offsets = {"chip": k // 2, "core": lax.rem(k, 2)}
    else:
        offsets = {axes[0]: k}
    coords, index = {}, 0
    for name in axes:
        me, count, offset = lax.axis_index(name), sizes[name], offsets[name]
        if name == "chip" and count == 4:
            x = lax.rem(lax.rem(me, 2) + lax.rem(offset, 2), 2)
            coords[name] = 2 * lax.rem(me // 2 + offset // 2, 2) + x
        else:
            coords[name] = lax.rem(me + (count - offset if back else offset), count)
        index = index * count + coords[name]
    return index, coords


def remote(src, dst, send_sem, recv_sem, coords):
    return pltpu.make_async_remote_copy(
        src_ref=src,
        dst_ref=dst,
        send_sem=send_sem,
        recv_sem=recv_sem,
        device_id=coords,
        device_id_type=MESH,
    )


def each(start, stop, body):
    def step(k, carry):
        body(k)
        return carry

    lax.fori_loop(start, stop, step, 0)


class Item:
    late = False
    final = False
    aliased = False
    pre = 0
    hooks = ()

    def at(self, *hooks):
        self.hooks = hooks
        return self

    def steps(self, ins, outs, scratch):
        yield


class AllToAll(Item):
    final = True

    def __init__(self, sizes, array, axes, spread=False, by_shard=False, late=False, source=None):
        self.sizes, self.axes, self.spread, self.late = sizes, axes, spread, late
        self.by_shard = by_shard
        self.count = axes_size(sizes, axes)
        self.source = source
        self.inputs = [] if source is not None else [array]
        piece = tuple(array.shape) if spread else tuple(array.shape[1:])
        self.in_specs = [VMEM_SPEC] * len(self.inputs)
        self.out_shapes = [jax.ShapeDtypeStruct((self.count,) + piece, array.dtype)]
        self.out_specs = [VMEM_SPEC]
        self.scratch = [
            pltpu.SemaphoreType.DMA((self.count,)),
            pltpu.SemaphoreType.DMA((self.count,)),
        ]

    def index(self, peer):
        return lax.rem(peer, self.sizes["shard"]) if self.by_shard else peer

    def copy(self, k, ins, outs, scratch):
        me = lax.axis_index(self.axes)
        peer, coords = partner(k, self.axes, self.sizes)
        return remote(
            ins[0] if self.spread else ins[0].at[self.index(peer)],
            outs[0].at[me],
            scratch[0].at[k],
            scratch[1].at[k],
            coords,
        )

    def steps(self, ins, outs, scratch):
        each(1, self.count, lambda k: self.copy(k, ins, outs, scratch).start())
        me = lax.axis_index(self.axes)
        outs[0][me] = ins[0][...] if self.spread else ins[0][self.index(me)]
        yield
        each(1, self.count, lambda k: self.copy(k, ins, outs, scratch).wait())


class Swap(AllToAll):
    def __init__(self, sizes, array):
        super().__init__(sizes, array, ("core",), spread=True, late=True)
        self.inputs, self.in_specs = [], []

    def steps(self, ins, outs, scratch):
        core = lax.axis_index("core")

        def copy():
            here = outs[0].at[core]
            return remote(here, here, scratch[0].at[1], scratch[1].at[1], {"core": 1 - core})

        copy().start()
        yield
        copy().wait()


class Stepwise(AllToAll):
    def __init__(self, sizes, array, source):
        super().__init__(sizes, array, REP, source=source)

    def copy_to(self, peer):
        me = lax.axis_index(REP)
        return remote(
            self.src.at[peer],
            self.dst.at[me],
            self.sems[0].at[peer],
            self.sems[1].at[me],
            peer_coords(peer, REP, self.sizes),
        )

    def send(self, peer):
        pl.when(peer != lax.axis_index(REP))(lambda: self.copy_to(peer).start())

    def steps(self, ins, outs, scratch):
        self.src, self.dst, self.sems = ins[0], outs[0], scratch
        yield
        me = lax.axis_index(REP)
        outs[0][me] = ins[0][me]

        def wait(k):
            peer = lax.rem(me + k, self.count)
            remote(
                self.src.at[me],
                self.dst.at[peer],
                self.sems[0].at[peer],
                self.sems[1].at[peer],
                peer_coords(peer, REP, self.sizes),
            ).wait_recv()
            self.copy_to(peer).wait_send()

        each(1, self.count, wait)


class Heads(Item):
    final = True
    late = True

    def __init__(self, sizes, array, to, source):
        self.sizes, self.to, self.source = sizes, to, source
        self.count = axes_size(sizes, REP)
        self.slots = array.shape[1] // 3
        self.main = array.shape[1] if self.slots != 2 else 4
        self.units = array.shape[1]
        self.inputs, self.in_specs = [], []
        self.out_shapes = [jax.ShapeDtypeStruct(array.shape, array.dtype)]
        self.out_specs = [VMEM_SPEC]
        dma = pltpu.SemaphoreType.DMA
        self.scratch = [dma((2, self.count)), dma((2, self.count))]

    def copy(self, k, ins, outs, scratch, extra, sending):
        me = lax.axis_index(REP)
        peer, coords = partner(k, REP, self.sizes, not sending)
        units = pl.ds(self.main, self.units - self.main) if extra else pl.ds(0, self.main)
        return peer, remote(
            ins[0].at[peer, units],
            outs[0].at[me if sending else peer, units],
            scratch[0].at[int(extra), k],
            scratch[1].at[int(extra), k],
            coords,
        )

    def every(self, ins, outs, scratch, sending, act):
        def main(k):
            act(self.copy(k, ins, outs, scratch, False, sending)[1])

        def extra(k):
            peer, copy = self.copy(k, ins, outs, scratch, True, sending)
            owner = peer if sending == self.to else lax.axis_index(REP)
            pl.when(apart(owner) == 1)(lambda: act(copy))

        each(1, self.count, main)
        if self.units > self.main:
            each(1, self.count, extra)

    def steps(self, ins, outs, scratch):
        self.every(ins, outs, scratch, True, lambda copy: copy.start())
        me = lax.axis_index(REP)
        outs[0][me] = ins[0][me]
        yield
        self.every(ins, outs, scratch, False, lambda copy: copy.wait_recv())
        self.every(ins, outs, scratch, True, lambda copy: copy.wait_send())


def apart(rep):
    last = KEY_VALUE_HEADS - 1
    return jnp.minimum((2 * rep + 1) // GROUP, last) - jnp.minimum((2 * rep) // GROUP, last)


def key_slots(slots):
    return [0, apart(lax.axis_index(REP))] if slots == 2 else list(range(slots))


def key_unit(slots, slot):
    return slots + 2 * slot


def value_unit(slots, slot):
    return slots + 2 * slot + 1


def flipped(chip, k):
    x, y = lax.rem(chip, 2), chip // 2
    x = 1 - x if k in (1, 3) else x
    y = 1 - y if k in (2, 3) else y
    return 2 * y + x


class Plane:
    def __init__(self, sizes, pair, lo, hi):
        self.pair, self.lo, self.hi, self.chips = pair, lo, hi, sizes["chip"]
        self.relay = self.chips == 4
        self.near = (1, 2) if self.relay else tuple(range(1, self.chips))
        self.scratch = [pltpu.SemaphoreType.DMA((self.chips, hi))] * (4 if pair else 2)

    def bind(self, region, path, guard, other, sems):
        self.region, self.path, self.guard, self.other, self.sems = region, path, guard, other, sems
        self.chip, self.core = lax.axis_index("chip"), lax.axis_index("core")

    def peer(self, k):
        return flipped(self.chip, k) if self.relay else lax.rem(self.chip + k, self.chips)

    def owner(self, k):
        if self.relay:
            return flipped(self.chip, k)
        return lax.rem(self.chip + self.chips - k, self.chips)

    def copy(self, t, k, owner, to):
        ref = self.region(t, owner, self.core)
        return remote(ref, ref, self.sems[0].at[k, t], self.sems[1].at[k, t], {"chip": to})

    def relayed(self, t, k):
        return self.copy(t, 3, self.owner(k), self.peer(3 - k))

    def pass_on(self, t, owner, core=None):
        ref = self.region(t, owner, self.core if core is None else core)
        return remote(
            ref, ref, self.sems[2].at[owner, t], self.sems[3].at[owner, t], {"core": 1 - self.core}
        )

    def parts(self, body, guard=None, span=None):
        lo, hi = span or (self.lo, self.hi)
        each(lo, hi, lambda t: (guard or self.guard)(t, lambda: body(t)))

    def start(self):
        def part(t):
            for k in self.near:
                self.copy(t, k, self.chip, self.peer(k)).start()
            if self.pair:
                self.pass_on(t, self.chip).start()

        self.parts(part)

    def arrived(self, t, k):
        self.copy(t, k, self.owner(k), self.chip).wait_recv()
        if self.pair:
            self.pass_on(t, self.owner(k)).start()

    def forward(self, span=None):
        def part(t):
            for k in self.near:
                self.arrived(t, k)
                if self.relay:
                    pl.when(self.path(t) == k - 1)(lambda: self.relayed(t, k).start())

        self.parts(part, span=span)

    def forwarded(self, span=None):
        if self.relay:
            self.parts(lambda t: self.arrived(t, 3), span=span)

    def finish(self):
        def sent(t):
            for k in self.near:
                self.copy(t, k, self.chip, self.peer(k)).wait_send()
                if self.relay:
                    pl.when(self.path(t) == k - 1)(lambda: self.relayed(t, k).wait_send())
            if self.pair:
                each(0, self.chips, lambda c: self.pass_on(t, c).wait_send())

        self.parts(sent)
        if self.pair:
            self.parts(
                lambda t: each(
                    0, self.chips, lambda c: self.pass_on(t, c, 1 - self.core).wait_recv()
                ),
                self.other,
            )


def always(t, body):
    body()


class Gather(Item):
    def __init__(self, sizes, array, split_axes, stages, half=False):
        self.sizes, self.split_axes, self.stages, self.half = sizes, split_axes, stages, half
        self.shards = sizes["shard"]
        self.slots = self.shards // 2 if half else self.shards
        self.pair = len(split_axes) == 2
        both = stages == "both"
        self.pre = 0 if stages == "plane" or half else 1
        self.inputs = [array]
        self.in_specs = [VMEM_SPEC if both else HBM_SPEC]
        if stages == "plane":
            shape, self.aliased = tuple(array.shape), True
        else:
            shape = (self.slots,) + tuple(array.shape)
        self.out_shapes = [jax.ShapeDtypeStruct(shape, array.dtype)]
        self.out_specs = [VMEM_SPEC if both else HBM_SPEC]
        dma = pltpu.SemaphoreType.DMA
        self.scratch = []
        if stages != "plane":
            self.scratch += [dma((self.shards,)), dma((self.shards,))]
        if stages == "z":
            self.scratch += [pltpu.VMEM(array.shape, array.dtype), dma((2,))]
        else:
            self.plane = Plane(sizes, self.pair, 1, self.shards)
            self.scratch += self.plane.scratch

    def guarded(self, z, body):
        if self.half:
            pl.when(z // self.slots == lax.axis_index("core"))(body)
        else:
            body()

    def slot(self, z):
        return lax.rem(z, self.slots) if self.half else z

    def z_copy(self, k, src, full, scratch, sending):
        me = lax.axis_index("shard")
        mine = lax.axis_index(self.split_axes)
        peer = lax.rem(me + k, self.shards) if sending else lax.rem(me + self.shards - k, self.shards)
        source = me if sending else peer
        dst = full.at[self.slot(source), mine]
        return remote(
            src.at[mine] if sending else dst,
            dst,
            scratch[0].at[k],
            scratch[1].at[k],
            {"shard": peer},
        )

    def z_start(self, src, full, scratch):
        self.guarded(
            lax.axis_index("shard"),
            lambda: each(1, self.shards, lambda k: self.z_copy(k, src, full, scratch, True).start()),
        )

    def z_finish(self, src, full, scratch):
        me = lax.axis_index("shard")

        def receive(k):
            peer = lax.rem(me + self.shards - k, self.shards)
            self.guarded(
                peer, lambda: self.z_copy(k, src, full, scratch, False).wait_recv()
            )

        each(1, self.shards, receive)

        def sent():
            each(1, self.shards, lambda k: self.z_copy(k, src, full, scratch, True).wait_send())

        self.guarded(me, sent)

    def steps(self, ins, outs, scratch):
        me = lax.axis_index("shard")
        src, full = ins[0], outs[0]
        if self.stages == "z":
            self.z_start(src, full, scratch)
            load = pltpu.make_async_copy(src, scratch[2], scratch[3].at[0])
            store = pltpu.make_async_copy(scratch[2], full.at[self.slot(me)], scratch[3].at[1])
            self.guarded(me, load.start)
            yield

            def both():
                load.wait()
                store.start()

            self.guarded(me, both)
            yield
            self.guarded(me, store.wait)
            self.z_finish(src, full, scratch)
            return

        def shard_of(t):
            return lax.rem(me + t, self.shards)

        def region(t, chip, core):
            return full.at[self.slot(shard_of(t)), 2 * chip + core if self.pair else chip]

        guard = (lambda t, body: self.guarded(shard_of(t), body)) if self.half else always
        if self.stages == "both":
            self.z_start(src, full, scratch)

            def keep():
                full[self.slot(me)] = src[...]

            self.guarded(me, keep)
        self.plane.bind(
            region, lambda t: lax.rem(shard_of(t), 2), guard, always, scratch[-len(self.plane.scratch) :]
        )
        if self.stages == "both":
            yield
            self.z_finish(src, full, scratch)
        self.plane.start()
        yield
        self.plane.forward()
        yield
        self.plane.forwarded()
        yield
        self.plane.finish()


class ChunkGather(Item):
    aliased = True
    final = True

    def __init__(self, sizes, array):
        self.shards, self.chunks = sizes["shard"], array.shape[2]
        self.each = self.shards - 1
        self.inputs, self.in_specs = [array], [HBM_SPEC]
        self.out_shapes = [jax.ShapeDtypeStruct(array.shape, array.dtype)]
        self.out_specs = [HBM_SPEC]
        self.plane = Plane(sizes, False, 0, self.chunks * self.each)
        self.scratch = self.plane.scratch

    def span(self, c):
        return (c * self.each, (c + 1) * self.each)

    def forward(self, c):
        self.plane.forward(self.span(c))

    def arrived(self, c):
        self.plane.forwarded(self.span(c))

    def steps(self, ins, outs, scratch):
        me = lax.axis_index("shard")

        def shard_of(t):
            return lax.rem(me + 1 + lax.rem(t, self.each), self.shards)

        self.plane.bind(
            lambda t, chip, core: outs[0].at[shard_of(t), chip, t // self.each],
            lambda t: lax.rem(shard_of(t), 2),
            always,
            always,
            scratch,
        )
        self.plane.start()
        yield
        self.plane.finish()


class Reduce(Item):
    def __init__(self, sizes, array, stages, half=False, late=False, source=None):
        self.stages, self.half, self.late, self.source = stages, half, late, source
        self.pre = int(stages[0] == "pair" and not late)
        self.chips, self.shards = sizes["chip"], sizes["shard"]
        self.slots = self.shards // 2
        lead = {"pair": 3, "plane": 2, "shard": 1, "spread": 0}[stages[0]]
        unit = tuple(array.shape[lead:])
        self.zs = array.shape[0]
        zs, chips, dtype = self.zs, self.chips, array.dtype
        self.inputs = [] if source is not None else [array]
        self.from_hbm = source is None and stages[0] == "plane"
        self.relay = chips == 4 and not late and "plane" in stages
        self.in_specs = [HBM_SPEC if self.from_hbm else VMEM_SPEC] * len(self.inputs)
        self.names, self.scratch = [], []

        def add(name, buffer):
            self.names.append(name)
            self.scratch.append(buffer)

        dma = pltpu.SemaphoreType.DMA
        if "pair" in stages:
            add("pair_got", pltpu.VMEM((zs, chips) + unit, dtype))
            add("pair_sum", pltpu.VMEM((zs, chips) + unit, dtype))
            add("pair_sems", dma((2,)))
        if self.relay:
            half_unit = (zs,) + unit[1:]
            add("near_got", pltpu.VMEM((2, 2) + half_unit, dtype))
            add("relay_sum", pltpu.VMEM((2,) + half_unit, dtype))
            add("relay_got", pltpu.VMEM((2,) + half_unit, dtype))
            add("near_sent", dma((2, 2)))
            add("near_arrived", dma((2, 2)))
            add("relay_sent", dma((2,)))
            add("relay_arrived", dma((2,)))
            if self.from_hbm:
                add("plane_own", pltpu.VMEM((zs,) + unit, dtype))
                add("far_own", pltpu.VMEM((2,) + half_unit, dtype))
                add("own_sems", dma((3,)))
            if stages[-1] != "plane":
                add("plane_sum", pltpu.VMEM((zs,) + unit, dtype))
        elif "plane" in stages:
            add("plane_got", pltpu.VMEM((chips - 1, zs) + unit, dtype))
            add("plane_sent", dma((chips,)))
            add("plane_arrived", dma((chips,)))
            if self.from_hbm:
                add("plane_own", pltpu.VMEM((zs,) + unit, dtype))
                add("own_sems", dma((1,)))
            if stages[-1] != "plane":
                add("plane_sum", pltpu.VMEM((zs,) + unit, dtype))
        if "shard" in stages:
            add("shard_got", pltpu.VMEM((self.shards - 1,) + unit, dtype))
            add("shard_sent", dma((self.shards,)))
            add("shard_arrived", dma((self.shards,)))
        shape = (zs,) + unit if stages[-1] == "plane" else unit
        if stages[-1] == "spread":
            shape = (chips,) + (() if half else (2,)) + unit
            self.plane = Plane(sizes, True, 0, unit[0])
            for index, buffer in enumerate(self.plane.scratch):
                add("spread%d" % index, buffer)
        self.out_shapes = [jax.ShapeDtypeStruct(shape, dtype)]
        self.out_specs = [VMEM_SPEC]

    def steps(self, ins, outs, scratch):
        buf = types.SimpleNamespace(**dict(zip(self.names, scratch)))
        chip, core, shard = (lax.axis_index(name) for name in ALL)
        now, out, last, sent = ins[0], outs[0], self.stages[-1], []
        mine = out.at[chip] if self.half else out.at[chip, core]

        def carrying(index):
            return index // self.slots == core

        def guard(t, body):
            if self.half:
                pl.when(carrying(shard))(body)
            else:
                body()

        def other(t, body):
            if self.half:
                pl.when(jnp.logical_not(carrying(shard)))(body)
            else:
                body()

        if "pair" in self.stages:
            pair = remote(
                now.at[:, :, 1 - core],
                buf.pair_got,
                buf.pair_sems.at[0],
                buf.pair_sems.at[1],
                {"core": 1 - core},
            )
            pair.start()
            yield
            pair.wait()
            given = now

            def add_pair(index):
                z, c = index // self.chips, lax.rem(index, self.chips)
                total = given[z, c, core].astype(f32) + buf.pair_got[z, c].astype(f32)
                buf.pair_sum[z, c] = total.astype(bf16)

            each(0, self.zs * self.chips, add_pair)
            now = buf.pair_sum
        if self.relay:
            source, target = now, out if last == "plane" else buf.plane_sum

            def near_copy(part, dest):
                near = flipped(chip, part + 1)
                return remote(
                    source.at[:, near if dest == 0 else flipped(chip, 3), part],
                    buf.near_got.at[part, dest],
                    buf.near_sent.at[part, dest],
                    buf.near_arrived.at[part, dest],
                    {"chip": near},
                )

            def relay_copy(part):
                return remote(
                    buf.relay_sum.at[part],
                    buf.relay_got.at[part],
                    buf.relay_sent.at[part],
                    buf.relay_arrived.at[part],
                    {"chip": flipped(chip, 2 - part)},
                )

            def own_copies():
                copies = [(source.at[:, chip], buf.plane_own)]
                for part in range(2):
                    far = flipped(chip, 2 - part)
                    copies.append((source.at[:, far, part], buf.far_own.at[part]))
                return [
                    pltpu.make_async_copy(src, dst, buf.own_sems.at[index])
                    for index, (src, dst) in enumerate(copies)
                ]

            for dest in (1, 0):
                for part in range(2):
                    near_copy(part, dest).start()
            if self.from_hbm:
                for copy in own_copies():
                    copy.start()
            yield
            if self.from_hbm:
                for copy in own_copies():
                    copy.wait()
            for part in range(2):
                near_copy(part, 1).wait_recv()
                far = flipped(chip, 2 - part)

                def add_far(z):
                    own = buf.far_own[part, z] if self.from_hbm else source[z, far, part]
                    total = own.astype(f32) + buf.near_got[part, 1, z].astype(f32)
                    buf.relay_sum[part, z] = total.astype(bf16)

                each(0, self.zs, add_far)
                relay_copy(part).start()
            yield
            for part in range(2):
                near_copy(part, 0).wait_recv()
                relay_copy(part).wait_recv()

                def add_near(z):
                    own = buf.plane_own[z, part] if self.from_hbm else source[z, chip, part]
                    total = own.astype(f32) + buf.near_got[part, 0, z].astype(f32)
                    target[z, part] = (total + buf.relay_got[part, z].astype(f32)).astype(bf16)

                each(0, self.zs, add_near)

            def relay_sent():
                for part in range(2):
                    relay_copy(part).wait_send()
                    for dest in range(2):
                        near_copy(part, dest).wait_send()

            sent.append(relay_sent)
            now = target
        elif "plane" in self.stages:
            partial = now

            def plane_copy(k):
                peer = lax.rem(chip + k, self.chips)
                return remote(
                    partial.at[:, peer],
                    buf.plane_got.at[k - 1],
                    buf.plane_sent.at[k],
                    buf.plane_arrived.at[k],
                    {"chip": peer},
                )

            each(1, self.chips, lambda k: plane_copy(k).start())
            if self.from_hbm:
                own = pltpu.make_async_copy(
                    partial.at[:, chip], buf.plane_own, buf.own_sems.at[0]
                )
                own.start()
            yield
            each(1, self.chips, lambda k: plane_copy(k).wait_recv())
            if self.from_hbm:
                own.wait()
            target = out if last == "plane" else buf.plane_sum

            def add_plane(z):
                total = (buf.plane_own[z] if self.from_hbm else partial[z, chip]).astype(f32)
                for k in range(self.chips - 1):
                    total = total + buf.plane_got[k, z].astype(f32)
                target[z] = total.astype(bf16)

            each(0, self.zs, add_plane)
            sent.append(lambda: each(1, self.chips, lambda k: plane_copy(k).wait_send()))
            now = target
        if "shard" in self.stages:
            summed = now

            def slot(index):
                return lax.rem(index, self.slots) if self.half else index

            def shard_copy(k):
                peer = lax.rem(shard + k, self.shards)
                return peer, remote(
                    summed.at[slot(peer)],
                    buf.shard_got.at[k - 1],
                    buf.shard_sent.at[k],
                    buf.shard_arrived.at[k],
                    {"shard": peer},
                )

            def shard_each(act):
                def one(k):
                    peer, copy = shard_copy(k)
                    if self.half:
                        pl.when(carrying(peer))(lambda: act(copy))
                    else:
                        act(copy)

                each(1, self.shards, one)

            shard_each(lambda copy: copy.start())
            yield

            def add_shard():
                each(1, self.shards, lambda k: shard_copy(k)[1].wait_recv())
                target = mine if last == "spread" else out
                for part in range(target.shape[0]):
                    total = summed[slot(shard), part].astype(f32)
                    for k in range(self.shards - 1):
                        total = total + buf.shard_got[k, part].astype(f32)
                    target[part] = total.astype(bf16)

            guard(0, add_shard)
            sent.append(lambda: shard_each(lambda copy: copy.wait_send()))
        if last == "spread":
            if "shard" not in self.stages:
                mine[...] = now[...]
            self.plane.bind(
                lambda t, c, k: out.at[c, t] if self.half else out.at[c, k, t],
                lambda t: lax.rem(t, 2),
                guard,
                other,
                scratch[-4:],
            )
            self.plane.start()
            yield
            self.plane.forward()
            yield
            self.plane.forwarded()
            yield
            self.plane.finish()
        for wait in sent:
            wait()


class Compute:
    def __init__(self, body, inputs, out_shapes, scratch=()):
        self.body, self.inputs, self.out_shapes = body, list(inputs), list(out_shapes)
        self.scratch = list(scratch)


def greet_all(sizes, wide):
    barrier = pltpu.get_barrier_semaphore()
    groups = [ALL] if wide else [REP, ("shard",)]
    total = 0
    for axes in groups:
        count, me = axes_size(sizes, axes), lax.axis_index(axes)
        total += count - 1

        def greet(k):
            peer = peer_coords(lax.rem(me + k, count), axes, sizes)
            pl.semaphore_signal(barrier, inc=1, device_id=peer, device_id_type=MESH)

        each(1, count, greet)
    pl.semaphore_wait(barrier, total)


DONE = object()


def run(collective_id, name, sizes, items, compute=None, vmem=None):
    wide = any(getattr(item, "axes", ()) == ALL for item in items)
    compute = compute or Compute(None, [], [])
    inputs, in_specs, out_shapes, out_specs, scratch, aliases = [], [], [], [], [], {}
    spans = []
    for item in items:
        if item.aliased:
            aliases[len(inputs)] = len(out_shapes)
        spans.append((len(inputs), len(out_shapes), len(scratch)))
        inputs += item.inputs
        in_specs += item.in_specs
        out_shapes += item.out_shapes
        out_specs += item.out_specs
        scratch += item.scratch
    own = (len(inputs), len(out_shapes), len(scratch))
    inputs += compute.inputs
    in_specs += [VMEM_SPEC] * len(compute.inputs)
    out_shapes += compute.out_shapes
    out_specs += [VMEM_SPEC] * len(compute.out_shapes)
    scratch += compute.scratch
    n_in, n_out = len(inputs), len(out_shapes)

    def kernel(*refs):
        ins, outs, tmp = refs[:n_in], refs[n_in : n_in + n_out], refs[n_in + n_out :]

        def parts(index):
            item, (a, b, c) = items[index], spans[index]
            item_ins = ins[a : a + len(item.inputs)]
            if getattr(item, "source", None) is not None:
                item_ins = [outs[own[1] + item.source]]
            return (
                item_ins,
                outs[b : b + len(item.out_shapes)],
                tmp[c : c + len(item.scratch)],
            )

        greet_all(sizes, wide)
        going = {}
        for index, item in enumerate(items):
            if not item.late:
                going[index] = item.steps(*parts(index))
                next(going[index])
        for index, item in enumerate(items):
            if not item.late:
                for _ in range(item.pre):
                    next(going[index])
        def hook(n):
            for index, item in enumerate(items):
                if n in item.hooks:
                    if index not in going:
                        going[index] = item.steps(*parts(index))
                    next(going[index], DONE)

        hook.outs = [parts(index)[1] for index in range(len(items))]
        if compute.body is not None:
            compute.body(ins[own[0] :], outs[own[1] :], tmp[own[2] :], hook)
        for index, item in enumerate(items):
            if index not in going:
                going[index] = item.steps(*parts(index))
                next(going[index])
        for final in (False, True):
            left = [index for index, item in enumerate(items) if item.final == final]
            while left:
                left = [index for index in left if next(going[index], DONE) is not DONE]

    return pl.pallas_call(
        kernel,
        out_shape=out_shapes,
        in_specs=in_specs,
        out_specs=out_specs,
        scratch_shapes=scratch,
        input_output_aliases=aliases,
        compiler_params=pltpu.CompilerParams(
            collective_id=collective_id, has_side_effects=True, vmem_limit_bytes=vmem
        ),
        name=name,
    )(*inputs)


def mask_rows(code_row):
    index = lax.broadcasted_iota(jnp.int32, (16, code_row.shape[1]), 0)
    return jnp.where(index == code_row, 0.0, NEGATIVE_HUGE).astype(bf16)


def segment_rows(segment_row):
    index = lax.broadcasted_iota(jnp.int32, (16, segment_row.shape[1]), 0)
    return jnp.where(index == segment_row, 1.0, 0.0).astype(bf16)


def as_column(row):
    return jnp.transpose(jnp.broadcast_to(row, (128, row.shape[1])))[:, :1]


def diagonal_bias(info):
    code, place = as_column(info[0:1]), as_column(info[2:3])
    allowed = (place == info[2:3]) | ((code == info[1:2]) & (place <= info[2:3]))
    return jnp.where(allowed, 0.0, NEGATIVE_HUGE)


def forward_body(home, ins, outs, tmp, hook):
    qkv_ref, info_ref = ins
    out_ref, keep_ref, lse_ref = outs
    bias, acc, stat = tmp
    blocks, slots = qkv_ref.shape[0], qkv_ref.shape[1] // 3
    source = key_slots(slots)
    key = [key_unit(slots, source[m]) for m in range(slots)]
    value = [value_unit(slots, source[m]) for m in range(slots)]

    @pl.loop(0, blocks)
    def _(turn):
        i = lax.rem(lax.axis_index(REP) + turn, blocks)
        for n, step in enumerate((blocks // 2, blocks - 2, blocks - 1)):
            pl.when(turn == step)(lambda: hook(n))
        bias[...] = diagonal_bias(info_ref[i])
        seg = segment_rows(info_ref[i, 1:2])
        qa = [jnp.concatenate([qkv_ref[i, m], seg], axis=0) for m in range(slots)]
        for m in range(slots):
            s = dot(jnp.transpose(qkv_ref[i, key[m]]), qkv_ref[i, m]) + bias[...]
            top = jnp.max(s, axis=0, keepdims=True)
            p = jnp.exp(s - top)
            stat[2 * m : 2 * m + 1] = top
            stat[2 * m + 1 : 2 * m + 2] = jnp.sum(p, axis=0, keepdims=True)
            acc[m] = dot(qkv_ref[i, value[m]], p.astype(bf16))

        @pl.loop(0, i)
        def _(j):
            mask = mask_rows(info_ref[j, 0:1])
            for m in range(slots):
                ka = jnp.transpose(jnp.concatenate([qkv_ref[j, key[m]], mask], axis=0))
                s = dot(ka, qa[m])
                old = stat[2 * m : 2 * m + 1]
                top = jnp.maximum(old, jnp.max(s, axis=0, keepdims=True))
                p = jnp.exp(s - top)
                factor = jnp.exp(old - top)
                stat[2 * m : 2 * m + 1] = top
                stat[2 * m + 1 : 2 * m + 2] = stat[2 * m + 1 : 2 * m + 2] * factor + jnp.sum(
                    p, axis=0, keepdims=True
                )
                acc[m] = acc[m] * factor + dot(qkv_ref[j, value[m]], p.astype(bf16))

        for m in range(slots):
            total = stat[2 * m + 1 : 2 * m + 2]
            result = acc[m] / total
            out_ref[i, m] = result.astype(bf16)
            keep_ref[i, m] = result
            lse_ref[i, m : m + 1] = stat[2 * m : 2 * m + 1] + jnp.log(total)
        home.send(i)


def backward_body(ins, outs, tmp, hook):
    qkv_ref, do_ref, keep_ref, lse_ref, info_ref = ins
    (out_ref,) = outs
    bias, dq, qn, don, delta = tmp
    blocks, slots = qkv_ref.shape[0], qkv_ref.shape[1] // 3
    source = key_slots(slots)
    key = [key_unit(slots, source[m]) for m in range(slots)]
    value = [value_unit(slots, source[m]) for m in range(slots)]

    @pl.loop(0, blocks)
    def _(i):
        for m in range(slots):
            qn[i, m] = jnp.transpose(qkv_ref[i, m])
            don[i, m] = jnp.transpose(do_ref[i, m])
            delta[i, m : m + 1] = jnp.sum(
                do_ref[i, m].astype(f32) * keep_ref[i, m], axis=0, keepdims=True
            )
            dq[i, m] = jnp.zeros_like(dq[i, m])

    @pl.loop(0, blocks)
    def _(j):
        for n, step in enumerate((blocks // 2 - 1, blocks // 2, blocks - 2)):
            pl.when(j == step)(lambda: hook(n))
        bias[...] = diagonal_bias(info_ref[j])
        mask = mask_rows(info_ref[j, 0:1])
        kn = [jnp.transpose(qkv_ref[j, key[m]]) for m in range(slots)]
        ka = [
            jnp.transpose(jnp.concatenate([qkv_ref[j, key[m]], mask], axis=0)) for m in range(slots)
        ]
        vn = [jnp.transpose(qkv_ref[j, value[m]]) for m in range(slots)]

        def tile(i, m, s):
            p = jnp.exp(s - lse_ref[i, m : m + 1])
            dp = dot(vn[m], do_ref[i, m])
            ds = (p * (dp - delta[i, m : m + 1])).astype(bf16)
            dq[i, m] += dot(qkv_ref[j, key[m]], ds)
            return dot(ds, qn[i, m]), dot(p.astype(bf16), don[i, m])

        start = []
        for m in range(slots):
            start += list(tile(j, m, dot(kn[m], qkv_ref[j, m]) + bias[...]))

        def later(i, carry):
            seg = segment_rows(info_ref[i, 1:2])
            new = []
            for m in range(slots):
                qa = jnp.concatenate([qkv_ref[i, m], seg], axis=0)
                a, b = tile(i, m, dot(ka[m], qa))
                new += [carry[2 * m] + a, carry[2 * m + 1] + b]
            return tuple(new)

        done = lax.fori_loop(j + 1, blocks, later, tuple(start))
        done = [jnp.transpose(value) for value in done]
        if slots == 2:
            shared = (1 - source[1]).astype(f32)
            done[0] = done[0] + done[2] * shared
            done[1] = done[1] + done[3] * shared
        for m in range(slots):
            out_ref[j, key_unit(slots, m)] = done[2 * m].astype(bf16)
            out_ref[j, value_unit(slots, m)] = done[2 * m + 1].astype(bf16)

    @pl.loop(0, blocks)
    def _(i):
        for m in range(slots):
            out_ref[i, m] = (dq[i, m] * HEAD_DIM ** (-0.5)).astype(bf16)


def ffn_body(late, ins, outs, tmp, hook):
    first_ref, down_ref, attn_ref, out_ref, hidden_ref, grad_ref, scale_ref, gain_ref = ins
    gu_grad_ref, down_grad_ref, part_ref, branch_ref = outs
    raw, weight, ffn, dx, sem = tmp
    (x_ref,), (gf_ref,), (late_ref,) = hook.outs[:3]
    cores, rows, width = x_ref.shape
    core = lax.axis_index("core")
    shards, filled = raw.shape[0], width // raw.shape[0]
    columns = weight.shape[1]
    half = columns // 2
    padded = raw.shape[1] * raw.shape[2]

    @pl.loop(0, rows // 128)
    def _(block):
        at = pl.ds(pl.multiple_of(block * 128, 128), 128)
        branch = dot(attn_ref[:filled, at], out_ref[0, :filled], 0, 0)
        for z in range(1, shards):
            here = attn_ref[z * filled : (z + 1) * filled, at]
            branch = branch + dot(here, out_ref[z, :filled], 0, 0)
        branch_ref[at] = branch
        x_ref[core, at] = rms_scale(hidden_ref[at].astype(f32) + branch, gain_ref[...]).astype(bf16)
        gf_ref[core, at] = (scale_ref[at] * grad_ref[at].astype(f32)).astype(bf16)

    hook(0)

    def compact(get):
        for z in range(shards):
            weight[z * filled : (z + 1) * filled] = get(z)[:filled]

    compact(lambda z: first_ref[z].reshape(padded, columns))
    hook(1)
    x = x_ref[...].reshape(cores * rows, width)
    gf = gf_ref[...].reshape(cores * rows, width)

    @pl.loop(0, late.chunks + 1)
    def _(k):
        at = pl.multiple_of(k * columns, columns)
        down = down_ref[pl.ds(pl.multiple_of(k * half, half), half)]

        @pl.when(k < late.chunks)
        def _():
            late.forward(k)

        both = dot(x, weight[...])
        gate, up = both[:, :half], both[:, half:]
        sig = 1.0 / (1.0 + jnp.exp(-gate))
        act = gate * sig
        hidden = (act * up).astype(bf16)
        grad_hidden = dot(gf, down, 1, 1)
        grad_gate = (grad_hidden * up * (sig * (1.0 + gate * (1.0 - sig)))).astype(bf16)
        grad_up = (grad_hidden * act).astype(bf16)
        grads = jnp.concatenate([grad_gate, grad_up], axis=1)
        ffn_now = dot(hidden, down)
        dx_now = dot(grads, weight[...], 1, 1)

        @pl.when(k == 0)
        def _():
            ffn[...] = ffn_now
            dx[...] = dx_now

        @pl.when(k > 0)
        def _():
            ffn[...] += ffn_now
            dx[...] += dx_now

        @pl.when(k == late.chunks)
        def _():
            for c in range(cores):
                part_ref[c, 0] = dx[c * rows : (c + 1) * rows].astype(bf16)
                part_ref[c, 1] = ffn[c * rows : (c + 1) * rows].astype(bf16)
            hook(2)

        load = pltpu.make_async_copy(late_ref.at[:, :, jnp.minimum(k, late.chunks - 1)], raw, sem.at[0])

        @pl.when(k < late.chunks)
        def _():
            late.arrived(k)
            load.start()

        gu_grad = dot(x, grads, 0, 0)
        for z in range(shards):
            gu_grad_ref[z, :filled, pl.ds(at, columns)] = gu_grad[
                z * filled : (z + 1) * filled
            ].astype(bf16)
            if padded > filled:
                gu_grad_ref[z, filled:, pl.ds(at, columns)] = jnp.zeros(
                    (padded - filled, columns), bf16
                )
        down_grad_ref[pl.ds(pl.multiple_of(k * half, half), half)] = dot(hidden, gf, 0, 0).astype(
            bf16
        )

        @pl.when(k < late.chunks)
        def _():
            load.wait()
            compact(lambda z: raw[z].reshape(padded, columns))


def rms_scale(rows, gain):
    return rows * lax.rsqrt(jnp.mean(rows * rows, axis=-1, keepdims=True) + EPSILON) * gain


def norm_back(rows, gain, grad):
    r = lax.rsqrt(jnp.mean(rows * rows, axis=-1, keepdims=True) + EPSILON)
    scaled = gain * grad
    back = r * scaled - rows * (r * r * r) * jnp.mean(scaled * rows, axis=-1, keepdims=True)
    return back, jnp.sum(grad * rows * r, axis=0)


def line_layout(lengths_row, positions):
    seq_ends = jnp.cumsum(lengths_row, dtype=jnp.int32)
    reached = seq_ends[None, :] <= positions[:, None]
    segment = jnp.sum(reached.astype(jnp.int32), axis=1)
    starts = jnp.max(jnp.where(reached, seq_ends[None, :], 0), axis=1)
    return segment, positions - starts, positions < seq_ends[-1]


def project_body(ins, outs, tmp, hook):
    hidden_ref, weight_ref, gain_ref, cos_ref, sin_ref = ins
    sent_ref, normed_ref, full_ref = outs
    reps, units, _, rows = sent_ref.shape
    slots, filled = units // 3, full_ref.shape[0] // weight_ref.shape[0]
    for z in range(weight_ref.shape[0]):
        full_ref[z * filled : (z + 1) * filled] = weight_ref[z, :filled]
    hidden = hidden_ref[...].astype(f32)
    normed = rms_scale(hidden, gain_ref[...]).astype(bf16)
    normed_ref[...] = normed
    cosines, sines = cos_ref[...], sin_ref[...]
    half, columns = HEAD_DIM // 2, full_ref.shape[1]

    def put(kind, head, value):
        slot = head % slots
        unit = (slot, key_unit(slots, slot), value_unit(slots, slot))[kind]
        sent_ref[head // slots, unit] = value

    for start in range(0, columns, 256):
        stop = min(start + 256, columns)
        block = jnp.transpose(dot(normed, full_ref[:, start:stop]))
        for head in range(start // HEAD_DIM, stop // HEAD_DIM):
            at = head * HEAD_DIM - start
            a, b = block[at : at + half], block[at + half : at + HEAD_DIM]
            if head < QUERY_HEADS:
                scale = HEAD_DIM ** (-0.5)
                put(
                    0,
                    head,
                    (
                        jnp.concatenate(
                            [a * cosines - b * sines, b * cosines + a * sines], axis=0
                        )
                        * scale
                    ).astype(bf16),
                )
            elif head < QUERY_HEADS + KEY_VALUE_HEADS:
                value = jnp.concatenate(
                    [a * cosines - b * sines, b * cosines + a * sines], axis=0
                ).astype(bf16)
                for m in range(GROUP):
                    put(1, (head - QUERY_HEADS) * GROUP + m, value)
            else:
                value = block[at : at + HEAD_DIM].astype(bf16)
                for m in range(GROUP):
                    put(2, (head - QUERY_HEADS - KEY_VALUE_HEADS) * GROUP + m, value)
    for head in range(QUERY_HEADS, reps * slots):
        for kind in range(3):
            put(kind, head, jnp.zeros((HEAD_DIM, rows), bf16))


def project_back_body(ins, outs, tmp, hook):
    (grads_ref, cos_ref, sin_ref, weight_ref, hidden_ref, normed_ref, gain_ref, base_ref) = ins[:8]
    vectors_ref = ins[8]
    sent_ref, weight_grad_ref, vectors_grad_ref = outs
    (dt,) = tmp
    slots, half = grads_ref.shape[1] // 3, HEAD_DIM // 2
    cosines, sines = cos_ref[...], sin_ref[...]

    def get(kind, head):
        slot = head % slots
        unit = (slot, key_unit(slots, slot), value_unit(slots, slot))[kind]
        return grads_ref[head // slots, unit].astype(f32)

    def back(value):
        a, b = value[:half], value[half:]
        return jnp.concatenate([a * cosines + b * sines, b * cosines - a * sines], axis=0)

    for head in range(QUERY_HEADS):
        dt[head * HEAD_DIM : (head + 1) * HEAD_DIM] = back(get(0, head)).astype(bf16)
    for group in range(KEY_VALUE_HEADS):
        for kind in (1, 2):
            value = get(kind, group * GROUP)
            for head in range(group * GROUP + 1, (group + 1) * GROUP):
                if slots != 2 or head % 2 == 0:
                    value = value + get(kind, head)
            if kind == 1:
                value = back(value)
            at = (QUERY_HEADS + (kind - 1) * KEY_VALUE_HEADS + group) * HEAD_DIM
            dt[at : at + HEAD_DIM] = value.astype(bf16)
    grad = dot(dt[...], weight_ref[...], 0, 1)
    norm_grad, gain_grad = norm_back(hidden_ref[...].astype(f32), gain_ref[...], grad)
    index = lax.broadcasted_iota(jnp.int32, vectors_ref.shape, 0)
    vectors = jnp.where(index == 0, gain_grad[None], vectors_ref[...])
    piece = vectors_grad_ref.shape[2]
    for z in range(vectors_grad_ref.shape[0]):
        vectors_grad_ref[z] = vectors[:, z * piece : (z + 1) * piece]
    total = (base_ref[...] + norm_grad).astype(bf16)
    devices, per_pair = sent_ref.shape[:2]
    sent_ref[...] = total.reshape(sent_ref.shape)
    hook(0)
    shards, chips, cores, parts, unit, columns = weight_grad_ref.shape
    filled = normed_ref.shape[1] // shards
    places = [(c, k, p) for c in range(chips) for k in range(cores) for p in range(parts)]
    for start in range(0, columns, 256):
        stop = min(start + 256, columns)
        block = dot(normed_ref[...], dt[start:stop], 0, 1)
        for z in range(shards):
            for r, place in enumerate(places):
                size = max(0, min(unit, filled - r * unit))
                at = z * filled + r * unit
                here = weight_grad_ref.at[z, *place]
                if size:
                    here[:size, start:stop] = block[at : at + size].astype(bf16)
                if size < unit:
                    here[size:, start:stop] = jnp.zeros((unit - size, stop - start), bf16)


def prepare_body(ins, outs, tmp, hook):
    to_slot_ref, cotangent_ref, gate_ref, up_ref, down_ref = ins
    slots_ref, first_ref, late_ref, down_rows_ref = outs
    hook(0)
    sent = dot(to_slot_ref[...], cotangent_ref[...]).astype(bf16)
    slots_ref[...] = sent.reshape(slots_ref.shape)
    chips, unit = first_ref.shape[:2]
    filled, half = gate_ref.shape[0], gate_ref.shape[1] // 2
    for chip in range(chips):
        size = max(0, min(unit, filled - chip * unit))
        for chunk in range(late_ref.shape[1] + 1):
            target = late_ref.at[chip, chunk - 1] if chunk else first_ref.at[chip]
            at = pl.multiple_of(lax.axis_index("core") * half + chunk * FF_CHUNK, FF_CHUNK)
            for which, source in enumerate((gate_ref, up_ref)):
                columns = pl.ds(which * FF_CHUNK, FF_CHUNK)
                if size:
                    rows = pl.ds(chip * unit, size)
                    target[:size, columns] = source[rows, pl.ds(at, FF_CHUNK)]
                if size < unit:
                    target[size:, columns] = jnp.zeros((unit - size, FF_CHUNK), bf16)
    count = down_rows_ref.shape[0]
    for start in range(0, count, 128):
        stop = min(start + 128, count)
        down_rows_ref[start:stop] = jnp.transpose(down_ref[:, start:stop])


def grads_body(ins, outs, tmp, hook):
    (parts_ref, hidden_ref, branch_ref, grad_ref, scale_ref, logit_ref, gain_ref, router_ref) = ins[:8]
    out_weight_ref, attn_ref = ins[8:]
    sent_ref, result_ref, base_ref, vectors_ref, out_grad_ref = outs
    (grad_attn,) = tmp
    rows, width = hidden_ref.shape
    group = 64 // result_ref.shape[1]

    def block(b, carry):
        at = pl.ds(pl.multiple_of(b * 64, 64), 64)
        hidden, branch = hidden_ref[at].astype(f32), branch_ref[at]
        grad, scale = grad_ref[at].astype(f32), scale_ref[at]
        grad_normed = parts_ref[0, 0, at].astype(f32) + parts_ref[1, 0, at].astype(f32)
        ffn = parts_ref[0, 1, at].astype(f32) + parts_ref[1, 1, at].astype(f32)
        total = branch + ffn
        result = (hidden + scale * total).astype(bf16)
        result_ref[pl.ds(b * group, group)] = result.reshape(group, *result_ref.shape[1:])
        grad_logit = logit_ref[at] * jnp.sum(grad * total, axis=1, keepdims=True)
        grad_middle, gain_grad = norm_back(hidden + branch, gain_ref[...], grad_normed)
        grad_attn[at] = (scale * grad + grad_middle).astype(bf16)
        base_ref[at] = grad + grad_middle + grad_logit * router_ref[...]
        router_grad = jnp.sum(grad_logit * hidden, axis=0)
        return carry[0] + gain_grad[None], carry[1] + router_grad[None]

    zero = jnp.zeros((1, width), f32)
    gain_grad, router_grad = lax.fori_loop(0, rows // 64, block, (zero, zero))
    index = lax.broadcasted_iota(jnp.int32, vectors_ref.shape, 0)
    vectors_ref[...] = jnp.where(index == 1, gain_grad, jnp.where(index == 2, router_grad, 0.0))
    reps, slots = sent_ref.shape[:2]
    shards, filled = out_weight_ref.shape[0], width // out_weight_ref.shape[0]
    for z in range(shards):
        piece = dot(out_weight_ref[z, :filled], grad_attn[...], 1, 1).astype(bf16)
        start = z * filled
        while start < (z + 1) * filled:
            head = start // HEAD_DIM
            stop = min((head + 1) * HEAD_DIM, (z + 1) * filled)
            rows_of_head = pl.ds(start - head * HEAD_DIM, stop - start)
            sent_ref[head // slots, head % slots, rows_of_head] = piece[
                start - z * filled : stop - z * filled
            ]
            start = stop
    for head in range(width // HEAD_DIM, reps * slots):
        sent_ref[head // slots, head % slots] = jnp.zeros(sent_ref.shape[2:], bf16)
    hook(0)
    _, chips, cores, parts, unit, _ = out_grad_ref.shape
    places = [(c, k, p) for c in range(chips) for k in range(cores) for p in range(parts)]
    for z in range(shards):
        piece = dot(attn_ref[z * filled : (z + 1) * filled], grad_attn[...])
        for r, place in enumerate(places):
            size = max(0, min(unit, filled - r * unit))
            here = out_grad_ref.at[z, *place]
            if size:
                here[:size] = piece[r * unit : r * unit + size].astype(bf16)
            if size < unit:
                here[size:] = jnp.zeros((unit - size, width), bf16)


def finalize_kernel(*refs):
    gate_up_ref, down_ref, out_ref, qkv_ref, slot_ref, result_ref, grad_ref = refs[:7]
    gate, up, down, out, query, key, value, result, grad = refs[7:]
    lanes = lax.broadcasted_iota(jnp.int32, (slot_ref.shape[0], result_ref.shape[0]), 1)
    from_slot = jnp.where(lanes == slot_ref[...], 1.0, 0.0).astype(bf16)
    result[...] = dot(from_slot, result_ref[...]).astype(bf16)
    grad[...] = dot(from_slot, grad_ref[...]).astype(bf16)
    cores, rows, columns = gate_up_ref.shape[1:]
    half = columns // 2
    for core in range(cores):
        for start in range(0, columns, 2 * FF_CHUNK):
            at = core * half + start // 2
            middle = start + FF_CHUNK
            gate[:, at : at + FF_CHUNK] = gate_up_ref[0, core, :, start:middle].astype(f32)
            up[:, at : at + FF_CHUNK] = gate_up_ref[0, core, :, middle : middle + FF_CHUNK].astype(f32)
    down[...] = down_ref[0].astype(f32)
    out[...] = out_ref[0].astype(f32)
    ends = (query.shape[1], query.shape[1] + key.shape[1])
    qkv = qkv_ref[0].astype(f32)
    query[...] = qkv[:, : ends[0]]
    key[...] = qkv[:, ends[0] : ends[1]]
    value[...] = qkv[:, ends[1] :]


def finalize(gate_up, down, out, qkv, slot_of_row, result, grad, shard_rows, key_width):
    chips, rows = gate_up.shape[0], gate_up.shape[2]
    width, hidden = out.shape[2], gate_up.shape[3]
    columns = (hidden, hidden, None, width, width, key_width, key_width)
    count = result.shape[0] // chips

    def out_spec(array_columns):
        shape = tuple(down.shape[1:]) if array_columns is None else (rows, array_columns)
        return pl.BlockSpec(shape, lambda c: (c, 0))

    def out_type(array_columns):
        shape = (chips * down.shape[1], down.shape[2])
        shape = shape if array_columns is None else (shard_rows, array_columns)
        return jax.ShapeDtypeStruct(shape, f32)

    return pl.pallas_call(
        finalize_kernel,
        grid=(chips,),
        in_specs=[pl.BlockSpec((1, 2, rows, hidden), lambda c: (c, 0, 0, 0))]
        + [pl.BlockSpec((1,) + tuple(a.shape[1:]), lambda c: (c, 0, 0)) for a in (down, out, qkv)]
        + [pl.BlockSpec((count, 1), lambda c: (c, 0))]
        + [pl.BlockSpec(result.shape, lambda c: (0, 0))] * 2,
        out_specs=[out_spec(c) for c in columns]
        + [pl.BlockSpec((count, width), lambda c: (c, 0))] * 2,
        out_shape=[out_type(c) for c in columns] + [jax.ShapeDtypeStruct(result.shape, bf16)] * 2,
        name="finalize",
    )(gate_up, down, out, qkv, slot_of_row[:, None], result, grad)


def rounded_up(value, unit):
    return -(-value // unit) * unit


def local(
    sizes,
    hidden_in,
    cotangent,
    destination,
    seq_lengths,
    gate_mask,
    query_weight,
    key_matrix,
    value_matrix,
    out_weight,
    gate_weight,
    up_weight,
    down_weight,
    attn_gain,
    ffn_gain,
    router_weight,
):
    rows, width = hidden_in.shape
    chips, shards = sizes["chip"], sizes["shard"]
    reps = 2 * chips
    devices = reps * shards
    per_pair = rows // devices
    slots = -(-QUERY_HEADS // reps)
    padded_heads = slots * reps
    chip, core, shard = lax.axis_index("chip"), lax.axis_index("core"), lax.axis_index("shard")
    rep = lax.axis_index(REP)
    shard_rows = query_weight.shape[0]
    rep_unit = rounded_up(-(-shard_rows // reps), 8)
    padded = rep_unit * reps
    chip_unit = padded // chips
    ff_half = gate_weight.shape[1] // 2
    chunks = ff_half // FF_CHUNK

    def padded_rows(array):
        return jnp.pad(array, ((0, padded - shard_rows), (0, 0)))

    qkv_shard = padded_rows(jnp.concatenate([query_weight, key_matrix, value_matrix], axis=1))
    qkv_shard = qkv_shard.reshape(reps, rep_unit, -1)
    out_shard = padded_rows(out_weight).reshape(reps, rep_unit, width)
    down_unit = down_weight.shape[0] // chips
    vectors = jnp.stack([attn_gain, ffn_gain, router_weight]).astype(f32)
    vectors = jnp.pad(vectors, ((0, 5), (0, 0)))

    row_index = jnp.arange(rows, dtype=jnp.int32)
    target = destination // rows
    earlier = (target[None, :] == target[:, None]) & (row_index[None, :] < row_index[:, None])
    slot_of_row = target * per_pair + jnp.sum(earlier.astype(jnp.int32), axis=1)
    to_slot = slot_of_row[None, :] == row_index[:, None]
    to_slot_b = to_slot.astype(bf16)
    place_sent = jnp.sum(jnp.where(to_slot, (destination % rows)[None, :], 0), axis=1)
    place_sent = place_sent.reshape(devices, 1, per_pair)
    place_sent = jnp.pad(place_sent, ((0, 0), (0, 0), (0, 128 - per_pair)))

    def by_slot(tokens):
        tokens = jnp.dot(to_slot_b, tokens, preferred_element_type=f32).astype(bf16)
        return tokens.reshape(devices, per_pair, width)

    first_type = jax.ShapeDtypeStruct((chips, chip_unit, 2 * FF_CHUNK), bf16)
    late_type = jax.ShapeDtypeStruct((chips, chunks - 1, chip_unit, 2 * FF_CHUNK), bf16)
    tokens_type = jax.ShapeDtypeStruct((devices, per_pair, width), bf16)
    got_hidden, got_place, vectors_got, qkv_full, grad_slots, first_shard, late_shard, down_shard = run(
        1,
        "first",
        sizes,
        [
            AllToAll(sizes, by_slot(hidden_in), ALL, late=True).at(0),
            AllToAll(sizes, place_sent, ALL, late=True).at(0),
            AllToAll(sizes, vectors, ("shard",), spread=True),
            Gather(sizes, qkv_shard, REP, "both"),
        ],
        Compute(
            prepare_body,
            [to_slot_b, cotangent, gate_weight, up_weight, jnp.transpose(down_weight)],
            [
                tokens_type,
                first_type,
                late_type,
                jax.ShapeDtypeStruct(down_weight.shape, bf16),
            ],
        ),
    )
    down_shard = down_shard.reshape(chips, down_unit, width)
    hidden = got_hidden.reshape(rows, width)
    place = got_place[:, 0, :per_pair].reshape(rows)
    qkv_full = qkv_full.reshape(shards, padded, -1)
    vectors_full = jnp.transpose(vectors_got[:, :3], (1, 0, 2)).reshape(3, width)
    gain_one, gain_two, full_router = vectors_full[0], vectors_full[1], vectors_full[2]
    router_logit = jnp.sum(hidden.astype(f32) * full_router, axis=1)
    gate_value = jax.nn.sigmoid(router_logit)

    positions = rep * rows + place
    segment, within, is_valid = line_layout(seq_lengths[0], positions)
    here = place[:, None] == row_index[None, :]
    gate_here = jnp.sum(jnp.where(here, gate_mask[None, :], 0), axis=1)
    active = is_valid & (gate_here == 1)
    key_code = jnp.where(active, segment, -1)
    active_f = active.astype(f32)
    branch_scale = (active_f * gate_value)[:, None]
    logit_scale = branch_scale * (1.0 - gate_value)[:, None]
    info = jnp.pad(jnp.stack([key_code, segment, place]), ((0, 5), (0, 0)))
    steps = jnp.arange(HEAD_DIM // 2).astype(f32)
    frequency = jnp.power(ROPE_BASE, -2.0 * steps / HEAD_DIM)
    angles = frequency[:, None] * within.astype(f32)[None, :]
    cosines, sines = jnp.cos(angles), jnp.sin(angles)

    heads_shape = (reps, 3 * slots, HEAD_DIM, rows)
    heads_type = jax.ShapeDtypeStruct(heads_shape, bf16)
    first_z, late_z, out_z, info_got, qkv_got, _, first_normalized, qkv_weights = run(
        2,
        "project",
        sizes,
        [
            Gather(sizes, first_shard, ("chip",), "z"),
            Gather(sizes, late_shard, ("chip",), "z"),
            Gather(sizes, out_shard, REP, "z"),
            AllToAll(sizes, info, REP, spread=True),
            Heads(sizes, heads_type, True, 0),
        ],
        Compute(
            project_body,
            [hidden, qkv_full, gain_one[None], cosines, sines],
            [
                heads_type,
                jax.ShapeDtypeStruct((rows, width), bf16),
                jax.ShapeDtypeStruct((width, qkv_full.shape[2]), bf16),
            ],
        ),
    )
    slot_type = jax.ShapeDtypeStruct((reps, slots, HEAD_DIM, rows), bf16)
    home = Stepwise(sizes, slot_type, 0)
    first_full, down_full, out_full, got_grad, att_home, _, att_keep, lse = run(
        3,
        "attend",
        sizes,
        [
            Gather(sizes, first_z, ("chip",), "plane").at(1),
            Gather(sizes, down_shard, ("chip",), "both", half=True).at(0, 2),
            Gather(sizes, out_z, REP, "plane").at(1),
            AllToAll(sizes, grad_slots, ALL),
            home,
        ],
        Compute(
            functools.partial(forward_body, home),
            [qkv_got, info_got],
            [
                slot_type,
                jax.ShapeDtypeStruct(slot_type.shape, f32),
                jax.ShapeDtypeStruct((reps, 8, rows), f32),
            ],
            [
                pltpu.VMEM((rows, rows), f32),
                pltpu.VMEM((slots, HEAD_DIM, rows), f32),
                pltpu.VMEM((8, rows), f32),
            ],
        ),
    )
    attn_out_t = att_home.reshape(padded_heads * HEAD_DIM, rows)
    out_rows = out_full.reshape(shards, padded, width)
    down = down_full.reshape(ff_half, width)
    grad_out = got_grad.reshape(rows, width)
    late = ChunkGather(sizes, late_z)
    parts_type = jax.ShapeDtypeStruct((2, 2, rows, width), bf16)
    own_type = jax.ShapeDtypeStruct((rows, width), bf16)
    _, _, _, parts_got, gate_up_grad, down_grad, _, attn_branch = run(
        4,
        "feed_forward",
        sizes,
        [
            Swap(sizes, own_type).at(0, 1),
            Swap(sizes, own_type).at(0, 1),
            late,
            AllToAll(sizes, parts_type, ("core",), late=True, source=2).at(2),
        ],
        Compute(
            functools.partial(ffn_body, late),
            [
                first_full,
                down,
                attn_out_t,
                out_rows,
                hidden,
                grad_out,
                branch_scale,
                gain_two[None],
            ],
            [
                jax.ShapeDtypeStruct((shards, padded, 2 * ff_half), bf16),
                jax.ShapeDtypeStruct(down.shape, bf16),
                parts_type,
                jax.ShapeDtypeStruct((rows, width), f32),
            ],
            [
                pltpu.VMEM((shards, chips, chip_unit, 2 * FF_CHUNK), bf16),
                pltpu.VMEM((width, 2 * FF_CHUNK), bf16),
                pltpu.VMEM((2 * rows, width), f32),
                pltpu.VMEM((2 * rows, width), f32),
                pltpu.SemaphoreType.DMA((1,)),
            ],
        ),
        vmem=67_000_000,
    )
    parts = 2 if chips == 4 else 1
    out_grad_type = jax.ShapeDtypeStruct((shards, chips, 2, parts, rep_unit // parts, width), bf16)
    grad_got, _, result, base, vector_grads, out_grad = run(
        6,
        "grads",
        sizes,
        [AllToAll(sizes, slot_type, REP, late=True, source=0).at(0)],
        Compute(
            grads_body,
            [
                parts_got,
                hidden,
                attn_branch,
                grad_out,
                branch_scale,
                logit_scale,
                gain_two[None],
                full_router[None],
                out_rows,
                attn_out_t,
            ],
            [
                slot_type,
                tokens_type,
                jax.ShapeDtypeStruct((rows, width), f32),
                jax.ShapeDtypeStruct((8, width), f32),
                out_grad_type,
            ],
            [pltpu.VMEM((rows, width), bf16)],
        ),
    )
    gate_up_grad = gate_up_grad.reshape(shards, chips, parts, chip_unit // parts, 2 * ff_half)
    down_grad = down_grad.reshape(shards // 2, chips, parts, down_unit // parts, width)
    gate_up_sum, down_sum, out_sum, home_out, heads_home, _ = run(
        7,
        "attend_back",
        sizes,
        [
            Reduce(sizes, gate_up_grad, ("plane", "shard")).at(0, 2),
            Reduce(sizes, down_grad, ("plane",)).at(1),
            Reduce(sizes, out_grad, ("pair", "plane")).at(1),
            AllToAll(sizes, result, ALL),
            Heads(sizes, heads_type, False, 0),
        ],
        Compute(
            backward_body,
            [qkv_got, grad_got, att_keep, lse, info_got],
            [heads_type],
            [
                pltpu.VMEM((rows, rows), f32),
                pltpu.VMEM((reps, slots, HEAD_DIM, rows), f32),
                pltpu.VMEM((reps, slots, rows, HEAD_DIM), bf16),
                pltpu.VMEM((reps, slots, rows, HEAD_DIM), bf16),
                pltpu.VMEM((reps, 8, rows), f32),
            ],
        ),
    )

    qkv_columns = qkv_weights.shape[1]
    qkv_grad_type = jax.ShapeDtypeStruct(
        (shards, chips, 2, parts, rep_unit // parts, qkv_columns), bf16
    )
    vectors_type = jax.ShapeDtypeStruct((shards, 8, shard_rows), f32)
    qkv_home, gate_up_home, down_home, out_home, home_grad, vectors_home = run(
        8,
        "project_back",
        sizes,
        [
            Reduce(sizes, qkv_grad_type, ("pair", "plane", "shard", "spread"), late=True, source=1),
            Reduce(sizes, gate_up_sum, ("spread",)),
            Reduce(sizes, down_sum, ("shard", "spread"), half=True),
            Reduce(sizes, out_sum, ("shard", "spread")),
            AllToAll(sizes, tokens_type, ALL, late=True, source=0).at(0),
            AllToAll(sizes, vectors_type, ALL, by_shard=True, late=True, source=2).at(0),
        ],
        Compute(
            project_back_body,
            [
                heads_home,
                cosines,
                sines,
                qkv_weights,
                hidden,
                first_normalized,
                gain_one[None],
                base,
                vector_grads,
            ],
            [tokens_type, qkv_grad_type, vectors_type],
            [pltpu.VMEM((qkv_columns, rows), bf16)],
        ),
    )[:6]
    weight_grads = finalize(
        gate_up_home.reshape(chips, 2, chip_unit, 2 * ff_half),
        down_home.reshape(chips, down_unit, width),
        out_home.reshape(chips, chip_unit, width),
        qkv_home.reshape(chips, chip_unit, qkv_columns),
        slot_of_row,
        home_out.reshape(rows, width),
        home_grad.reshape(rows, width),
        shard_rows,
        key_matrix.shape[1],
    )
    gate_total, up_total, down_total, out_total, query_total, key_total, value_total = weight_grads[:7]
    vector_total = jnp.sum(vectors_home, axis=0)

    return (
        *weight_grads[7:],
        query_total,
        key_total,
        value_total,
        out_total,
        gate_total,
        up_total,
        down_total,
        vector_total[0],
        vector_total[1],
        vector_total[2],
    )


def solution(mesh):
    reps, shards = mesh.shape["rep"], mesh.shape["shard"]
    sizes = {"chip": reps // 2, "core": 2, "shard": shards}
    split_mesh = Mesh(mesh.devices.reshape(reps // 2, 2, shards), ALL)
    tokens, tokens_1d = P(ALL, None), P(ALL)
    weight, vector = P("shard", None), P("shard")
    return jax.shard_map(
        functools.partial(local, sizes),
        mesh=split_mesh,
        in_specs=(tokens, tokens, tokens_1d, weight, tokens_1d) + (weight,) * 7 + (vector,) * 3,
        out_specs=(tokens, tokens) + (weight,) * 7 + (vector,) * 3,
        check_vma=False,
    )
```

```python
import functools
import types

import jax
import jax.numpy as jnp
from jax import lax
from jax.experimental import pallas as pl
from jax.experimental.pallas import tpu as pltpu
from jax.sharding import Mesh
from jax.sharding import PartitionSpec as P

QUERY_HEADS = 15
KEY_VALUE_HEADS = 5
HEAD_DIM = 64
GROUP = QUERY_HEADS // KEY_VALUE_HEADS
EPSILON = 1e-05
NEGATIVE_HUGE = -1e30
ROPE_BASE = 10000.0
FF_CHUNK = 256
bf16 = jnp.bfloat16
f32 = jnp.float32
MESH = pl.DeviceIdType.MESH
REP = ("chip", "core")
ALL = ("chip", "core", "shard")
VMEM_SPEC = pl.BlockSpec(memory_space=pltpu.VMEM)
HBM_SPEC = pl.BlockSpec(memory_space=pl.ANY)


def dot(a, b, ca=1, cb=0):
    return lax.dot_general(a, b, (((ca,), (cb,)), ((), ())), preferred_element_type=f32)


def axes_size(sizes, axes):
    total = 1
    for name in axes:
        total *= sizes[name]
    return total


def peer_coords(index, axes, sizes):
    coords = {}
    for name in reversed(axes):
        coords[name] = lax.rem(index, sizes[name])
        index = index // sizes[name]
    return coords


def partner(k, axes, sizes, back=False):
    if axes == ALL:
        reps = axes_size(sizes, REP)
        offsets = {"chip": lax.rem(k, reps) // 2, "core": lax.rem(k, 2), "shard": k // reps}
    elif axes == REP:
        offsets = {"chip": k // 2, "core": lax.rem(k, 2)}
    else:
        offsets = {axes[0]: k}
    coords, index = {}, 0
    for name in axes:
        me, count, offset = lax.axis_index(name), sizes[name], offsets[name]
        if name == "chip" and count == 4:
            x = lax.rem(lax.rem(me, 2) + lax.rem(offset, 2), 2)
            coords[name] = 2 * lax.rem(me // 2 + offset // 2, 2) + x
        else:
            coords[name] = lax.rem(me + (count - offset if back else offset), count)
        index = index * count + coords[name]
    return index, coords


def remote(src, dst, send_sem, recv_sem, coords):
    return pltpu.make_async_remote_copy(
        src_ref=src,
        dst_ref=dst,
        send_sem=send_sem,
        recv_sem=recv_sem,
        device_id=coords,
        device_id_type=MESH,
    )


def each(start, stop, body):
    def step(k, carry):
        body(k)
        return carry

    lax.fori_loop(start, stop, step, 0)


class Item:
    late = False
    final = False
    aliased = False
    pre = 0
    hooks = ()

    def at(self, *hooks):
        self.hooks = hooks
        return self

    def steps(self, ins, outs, scratch):
        yield


class AllToAll(Item):
    final = True

    def __init__(self, sizes, array, axes, spread=False, by_shard=False, late=False, source=None):
        self.sizes, self.axes, self.spread, self.late = sizes, axes, spread, late
        self.by_shard = by_shard
        self.count = axes_size(sizes, axes)
        self.source = source
        self.inputs = [] if source is not None else [array]
        piece = tuple(array.shape) if spread else tuple(array.shape[1:])
        self.in_specs = [VMEM_SPEC] * len(self.inputs)
        self.out_shapes = [jax.ShapeDtypeStruct((self.count,) + piece, array.dtype)]
        self.out_specs = [VMEM_SPEC]
        self.scratch = [
            pltpu.SemaphoreType.DMA((self.count,)),
            pltpu.SemaphoreType.DMA((self.count,)),
        ]

    def index(self, peer):
        return lax.rem(peer, self.sizes["shard"]) if self.by_shard else peer

    def copy(self, k, ins, outs, scratch):
        me = lax.axis_index(self.axes)
        peer, coords = partner(k, self.axes, self.sizes)
        return remote(
            ins[0] if self.spread else ins[0].at[self.index(peer)],
            outs[0].at[me],
            scratch[0].at[k],
            scratch[1].at[k],
            coords,
        )

    def steps(self, ins, outs, scratch):
        each(1, self.count, lambda k: self.copy(k, ins, outs, scratch).start())
        me = lax.axis_index(self.axes)
        outs[0][me] = ins[0][...] if self.spread else ins[0][self.index(me)]
        yield
        each(1, self.count, lambda k: self.copy(k, ins, outs, scratch).wait())


class Swap(AllToAll):
    def __init__(self, sizes, array):
        super().__init__(sizes, array, ("core",), spread=True, late=True)
        self.inputs, self.in_specs = [], []

    def steps(self, ins, outs, scratch):
        core = lax.axis_index("core")

        def copy():
            here = outs[0].at[core]
            return remote(here, here, scratch[0].at[1], scratch[1].at[1], {"core": 1 - core})

        copy().start()
        yield
        copy().wait()


class Stepwise(AllToAll):
    def __init__(self, sizes, array, source):
        super().__init__(sizes, array, REP, source=source)

    def copy_to(self, peer):
        me = lax.axis_index(REP)
        return remote(
            self.src.at[peer],
            self.dst.at[me],
            self.sems[0].at[peer],
            self.sems[1].at[me],
            peer_coords(peer, REP, self.sizes),
        )

    def send(self, peer):
        pl.when(peer != lax.axis_index(REP))(lambda: self.copy_to(peer).start())

    def steps(self, ins, outs, scratch):
        self.src, self.dst, self.sems = ins[0], outs[0], scratch
        yield
        me = lax.axis_index(REP)
        outs[0][me] = ins[0][me]

        def wait(k):
            peer = lax.rem(me + k, self.count)
            remote(
                self.src.at[me],
                self.dst.at[peer],
                self.sems[0].at[peer],
                self.sems[1].at[peer],
                peer_coords(peer, REP, self.sizes),
            ).wait_recv()
            self.copy_to(peer).wait_send()

        each(1, self.count, wait)


class Heads(Item):
    final = True
    late = True

    def __init__(self, sizes, array, to, source):
        self.sizes, self.to, self.source = sizes, to, source
        self.count = axes_size(sizes, REP)
        self.slots = array.shape[1] // 3
        self.main = array.shape[1] if self.slots != 2 else 4
        self.units = array.shape[1]
        self.inputs, self.in_specs = [], []
        self.out_shapes = [jax.ShapeDtypeStruct(array.shape, array.dtype)]
        self.out_specs = [VMEM_SPEC]
        dma = pltpu.SemaphoreType.DMA
        self.scratch = [dma((2, self.count)), dma((2, self.count))]

    def copy(self, k, ins, outs, scratch, extra, sending):
        me = lax.axis_index(REP)
        peer, coords = partner(k, REP, self.sizes, not sending)
        units = pl.ds(self.main, self.units - self.main) if extra else pl.ds(0, self.main)
        return peer, remote(
            ins[0].at[peer, units],
            outs[0].at[me if sending else peer, units],
            scratch[0].at[int(extra), k],
            scratch[1].at[int(extra), k],
            coords,
        )

    def every(self, ins, outs, scratch, sending, act):
        def main(k):
            act(self.copy(k, ins, outs, scratch, False, sending)[1])

        def extra(k):
            peer, copy = self.copy(k, ins, outs, scratch, True, sending)
            owner = peer if sending == self.to else lax.axis_index(REP)
            pl.when(apart(owner) == 1)(lambda: act(copy))

        each(1, self.count, main)
        if self.units > self.main:
            each(1, self.count, extra)

    def steps(self, ins, outs, scratch):
        self.every(ins, outs, scratch, True, lambda copy: copy.start())
        me = lax.axis_index(REP)
        outs[0][me] = ins[0][me]
        yield
        self.every(ins, outs, scratch, False, lambda copy: copy.wait_recv())
        self.every(ins, outs, scratch, True, lambda copy: copy.wait_send())


def apart(rep):
    last = KEY_VALUE_HEADS - 1
    return jnp.minimum((2 * rep + 1) // GROUP, last) - jnp.minimum((2 * rep) // GROUP, last)


def key_slots(slots):
    return [0, apart(lax.axis_index(REP))] if slots == 2 else list(range(slots))


def key_unit(slots, slot):
    return slots + 2 * slot


def value_unit(slots, slot):
    return slots + 2 * slot + 1


def flipped(chip, k):
    x, y = lax.rem(chip, 2), chip // 2
    x = 1 - x if k in (1, 3) else x
    y = 1 - y if k in (2, 3) else y
    return 2 * y + x


class Plane:
    def __init__(self, sizes, pair, lo, hi):
        self.pair, self.lo, self.hi, self.chips = pair, lo, hi, sizes["chip"]
        self.relay = self.chips == 4
        self.near = (1, 2) if self.relay else tuple(range(1, self.chips))
        self.scratch = [pltpu.SemaphoreType.DMA((self.chips, hi))] * (4 if pair else 2)

    def bind(self, region, path, guard, other, sems):
        self.region, self.path, self.guard, self.other, self.sems = region, path, guard, other, sems
        self.chip, self.core = lax.axis_index("chip"), lax.axis_index("core")

    def peer(self, k):
        return flipped(self.chip, k) if self.relay else lax.rem(self.chip + k, self.chips)

    def owner(self, k):
        if self.relay:
            return flipped(self.chip, k)
        return lax.rem(self.chip + self.chips - k, self.chips)

    def copy(self, t, k, owner, to):
        ref = self.region(t, owner, self.core)
        return remote(ref, ref, self.sems[0].at[k, t], self.sems[1].at[k, t], {"chip": to})

    def relayed(self, t, k):
        return self.copy(t, 3, self.owner(k), self.peer(3 - k))

    def pass_on(self, t, owner, core=None):
        ref = self.region(t, owner, self.core if core is None else core)
        return remote(
            ref, ref, self.sems[2].at[owner, t], self.sems[3].at[owner, t], {"core": 1 - self.core}
        )

    def parts(self, body, guard=None, span=None):
        lo, hi = span or (self.lo, self.hi)
        each(lo, hi, lambda t: (guard or self.guard)(t, lambda: body(t)))

    def start(self):
        def part(t):
            for k in self.near:
                self.copy(t, k, self.chip, self.peer(k)).start()
            if self.pair:
                self.pass_on(t, self.chip).start()

        self.parts(part)

    def arrived(self, t, k):
        self.copy(t, k, self.owner(k), self.chip).wait_recv()
        if self.pair:
            self.pass_on(t, self.owner(k)).start()

    def forward(self, span=None):
        def part(t):
            for k in self.near:
                self.arrived(t, k)
                if self.relay:
                    pl.when(self.path(t) == k - 1)(lambda: self.relayed(t, k).start())

        self.parts(part, span=span)

    def forwarded(self, span=None):
        if self.relay:
            self.parts(lambda t: self.arrived(t, 3), span=span)

    def finish(self):
        def sent(t):
            for k in self.near:
                self.copy(t, k, self.chip, self.peer(k)).wait_send()
                if self.relay:
                    pl.when(self.path(t) == k - 1)(lambda: self.relayed(t, k).wait_send())
            if self.pair:
                each(0, self.chips, lambda c: self.pass_on(t, c).wait_send())

        self.parts(sent)
        if self.pair:
            self.parts(
                lambda t: each(
                    0, self.chips, lambda c: self.pass_on(t, c, 1 - self.core).wait_recv()
                ),
                self.other,
            )


def always(t, body):
    body()


class Gather(Item):
    def __init__(self, sizes, array, split_axes, stages, half=False):
        self.sizes, self.split_axes, self.stages, self.half = sizes, split_axes, stages, half
        self.shards = sizes["shard"]
        self.slots = self.shards // 2 if half else self.shards
        self.pair = len(split_axes) == 2
        both = stages == "both"
        self.pre = 0 if stages == "plane" or half else 1
        self.inputs = [array]
        self.in_specs = [VMEM_SPEC if both else HBM_SPEC]
        if stages == "plane":
            shape, self.aliased = tuple(array.shape), True
        else:
            shape = (self.slots,) + tuple(array.shape)
        self.out_shapes = [jax.ShapeDtypeStruct(shape, array.dtype)]
        self.out_specs = [VMEM_SPEC if both else HBM_SPEC]
        dma = pltpu.SemaphoreType.DMA
        self.scratch = []
        if stages != "plane":
            self.scratch += [dma((self.shards,)), dma((self.shards,))]
        if stages == "z":
            self.scratch += [pltpu.VMEM(array.shape, array.dtype), dma((2,))]
        else:
            self.plane = Plane(sizes, self.pair, 1, self.shards)
            self.scratch += self.plane.scratch

    def guarded(self, z, body):
        if self.half:
            pl.when(z // self.slots == lax.axis_index("core"))(body)
        else:
            body()

    def slot(self, z):
        return lax.rem(z, self.slots) if self.half else z

    def z_copy(self, k, src, full, scratch, sending):
        me = lax.axis_index("shard")
        mine = lax.axis_index(self.split_axes)
        peer = lax.rem(me + k, self.shards) if sending else lax.rem(me + self.shards - k, self.shards)
        source = me if sending else peer
        dst = full.at[self.slot(source), mine]
        return remote(
            src.at[mine] if sending else dst,
            dst,
            scratch[0].at[k],
            scratch[1].at[k],
            {"shard": peer},
        )

    def z_start(self, src, full, scratch):
        self.guarded(
            lax.axis_index("shard"),
            lambda: each(1, self.shards, lambda k: self.z_copy(k, src, full, scratch, True).start()),
        )

    def z_finish(self, src, full, scratch):
        me = lax.axis_index("shard")

        def receive(k):
            peer = lax.rem(me + self.shards - k, self.shards)
            self.guarded(
                peer, lambda: self.z_copy(k, src, full, scratch, False).wait_recv()
            )

        each(1, self.shards, receive)

        def sent():
            each(1, self.shards, lambda k: self.z_copy(k, src, full, scratch, True).wait_send())

        self.guarded(me, sent)

    def steps(self, ins, outs, scratch):
        me = lax.axis_index("shard")
        src, full = ins[0], outs[0]
        if self.stages == "z":
            self.z_start(src, full, scratch)
            load = pltpu.make_async_copy(src, scratch[2], scratch[3].at[0])
            store = pltpu.make_async_copy(scratch[2], full.at[self.slot(me)], scratch[3].at[1])
            self.guarded(me, load.start)
            yield

            def both():
                load.wait()
                store.start()

            self.guarded(me, both)
            yield
            self.guarded(me, store.wait)
            self.z_finish(src, full, scratch)
            return

        def shard_of(t):
            return lax.rem(me + t, self.shards)

        def region(t, chip, core):
            return full.at[self.slot(shard_of(t)), 2 * chip + core if self.pair else chip]

        guard = (lambda t, body: self.guarded(shard_of(t), body)) if self.half else always
        if self.stages == "both":
            self.z_start(src, full, scratch)

            def keep():
                full[self.slot(me)] = src[...]

            self.guarded(me, keep)
        self.plane.bind(
            region, lambda t: lax.rem(shard_of(t), 2), guard, always, scratch[-len(self.plane.scratch) :]
        )
        if self.stages == "both":
            yield
            self.z_finish(src, full, scratch)
        self.plane.start()
        yield
        self.plane.forward()
        yield
        self.plane.forwarded()
        yield
        self.plane.finish()


class ChunkGather(Item):
    aliased = True
    final = True

    def __init__(self, sizes, array):
        self.shards, self.chunks = sizes["shard"], array.shape[2]
        self.each = self.shards - 1
        self.inputs, self.in_specs = [array], [HBM_SPEC]
        self.out_shapes = [jax.ShapeDtypeStruct(array.shape, array.dtype)]
        self.out_specs = [HBM_SPEC]
        self.plane = Plane(sizes, False, 0, self.chunks * self.each)
        self.scratch = self.plane.scratch

    def span(self, c):
        return (c * self.each, (c + 1) * self.each)

    def forward(self, c):
        self.plane.forward(self.span(c))

    def arrived(self, c):
        self.plane.forwarded(self.span(c))

    def steps(self, ins, outs, scratch):
        me = lax.axis_index("shard")

        def shard_of(t):
            return lax.rem(me + 1 + lax.rem(t, self.each), self.shards)

        self.plane.bind(
            lambda t, chip, core: outs[0].at[shard_of(t), chip, t // self.each],
            lambda t: lax.rem(shard_of(t), 2),
            always,
            always,
            scratch,
        )
        self.plane.start()
        yield
        self.plane.finish()


class Reduce(Item):
    def __init__(self, sizes, array, stages, half=False, late=False, source=None):
        self.stages, self.half, self.late, self.source = stages, half, late, source
        self.pre = int(stages[0] == "pair" and not late)
        self.chips, self.shards = sizes["chip"], sizes["shard"]
        self.slots = self.shards // 2
        lead = {"pair": 3, "plane": 2, "shard": 1, "spread": 0}[stages[0]]
        unit = tuple(array.shape[lead:])
        self.zs = array.shape[0]
        zs, chips, dtype = self.zs, self.chips, array.dtype
        self.inputs = [] if source is not None else [array]
        self.from_hbm = source is None and stages[0] == "plane"
        self.relay = chips == 4 and not late and "plane" in stages
        self.in_specs = [HBM_SPEC if self.from_hbm else VMEM_SPEC] * len(self.inputs)
        self.names, self.scratch = [], []

        def add(name, buffer):
            self.names.append(name)
            self.scratch.append(buffer)

        dma = pltpu.SemaphoreType.DMA
        if "pair" in stages:
            add("pair_got", pltpu.VMEM((zs, chips) + unit, dtype))
            add("pair_sum", pltpu.VMEM((zs, chips) + unit, dtype))
            add("pair_sems", dma((2,)))
        if self.relay:
            half_unit = (zs,) + unit[1:]
            add("near_got", pltpu.VMEM((2, 2) + half_unit, dtype))
            add("relay_sum", pltpu.VMEM((2,) + half_unit, dtype))
            add("relay_got", pltpu.VMEM((2,) + half_unit, dtype))
            add("near_sent", dma((2, 2)))
            add("near_arrived", dma((2, 2)))
            add("relay_sent", dma((2,)))
            add("relay_arrived", dma((2,)))
            if self.from_hbm:
                add("plane_own", pltpu.VMEM((zs,) + unit, dtype))
                add("far_own", pltpu.VMEM((2,) + half_unit, dtype))
                add("own_sems", dma((3,)))
            if stages[-1] != "plane":
                add("plane_sum", pltpu.VMEM((zs,) + unit, dtype))
        elif "plane" in stages:
            add("plane_got", pltpu.VMEM((chips - 1, zs) + unit, dtype))
            add("plane_sent", dma((chips,)))
            add("plane_arrived", dma((chips,)))
            if self.from_hbm:
                add("plane_own", pltpu.VMEM((zs,) + unit, dtype))
                add("own_sems", dma((1,)))
            if stages[-1] != "plane":
                add("plane_sum", pltpu.VMEM((zs,) + unit, dtype))
        if "shard" in stages:
            add("shard_got", pltpu.VMEM((self.shards - 1,) + unit, dtype))
            add("shard_sent", dma((self.shards,)))
            add("shard_arrived", dma((self.shards,)))
        shape = (zs,) + unit if stages[-1] == "plane" else unit
        if stages[-1] == "spread":
            shape = (chips,) + (() if half else (2,)) + unit
            self.plane = Plane(sizes, True, 0, unit[0])
            for index, buffer in enumerate(self.plane.scratch):
                add("spread%d" % index, buffer)
        self.out_shapes = [jax.ShapeDtypeStruct(shape, dtype)]
        self.out_specs = [VMEM_SPEC]

    def steps(self, ins, outs, scratch):
        buf = types.SimpleNamespace(**dict(zip(self.names, scratch)))
        chip, core, shard = (lax.axis_index(name) for name in ALL)
        now, out, last, sent = ins[0], outs[0], self.stages[-1], []
        mine = out.at[chip] if self.half else out.at[chip, core]

        def carrying(index):
            return index // self.slots == core

        def guard(t, body):
            if self.half:
                pl.when(carrying(shard))(body)
            else:
                body()

        def other(t, body):
            if self.half:
                pl.when(jnp.logical_not(carrying(shard)))(body)
            else:
                body()

        if "pair" in self.stages:
            pair = remote(
                now.at[:, :, 1 - core],
                buf.pair_got,
                buf.pair_sems.at[0],
                buf.pair_sems.at[1],
                {"core": 1 - core},
            )
            pair.start()
            yield
            pair.wait()
            given = now

            def add_pair(index):
                z, c = index // self.chips, lax.rem(index, self.chips)
                total = given[z, c, core].astype(f32) + buf.pair_got[z, c].astype(f32)
                buf.pair_sum[z, c] = total.astype(bf16)

            each(0, self.zs * self.chips, add_pair)
            now = buf.pair_sum
        if self.relay:
            source, target = now, out if last == "plane" else buf.plane_sum

            def near_copy(part, dest):
                near = flipped(chip, part + 1)
                return remote(
                    source.at[:, near if dest == 0 else flipped(chip, 3), part],
                    buf.near_got.at[part, dest],
                    buf.near_sent.at[part, dest],
                    buf.near_arrived.at[part, dest],
                    {"chip": near},
                )

            def relay_copy(part):
                return remote(
                    buf.relay_sum.at[part],
                    buf.relay_got.at[part],
                    buf.relay_sent.at[part],
                    buf.relay_arrived.at[part],
                    {"chip": flipped(chip, 2 - part)},
                )

            def own_copies():
                copies = [(source.at[:, chip], buf.plane_own)]
                for part in range(2):
                    far = flipped(chip, 2 - part)
                    copies.append((source.at[:, far, part], buf.far_own.at[part]))
                return [
                    pltpu.make_async_copy(src, dst, buf.own_sems.at[index])
                    for index, (src, dst) in enumerate(copies)
                ]

            for dest in (1, 0):
                for part in range(2):
                    near_copy(part, dest).start()
            if self.from_hbm:
                for copy in own_copies():
                    copy.start()
            yield
            if self.from_hbm:
                for copy in own_copies():
                    copy.wait()
            for part in range(2):
                near_copy(part, 1).wait_recv()
                far = flipped(chip, 2 - part)

                def add_far(z):
                    own = buf.far_own[part, z] if self.from_hbm else source[z, far, part]
                    total = own.astype(f32) + buf.near_got[part, 1, z].astype(f32)
                    buf.relay_sum[part, z] = total.astype(bf16)

                each(0, self.zs, add_far)
                relay_copy(part).start()
            yield
            for part in range(2):
                near_copy(part, 0).wait_recv()
                relay_copy(part).wait_recv()

                def add_near(z):
                    own = buf.plane_own[z, part] if self.from_hbm else source[z, chip, part]
                    total = own.astype(f32) + buf.near_got[part, 0, z].astype(f32)
                    target[z, part] = (total + buf.relay_got[part, z].astype(f32)).astype(bf16)

                each(0, self.zs, add_near)

            def relay_sent():
                for part in range(2):
                    relay_copy(part).wait_send()
                    for dest in range(2):
                        near_copy(part, dest).wait_send()

            sent.append(relay_sent)
            now = target
        elif "plane" in self.stages:
            partial = now

            def plane_copy(k):
                peer = lax.rem(chip + k, self.chips)
                return remote(
                    partial.at[:, peer],
                    buf.plane_got.at[k - 1],
                    buf.plane_sent.at[k],
                    buf.plane_arrived.at[k],
                    {"chip": peer},
                )

            each(1, self.chips, lambda k: plane_copy(k).start())
            if self.from_hbm:
                own = pltpu.make_async_copy(
                    partial.at[:, chip], buf.plane_own, buf.own_sems.at[0]
                )
                own.start()
            yield
            each(1, self.chips, lambda k: plane_copy(k).wait_recv())
            if self.from_hbm:
                own.wait()
            target = out if last == "plane" else buf.plane_sum

            def add_plane(z):
                total = (buf.plane_own[z] if self.from_hbm else partial[z, chip]).astype(f32)
                for k in range(self.chips - 1):
                    total = total + buf.plane_got[k, z].astype(f32)
                target[z] = total.astype(bf16)

            each(0, self.zs, add_plane)
            sent.append(lambda: each(1, self.chips, lambda k: plane_copy(k).wait_send()))
            now = target
        if "shard" in self.stages:
            summed = now

            def slot(index):
                return lax.rem(index, self.slots) if self.half else index

            def shard_copy(k):
                peer = lax.rem(shard + k, self.shards)
                return peer, remote(
                    summed.at[slot(peer)],
                    buf.shard_got.at[k - 1],
                    buf.shard_sent.at[k],
                    buf.shard_arrived.at[k],
                    {"shard": peer},
                )

            def shard_each(act):
                def one(k):
                    peer, copy = shard_copy(k)
                    if self.half:
                        pl.when(carrying(peer))(lambda: act(copy))
                    else:
                        act(copy)

                each(1, self.shards, one)

            shard_each(lambda copy: copy.start())
            yield

            def add_shard():
                each(1, self.shards, lambda k: shard_copy(k)[1].wait_recv())
                target = mine if last == "spread" else out
                for part in range(target.shape[0]):
                    total = summed[slot(shard), part].astype(f32)
                    for k in range(self.shards - 1):
                        total = total + buf.shard_got[k, part].astype(f32)
                    target[part] = total.astype(bf16)

            guard(0, add_shard)
            sent.append(lambda: shard_each(lambda copy: copy.wait_send()))
        if last == "spread":
            if "shard" not in self.stages:

                def keep():
                    mine[...] = now[...]

                guard(0, keep)
            self.plane.bind(
                lambda t, c, k: out.at[c, t] if self.half else out.at[c, k, t],
                lambda t: lax.rem(t, 2),
                guard,
                other,
                scratch[-4:],
            )
            self.plane.start()
            yield
            self.plane.forward()
            yield
            self.plane.forwarded()
            yield
            self.plane.finish()
        for wait in sent:
            wait()


class Compute:
    def __init__(self, body, inputs, out_shapes, scratch=()):
        self.body, self.inputs, self.out_shapes = body, list(inputs), list(out_shapes)
        self.scratch = list(scratch)


def greet_all(sizes, wide):
    barrier = pltpu.get_barrier_semaphore()
    groups = [ALL] if wide else [REP, ("shard",)]
    total = 0
    for axes in groups:
        count, me = axes_size(sizes, axes), lax.axis_index(axes)
        total += count - 1

        def greet(k):
            peer = peer_coords(lax.rem(me + k, count), axes, sizes)
            pl.semaphore_signal(barrier, inc=1, device_id=peer, device_id_type=MESH)

        each(1, count, greet)
    pl.semaphore_wait(barrier, total)


DONE = object()


def run(collective_id, name, sizes, items, compute=None, vmem=None):
    wide = any(getattr(item, "axes", ()) == ALL for item in items)
    compute = compute or Compute(None, [], [])
    inputs, in_specs, out_shapes, out_specs, scratch, aliases = [], [], [], [], [], {}
    spans = []
    for item in items:
        if item.aliased:
            aliases[len(inputs)] = len(out_shapes)
        spans.append((len(inputs), len(out_shapes), len(scratch)))
        inputs += item.inputs
        in_specs += item.in_specs
        out_shapes += item.out_shapes
        out_specs += item.out_specs
        scratch += item.scratch
    own = (len(inputs), len(out_shapes), len(scratch))
    inputs += compute.inputs
    in_specs += [VMEM_SPEC] * len(compute.inputs)
    out_shapes += compute.out_shapes
    out_specs += [VMEM_SPEC] * len(compute.out_shapes)
    scratch += compute.scratch
    n_in, n_out = len(inputs), len(out_shapes)

    def kernel(*refs):
        ins, outs, tmp = refs[:n_in], refs[n_in : n_in + n_out], refs[n_in + n_out :]

        def parts(index):
            item, (a, b, c) = items[index], spans[index]
            item_ins = ins[a : a + len(item.inputs)]
            if getattr(item, "source", None) is not None:
                item_ins = [outs[own[1] + item.source]]
            return (
                item_ins,
                outs[b : b + len(item.out_shapes)],
                tmp[c : c + len(item.scratch)],
            )

        greet_all(sizes, wide)
        going = {}
        for index, item in enumerate(items):
            if not item.late:
                going[index] = item.steps(*parts(index))
                next(going[index])
        for index, item in enumerate(items):
            if not item.late:
                for _ in range(item.pre):
                    next(going[index])
        def hook(n):
            for index, item in enumerate(items):
                if n in item.hooks:
                    if index not in going:
                        going[index] = item.steps(*parts(index))
                    next(going[index], DONE)

        hook.outs = [parts(index)[1] for index in range(len(items))]
        if compute.body is not None:
            compute.body(ins[own[0] :], outs[own[1] :], tmp[own[2] :], hook)
        for index, item in enumerate(items):
            if index not in going:
                going[index] = item.steps(*parts(index))
                next(going[index])
        for final in (False, True):
            left = [index for index, item in enumerate(items) if item.final == final]
            while left:
                left = [index for index in left if next(going[index], DONE) is not DONE]

    return pl.pallas_call(
        kernel,
        out_shape=out_shapes,
        in_specs=in_specs,
        out_specs=out_specs,
        scratch_shapes=scratch,
        input_output_aliases=aliases,
        compiler_params=pltpu.CompilerParams(
            collective_id=collective_id, has_side_effects=True, vmem_limit_bytes=vmem
        ),
        name=name,
    )(*inputs)


def mask_rows(code_row):
    index = lax.broadcasted_iota(jnp.int32, (16, code_row.shape[1]), 0)
    return jnp.where(index == code_row, 0.0, NEGATIVE_HUGE).astype(bf16)


def segment_rows(segment_row):
    index = lax.broadcasted_iota(jnp.int32, (16, segment_row.shape[1]), 0)
    return jnp.where(index == segment_row, 1.0, 0.0).astype(bf16)


def as_column(row):
    return jnp.transpose(jnp.broadcast_to(row, (128, row.shape[1])))[:, :1]


def diagonal_bias(info):
    code, place = as_column(info[0:1]), as_column(info[2:3])
    allowed = (place == info[2:3]) | ((code == info[1:2]) & (place <= info[2:3]))
    return jnp.where(allowed, 0.0, NEGATIVE_HUGE)


def forward_body(home, ins, outs, tmp, hook):
    qkv_ref, info_ref = ins
    out_ref, keep_ref, lse_ref = outs
    bias, acc, stat = tmp
    blocks, slots = qkv_ref.shape[0], qkv_ref.shape[1] // 3
    source = key_slots(slots)
    key = [key_unit(slots, source[m]) for m in range(slots)]
    value = [value_unit(slots, source[m]) for m in range(slots)]

    @pl.loop(0, blocks)
    def _(turn):
        i = lax.rem(lax.axis_index(REP) + turn, blocks)
        for n, step in enumerate((blocks // 2, blocks - 2, blocks - 1)):
            pl.when(turn == step)(lambda: hook(n))
        bias[...] = diagonal_bias(info_ref[i])
        seg = segment_rows(info_ref[i, 1:2])
        qa = [jnp.concatenate([qkv_ref[i, m], seg], axis=0) for m in range(slots)]
        for m in range(slots):
            s = dot(jnp.transpose(qkv_ref[i, key[m]]), qkv_ref[i, m]) + bias[...]
            top = jnp.max(s, axis=0, keepdims=True)
            p = jnp.exp(s - top)
            stat[2 * m : 2 * m + 1] = top
            stat[2 * m + 1 : 2 * m + 2] = jnp.sum(p, axis=0, keepdims=True)
            acc[m] = dot(qkv_ref[i, value[m]], p.astype(bf16))

        @pl.loop(0, i)
        def _(j):
            mask = mask_rows(info_ref[j, 0:1])
            for m in range(slots):
                ka = jnp.transpose(jnp.concatenate([qkv_ref[j, key[m]], mask], axis=0))
                s = dot(ka, qa[m])
                old = stat[2 * m : 2 * m + 1]
                top = jnp.maximum(old, jnp.max(s, axis=0, keepdims=True))
                p = jnp.exp(s - top)
                factor = jnp.exp(old - top)
                stat[2 * m : 2 * m + 1] = top
                stat[2 * m + 1 : 2 * m + 2] = stat[2 * m + 1 : 2 * m + 2] * factor + jnp.sum(
                    p, axis=0, keepdims=True
                )
                acc[m] = acc[m] * factor + dot(qkv_ref[j, value[m]], p.astype(bf16))

        for m in range(slots):
            total = stat[2 * m + 1 : 2 * m + 2]
            result = acc[m] / total
            out_ref[i, m] = result.astype(bf16)
            keep_ref[i, m] = result
            lse_ref[i, m : m + 1] = stat[2 * m : 2 * m + 1] + jnp.log(total)
        home.send(i)


def backward_body(ins, outs, tmp, hook):
    qkv_ref, do_ref, keep_ref, lse_ref, info_ref = ins
    (out_ref,) = outs
    bias, dq, qn, don, delta = tmp
    blocks, slots = qkv_ref.shape[0], qkv_ref.shape[1] // 3
    source = key_slots(slots)
    key = [key_unit(slots, source[m]) for m in range(slots)]
    value = [value_unit(slots, source[m]) for m in range(slots)]

    @pl.loop(0, blocks)
    def _(i):
        for m in range(slots):
            qn[i, m] = jnp.transpose(qkv_ref[i, m])
            don[i, m] = jnp.transpose(do_ref[i, m])
            delta[i, m : m + 1] = jnp.sum(
                do_ref[i, m].astype(f32) * keep_ref[i, m], axis=0, keepdims=True
            )
            dq[i, m] = jnp.zeros_like(dq[i, m])

    @pl.loop(0, blocks)
    def _(j):
        for n, step in enumerate((blocks // 2, blocks // 2 + 1, blocks - 1)):
            pl.when(j == step)(lambda: hook(n))
        bias[...] = diagonal_bias(info_ref[j])
        mask = mask_rows(info_ref[j, 0:1])
        kn = [jnp.transpose(qkv_ref[j, key[m]]) for m in range(slots)]
        ka = [
            jnp.transpose(jnp.concatenate([qkv_ref[j, key[m]], mask], axis=0)) for m in range(slots)
        ]
        vn = [jnp.transpose(qkv_ref[j, value[m]]) for m in range(slots)]

        def tile(i, m, s):
            p = jnp.exp(s - lse_ref[i, m : m + 1])
            dp = dot(vn[m], do_ref[i, m])
            ds = (p * (dp - delta[i, m : m + 1])).astype(bf16)
            dq[i, m] += dot(qkv_ref[j, key[m]], ds)
            return dot(ds, qn[i, m]), dot(p.astype(bf16), don[i, m])

        start = []
        for m in range(slots):
            start += list(tile(j, m, dot(kn[m], qkv_ref[j, m]) + bias[...]))

        def later(i, carry):
            seg = segment_rows(info_ref[i, 1:2])
            new = []
            for m in range(slots):
                qa = jnp.concatenate([qkv_ref[i, m], seg], axis=0)
                a, b = tile(i, m, dot(ka[m], qa))
                new += [carry[2 * m] + a, carry[2 * m + 1] + b]
            return tuple(new)

        done = lax.fori_loop(j + 1, blocks, later, tuple(start))
        done = [jnp.transpose(value) for value in done]
        if slots == 2:
            shared = (1 - source[1]).astype(f32)
            done[0] = done[0] + done[2] * shared
            done[1] = done[1] + done[3] * shared
        for m in range(slots):
            out_ref[j, key_unit(slots, m)] = done[2 * m].astype(bf16)
            out_ref[j, value_unit(slots, m)] = done[2 * m + 1].astype(bf16)

    @pl.loop(0, blocks)
    def _(i):
        for m in range(slots):
            out_ref[i, m] = (dq[i, m] * HEAD_DIM ** (-0.5)).astype(bf16)


def ffn_body(late, ins, outs, tmp, hook):
    first_ref, down_ref, attn_ref, out_ref, hidden_ref, grad_ref, scale_ref, gain_ref = ins
    gu_grad_ref, down_grad_ref, part_ref, branch_ref = outs
    raw, weight, ffn, dx, sem = tmp
    (x_ref,), (gf_ref,), (late_ref,) = hook.outs[:3]
    cores, rows, width = x_ref.shape
    core = lax.axis_index("core")
    shards, filled = raw.shape[0], width // raw.shape[0]
    columns = weight.shape[1]
    half = columns // 2
    padded = raw.shape[1] * raw.shape[2]

    @pl.loop(0, rows // 128)
    def _(block):
        at = pl.ds(pl.multiple_of(block * 128, 128), 128)
        branch = dot(attn_ref[:filled, at], out_ref[0, :filled], 0, 0)
        for z in range(1, shards):
            here = attn_ref[z * filled : (z + 1) * filled, at]
            branch = branch + dot(here, out_ref[z, :filled], 0, 0)
        branch_ref[at] = branch
        x_ref[core, at] = rms_scale(hidden_ref[at].astype(f32) + branch, gain_ref[...]).astype(bf16)
        gf_ref[core, at] = (scale_ref[at] * grad_ref[at].astype(f32)).astype(bf16)

    hook(0)

    def compact(get):
        for z in range(shards):
            weight[z * filled : (z + 1) * filled] = get(z)[:filled]

    compact(lambda z: first_ref[z].reshape(padded, columns))
    hook(1)
    x = x_ref[...].reshape(cores * rows, width)
    gf = gf_ref[...].reshape(cores * rows, width)

    @pl.loop(0, late.chunks + 1)
    def _(k):
        at = pl.multiple_of(k * columns, columns)
        down = down_ref[pl.ds(pl.multiple_of(k * half, half), half)]

        @pl.when(k < late.chunks)
        def _():
            late.forward(k)

        both = dot(x, weight[...])
        gate, up = both[:, :half], both[:, half:]
        sig = 1.0 / (1.0 + jnp.exp(-gate))
        act = gate * sig
        hidden = (act * up).astype(bf16)
        grad_hidden = dot(gf, down, 1, 1)
        grad_gate = (grad_hidden * up * (sig * (1.0 + gate * (1.0 - sig)))).astype(bf16)
        grad_up = (grad_hidden * act).astype(bf16)
        grads = jnp.concatenate([grad_gate, grad_up], axis=1)
        ffn_now = dot(hidden, down)
        dx_now = dot(grads, weight[...], 1, 1)

        @pl.when(k == 0)
        def _():
            ffn[...] = ffn_now
            dx[...] = dx_now

        @pl.when(k > 0)
        def _():
            ffn[...] += ffn_now
            dx[...] += dx_now

        @pl.when(k == late.chunks)
        def _():
            for c in range(cores):
                part_ref[c, 0] = dx[c * rows : (c + 1) * rows].astype(bf16)
                part_ref[c, 1] = ffn[c * rows : (c + 1) * rows].astype(bf16)
            hook(2)

        load = pltpu.make_async_copy(late_ref.at[:, :, jnp.minimum(k, late.chunks - 1)], raw, sem.at[0])

        @pl.when(k < late.chunks)
        def _():
            late.arrived(k)
            load.start()

        gu_grad = dot(x, grads, 0, 0)
        for z in range(shards):
            gu_grad_ref[z, :filled, pl.ds(at, columns)] = gu_grad[
                z * filled : (z + 1) * filled
            ].astype(bf16)
            if padded > filled:
                gu_grad_ref[z, filled:, pl.ds(at, columns)] = jnp.zeros(
                    (padded - filled, columns), bf16
                )
        down_grad_ref[pl.ds(pl.multiple_of(k * half, half), half)] = dot(hidden, gf, 0, 0).astype(
            bf16
        )

        @pl.when(k < late.chunks)
        def _():
            load.wait()
            compact(lambda z: raw[z].reshape(padded, columns))


def rms_scale(rows, gain):
    return rows * lax.rsqrt(jnp.mean(rows * rows, axis=-1, keepdims=True) + EPSILON) * gain


def norm_back(rows, gain, grad):
    r = lax.rsqrt(jnp.mean(rows * rows, axis=-1, keepdims=True) + EPSILON)
    scaled = gain * grad
    back = r * scaled - rows * (r * r * r) * jnp.mean(scaled * rows, axis=-1, keepdims=True)
    return back, jnp.sum(grad * rows * r, axis=0)


def line_layout(lengths_row, positions):
    seq_ends = jnp.cumsum(lengths_row, dtype=jnp.int32)
    reached = seq_ends[None, :] <= positions[:, None]
    segment = jnp.sum(reached.astype(jnp.int32), axis=1)
    starts = jnp.max(jnp.where(reached, seq_ends[None, :], 0), axis=1)
    return segment, positions - starts, positions < seq_ends[-1]


def project_body(ins, outs, tmp, hook):
    hidden_ref, weight_ref, gain_ref, cos_ref, sin_ref = ins
    sent_ref, normed_ref, full_ref = outs
    reps, units, _, rows = sent_ref.shape
    slots, filled = units // 3, full_ref.shape[0] // weight_ref.shape[0]
    for z in range(weight_ref.shape[0]):
        full_ref[z * filled : (z + 1) * filled] = weight_ref[z, :filled]
    hidden = hidden_ref[...].astype(f32)
    normed = rms_scale(hidden, gain_ref[...]).astype(bf16)
    normed_ref[...] = normed
    cosines, sines = cos_ref[...], sin_ref[...]
    half, columns = HEAD_DIM // 2, full_ref.shape[1]

    def put(kind, head, value):
        slot = head % slots
        unit = (slot, key_unit(slots, slot), value_unit(slots, slot))[kind]
        sent_ref[head // slots, unit] = value

    for start in range(0, columns, 256):
        stop = min(start + 256, columns)
        block = jnp.transpose(dot(normed, full_ref[:, start:stop]))
        for head in range(start // HEAD_DIM, stop // HEAD_DIM):
            at = head * HEAD_DIM - start
            a, b = block[at : at + half], block[at + half : at + HEAD_DIM]
            if head < QUERY_HEADS:
                scale = HEAD_DIM ** (-0.5)
                put(
                    0,
                    head,
                    (
                        jnp.concatenate(
                            [a * cosines - b * sines, b * cosines + a * sines], axis=0
                        )
                        * scale
                    ).astype(bf16),
                )
            elif head < QUERY_HEADS + KEY_VALUE_HEADS:
                value = jnp.concatenate(
                    [a * cosines - b * sines, b * cosines + a * sines], axis=0
                ).astype(bf16)
                for m in range(GROUP):
                    put(1, (head - QUERY_HEADS) * GROUP + m, value)
            else:
                value = block[at : at + HEAD_DIM].astype(bf16)
                for m in range(GROUP):
                    put(2, (head - QUERY_HEADS - KEY_VALUE_HEADS) * GROUP + m, value)
    for head in range(QUERY_HEADS, reps * slots):
        for kind in range(3):
            put(kind, head, jnp.zeros((HEAD_DIM, rows), bf16))


def project_back_body(ins, outs, tmp, hook):
    (grads_ref, cos_ref, sin_ref, weight_ref, hidden_ref, normed_ref, gain_ref, base_ref) = ins[:8]
    vectors_ref = ins[8]
    sent_ref, weight_grad_ref, vectors_grad_ref = outs
    (dt,) = tmp
    slots, half = grads_ref.shape[1] // 3, HEAD_DIM // 2
    cosines, sines = cos_ref[...], sin_ref[...]

    def get(kind, head):
        slot = head % slots
        unit = (slot, key_unit(slots, slot), value_unit(slots, slot))[kind]
        return grads_ref[head // slots, unit].astype(f32)

    def back(value):
        a, b = value[:half], value[half:]
        return jnp.concatenate([a * cosines + b * sines, b * cosines - a * sines], axis=0)

    for head in range(QUERY_HEADS):
        dt[head * HEAD_DIM : (head + 1) * HEAD_DIM] = back(get(0, head)).astype(bf16)
    for group in range(KEY_VALUE_HEADS):
        for kind in (1, 2):
            value = get(kind, group * GROUP)
            for head in range(group * GROUP + 1, (group + 1) * GROUP):
                if slots != 2 or head % 2 == 0:
                    value = value + get(kind, head)
            if kind == 1:
                value = back(value)
            at = (QUERY_HEADS + (kind - 1) * KEY_VALUE_HEADS + group) * HEAD_DIM
            dt[at : at + HEAD_DIM] = value.astype(bf16)
    grad = dot(dt[...], weight_ref[...], 0, 1)
    norm_grad, gain_grad = norm_back(hidden_ref[...].astype(f32), gain_ref[...], grad)
    index = lax.broadcasted_iota(jnp.int32, vectors_ref.shape, 0)
    vectors = jnp.where(index == 0, gain_grad[None], vectors_ref[...])
    piece = vectors_grad_ref.shape[2]
    for z in range(vectors_grad_ref.shape[0]):
        vectors_grad_ref[z] = vectors[:, z * piece : (z + 1) * piece]
    total = (base_ref[...] + norm_grad).astype(bf16)
    devices, per_pair = sent_ref.shape[:2]
    sent_ref[...] = total.reshape(sent_ref.shape)
    hook(0)
    shards, chips, cores, parts, unit, columns = weight_grad_ref.shape
    filled = normed_ref.shape[1] // shards
    places = [(c, k, p) for c in range(chips) for k in range(cores) for p in range(parts)]
    for start in range(0, columns, 256):
        stop = min(start + 256, columns)
        block = dot(normed_ref[...], dt[start:stop], 0, 1)
        for z in range(shards):
            for r, place in enumerate(places):
                size = max(0, min(unit, filled - r * unit))
                at = z * filled + r * unit
                here = weight_grad_ref.at[z, *place]
                if size:
                    here[:size, start:stop] = block[at : at + size].astype(bf16)
                if size < unit:
                    here[size:, start:stop] = jnp.zeros((unit - size, stop - start), bf16)


def prepare_body(ins, outs, tmp, hook):
    to_slot_ref, cotangent_ref, gate_ref, up_ref, down_ref = ins
    slots_ref, first_ref, late_ref, down_rows_ref = outs
    hook(0)
    sent = dot(to_slot_ref[...], cotangent_ref[...], 1, 1).astype(bf16)
    slots_ref[...] = sent.reshape(slots_ref.shape)
    chips, unit = first_ref.shape[:2]
    filled, half = gate_ref.shape[0], gate_ref.shape[1] // 2
    for chip in range(chips):
        size = max(0, min(unit, filled - chip * unit))
        for chunk in range(late_ref.shape[1] + 1):
            target = late_ref.at[chip, chunk - 1] if chunk else first_ref.at[chip]
            at = pl.multiple_of(lax.axis_index("core") * half + chunk * FF_CHUNK, FF_CHUNK)
            for which, source in enumerate((gate_ref, up_ref)):
                columns = pl.ds(which * FF_CHUNK, FF_CHUNK)
                if size:
                    rows = pl.ds(chip * unit, size)
                    target[:size, columns] = source[rows, pl.ds(at, FF_CHUNK)]
                if size < unit:
                    target[size:, columns] = jnp.zeros((unit - size, FF_CHUNK), bf16)
    count = down_rows_ref.shape[0]
    for start in range(0, count, 128):
        stop = min(start + 128, count)
        down_rows_ref[start:stop] = jnp.transpose(down_ref[:, start:stop])


def grads_body(ins, outs, tmp, hook):
    (parts_ref, hidden_ref, branch_ref, grad_ref, scale_ref, logit_ref, gain_ref, router_ref) = ins[:8]
    out_weight_ref, attn_ref = ins[8:]
    sent_ref, result_ref, base_ref, vectors_ref, out_grad_ref = outs
    (grad_attn,) = tmp
    rows, width = hidden_ref.shape
    group = 64 // result_ref.shape[1]

    def block(b, carry):
        at = pl.ds(pl.multiple_of(b * 64, 64), 64)
        hidden, branch = hidden_ref[at].astype(f32), branch_ref[at]
        grad, scale = grad_ref[at].astype(f32), scale_ref[at]
        grad_normed = parts_ref[0, 0, at].astype(f32) + parts_ref[1, 0, at].astype(f32)
        ffn = parts_ref[0, 1, at].astype(f32) + parts_ref[1, 1, at].astype(f32)
        total = branch + ffn
        result = (hidden + scale * total).astype(bf16)
        result_ref[pl.ds(b * group, group)] = result.reshape(group, *result_ref.shape[1:])
        grad_logit = logit_ref[at] * jnp.sum(grad * total, axis=1, keepdims=True)
        grad_middle, gain_grad = norm_back(hidden + branch, gain_ref[...], grad_normed)
        grad_attn[at] = (scale * grad + grad_middle).astype(bf16)
        base_ref[at] = grad + grad_middle + grad_logit * router_ref[...]
        router_grad = jnp.sum(grad_logit * hidden, axis=0)
        return carry[0] + gain_grad[None], carry[1] + router_grad[None]

    zero = jnp.zeros((1, width), f32)
    gain_grad, router_grad = lax.fori_loop(0, rows // 64, block, (zero, zero))
    index = lax.broadcasted_iota(jnp.int32, vectors_ref.shape, 0)
    vectors_ref[...] = jnp.where(index == 1, gain_grad, jnp.where(index == 2, router_grad, 0.0))
    reps, slots = sent_ref.shape[:2]
    shards, filled = out_weight_ref.shape[0], width // out_weight_ref.shape[0]
    for z in range(shards):
        piece = dot(out_weight_ref[z, :filled], grad_attn[...], 1, 1).astype(bf16)
        start = z * filled
        while start < (z + 1) * filled:
            head = start // HEAD_DIM
            stop = min((head + 1) * HEAD_DIM, (z + 1) * filled)
            rows_of_head = pl.ds(start - head * HEAD_DIM, stop - start)
            sent_ref[head // slots, head % slots, rows_of_head] = piece[
                start - z * filled : stop - z * filled
            ]
            start = stop
    for head in range(width // HEAD_DIM, reps * slots):
        sent_ref[head // slots, head % slots] = jnp.zeros(sent_ref.shape[2:], bf16)
    hook(0)
    _, chips, cores, parts, unit, _ = out_grad_ref.shape
    places = [(c, k, p) for c in range(chips) for k in range(cores) for p in range(parts)]
    for z in range(shards):
        piece = dot(attn_ref[z * filled : (z + 1) * filled], grad_attn[...])
        for r, place in enumerate(places):
            size = max(0, min(unit, filled - r * unit))
            here = out_grad_ref.at[z, *place]
            if size:
                here[:size] = piece[r * unit : r * unit + size].astype(bf16)
            if size < unit:
                here[size:] = jnp.zeros((unit - size, width), bf16)


def finalize_kernel(*refs):
    gate_up_ref, out_ref, down_ref, qkv_ref, slot_ref, result_ref, grad_ref = refs[:7]
    gate, up, out, query, down, key, value, result, grad = refs[7:]
    cores, rows, columns = gate_up_ref.shape[1:]
    query_end = query.shape[1]

    @pl.when(pl.program_id(0) == 0)
    def _():
        slots = lax.broadcasted_iota(jnp.int32, (result_ref.shape[0], slot_ref.shape[1]), 0)
        to_slot = jnp.where(slots == slot_ref[...], 1.0, 0.0).astype(bf16)
        result[...] = dot(result_ref[...], to_slot, 0, 0).astype(bf16)
        grad[...] = dot(grad_ref[...], to_slot, 0, 0).astype(bf16)
        down[...] = jnp.transpose(down_ref[...]).astype(f32)
        heads = jnp.transpose(qkv_ref[:, query_end:])[:, : key.shape[1]].astype(f32)
        key[...] = heads[: key.shape[0]]
        value[...] = heads[key.shape[0] :]

    half = columns // 2
    for core in range(cores):
        for start in range(0, columns, 2 * FF_CHUNK):
            at = core * half + start // 2
            middle = start + FF_CHUNK
            gate[:, at : at + FF_CHUNK] = gate_up_ref[0, core, :, start:middle].astype(f32)
            up[:, at : at + FF_CHUNK] = gate_up_ref[0, core, :, middle : middle + FF_CHUNK].astype(f32)
    out[...] = out_ref[0].astype(f32)
    at = pl.ds(pl.multiple_of(pl.program_id(0) * rows, rows), rows)
    query[...] = qkv_ref[at, :query_end].astype(f32)


def finalize(gate_up, out, down, qkv, slot_of_row, result, grad, shard_rows, key_width):
    chips, rows = gate_up.shape[0], gate_up.shape[2]
    width, hidden = out.shape[2], gate_up.shape[3]
    by_chip = [(shard_rows, hidden), (shard_rows, hidden), (shard_rows, width), (shard_rows, width)]
    whole = [((width, down.shape[0]), f32)] + [((key_width, shard_rows), f32)] * 2
    whole += [((width, result.shape[0]), bf16)] * 2

    def full(shape):
        return pl.BlockSpec(tuple(shape), lambda c: (0,) * len(shape))

    slots = slot_of_row[None]
    totals = pl.pallas_call(
        finalize_kernel,
        grid=(chips,),
        in_specs=[
            pl.BlockSpec((1, 2, rows, hidden), lambda c: (c, 0, 0, 0)),
            pl.BlockSpec((1, rows, width), lambda c: (c, 0, 0)),
        ]
        + [full(array.shape) for array in (down, qkv, slots, result, grad)],
        out_specs=[pl.BlockSpec((rows, shape[1]), lambda c: (c, 0)) for shape in by_chip]
        + [full(shape) for shape, _ in whole],
        out_shape=[jax.ShapeDtypeStruct(shape, f32) for shape in by_chip]
        + [jax.ShapeDtypeStruct(shape, dtype) for shape, dtype in whole],
        name="finalize",
    )(gate_up, out, down, qkv, slots, result, grad)
    return list(totals[:4]) + [jnp.transpose(total) for total in totals[4:]]


def rounded_up(value, unit):
    return -(-value // unit) * unit


def local(
    sizes,
    hidden_in,
    cotangent,
    destination,
    seq_lengths,
    gate_mask,
    query_weight,
    key_matrix,
    value_matrix,
    out_weight,
    gate_weight,
    up_weight,
    down_weight,
    attn_gain,
    ffn_gain,
    router_weight,
):
    rows, width = hidden_in.shape
    chips, shards = sizes["chip"], sizes["shard"]
    reps = 2 * chips
    devices = reps * shards
    per_pair = rows // devices
    slots = -(-QUERY_HEADS // reps)
    padded_heads = slots * reps
    chip, core, shard = lax.axis_index("chip"), lax.axis_index("core"), lax.axis_index("shard")
    rep = lax.axis_index(REP)
    shard_rows = query_weight.shape[0]
    rep_unit = rounded_up(-(-shard_rows // reps), 8)
    padded = rep_unit * reps
    chip_unit = padded // chips
    ff_half = gate_weight.shape[1] // 2
    chunks = ff_half // FF_CHUNK

    def padded_rows(array):
        return jnp.pad(array, ((0, padded - shard_rows), (0, 0)))

    qkv_shard = padded_rows(jnp.concatenate([query_weight, key_matrix, value_matrix], axis=1))
    qkv_shard = qkv_shard.reshape(reps, rep_unit, -1)
    out_shard = padded_rows(out_weight).reshape(reps, rep_unit, width)
    down_unit = down_weight.shape[0] // chips
    vectors = jnp.stack([attn_gain, ffn_gain, router_weight]).astype(f32)
    vectors = jnp.pad(vectors, ((0, 5), (0, 0)))

    row_index = jnp.arange(rows, dtype=jnp.int32)
    target = destination // rows
    earlier = (target[None, :] == target[:, None]) & (row_index[None, :] < row_index[:, None])
    slot_of_row = target * per_pair + jnp.sum(earlier.astype(jnp.int32), axis=1)
    to_slot = slot_of_row[None, :] == row_index[:, None]
    to_slot_b = to_slot.astype(bf16)
    place_sent = jnp.sum(jnp.where(to_slot, (destination % rows)[None, :], 0), axis=1)
    place_sent = place_sent.reshape(devices, 1, per_pair)
    place_sent = jnp.pad(place_sent, ((0, 0), (0, 0), (0, 128 - per_pair)))

    def by_slot(tokens):
        tokens = jnp.dot(to_slot_b, tokens, preferred_element_type=f32).astype(bf16)
        return tokens.reshape(devices, per_pair, width)

    first_type = jax.ShapeDtypeStruct((chips, chip_unit, 2 * FF_CHUNK), bf16)
    late_type = jax.ShapeDtypeStruct((chips, chunks - 1, chip_unit, 2 * FF_CHUNK), bf16)
    tokens_type = jax.ShapeDtypeStruct((devices, per_pair, width), bf16)
    got_hidden, got_place, vectors_got, qkv_full, grad_slots, first_shard, late_shard, down_shard = run(
        1,
        "first",
        sizes,
        [
            AllToAll(sizes, by_slot(hidden_in), ALL, late=True).at(0),
            AllToAll(sizes, place_sent, ALL, late=True).at(0),
            AllToAll(sizes, vectors, ("shard",), spread=True),
            Gather(sizes, qkv_shard, REP, "both"),
        ],
        Compute(
            prepare_body,
            [
                to_slot_b,
                jnp.transpose(cotangent),
                gate_weight,
                up_weight,
                jnp.transpose(down_weight),
            ],
            [
                tokens_type,
                first_type,
                late_type,
                jax.ShapeDtypeStruct(down_weight.shape, bf16),
            ],
        ),
    )
    down_shard = down_shard.reshape(chips, down_unit, width)
    hidden = got_hidden.reshape(rows, width)
    place = got_place[:, 0, :per_pair].reshape(rows)
    qkv_full = qkv_full.reshape(shards, padded, -1)
    vectors_full = jnp.transpose(vectors_got[:, :3], (1, 0, 2)).reshape(3, width)
    gain_one, gain_two, full_router = vectors_full[0], vectors_full[1], vectors_full[2]
    router_logit = jnp.sum(hidden.astype(f32) * full_router, axis=1)
    gate_value = jax.nn.sigmoid(router_logit)

    positions = rep * rows + place
    segment, within, is_valid = line_layout(seq_lengths[0], positions)
    here = place[:, None] == row_index[None, :]
    gate_here = jnp.sum(jnp.where(here, gate_mask[None, :], 0), axis=1)
    active = is_valid & (gate_here == 1)
    key_code = jnp.where(active, segment, -1)
    active_f = active.astype(f32)
    branch_scale = (active_f * gate_value)[:, None]
    logit_scale = branch_scale * (1.0 - gate_value)[:, None]
    info = jnp.pad(jnp.stack([key_code, segment, place]), ((0, 5), (0, 0)))
    steps = jnp.arange(HEAD_DIM // 2).astype(f32)
    frequency = jnp.power(ROPE_BASE, -2.0 * steps / HEAD_DIM)
    angles = frequency[:, None] * within.astype(f32)[None, :]
    cosines, sines = jnp.cos(angles), jnp.sin(angles)

    heads_shape = (reps, 3 * slots, HEAD_DIM, rows)
    heads_type = jax.ShapeDtypeStruct(heads_shape, bf16)
    first_z, late_z, out_z, info_got, qkv_got, _, first_normalized, qkv_weights = run(
        2,
        "project",
        sizes,
        [
            Gather(sizes, first_shard, ("chip",), "z"),
            Gather(sizes, late_shard, ("chip",), "z"),
            Gather(sizes, out_shard, REP, "z"),
            AllToAll(sizes, info, REP, spread=True),
            Heads(sizes, heads_type, True, 0),
        ],
        Compute(
            project_body,
            [hidden, qkv_full, gain_one[None], cosines, sines],
            [
                heads_type,
                jax.ShapeDtypeStruct((rows, width), bf16),
                jax.ShapeDtypeStruct((width, qkv_full.shape[2]), bf16),
            ],
        ),
    )
    slot_type = jax.ShapeDtypeStruct((reps, slots, HEAD_DIM, rows), bf16)
    home = Stepwise(sizes, slot_type, 0)
    first_full, down_full, out_full, got_grad, att_home, _, att_keep, lse = run(
        3,
        "attend",
        sizes,
        [
            Gather(sizes, first_z, ("chip",), "plane").at(1),
            Gather(sizes, down_shard, ("chip",), "both", half=True).at(0, 2),
            Gather(sizes, out_z, REP, "plane").at(1),
            AllToAll(sizes, grad_slots, ALL),
            home,
        ],
        Compute(
            functools.partial(forward_body, home),
            [qkv_got, info_got],
            [
                slot_type,
                jax.ShapeDtypeStruct(slot_type.shape, f32),
                jax.ShapeDtypeStruct((reps, 8, rows), f32),
            ],
            [
                pltpu.VMEM((rows, rows), f32),
                pltpu.VMEM((slots, HEAD_DIM, rows), f32),
                pltpu.VMEM((8, rows), f32),
            ],
        ),
    )
    attn_out_t = att_home.reshape(padded_heads * HEAD_DIM, rows)
    out_rows = out_full.reshape(shards, padded, width)
    down = down_full.reshape(ff_half, width)
    grad_out = got_grad.reshape(rows, width)
    late = ChunkGather(sizes, late_z)
    parts_type = jax.ShapeDtypeStruct((2, 2, rows, width), bf16)
    own_type = jax.ShapeDtypeStruct((rows, width), bf16)
    _, _, _, parts_got, gate_up_grad, down_grad, _, attn_branch = run(
        4,
        "feed_forward",
        sizes,
        [
            Swap(sizes, own_type).at(0, 1),
            Swap(sizes, own_type).at(0, 1),
            late,
            AllToAll(sizes, parts_type, ("core",), late=True, source=2).at(2),
        ],
        Compute(
            functools.partial(ffn_body, late),
            [
                first_full,
                down,
                attn_out_t,
                out_rows,
                hidden,
                grad_out,
                branch_scale,
                gain_two[None],
            ],
            [
                jax.ShapeDtypeStruct((shards, padded, 2 * ff_half), bf16),
                jax.ShapeDtypeStruct(down.shape, bf16),
                parts_type,
                jax.ShapeDtypeStruct((rows, width), f32),
            ],
            [
                pltpu.VMEM((shards, chips, chip_unit, 2 * FF_CHUNK), bf16),
                pltpu.VMEM((width, 2 * FF_CHUNK), bf16),
                pltpu.VMEM((2 * rows, width), f32),
                pltpu.VMEM((2 * rows, width), f32),
                pltpu.SemaphoreType.DMA((1,)),
            ],
        ),
        vmem=67_000_000,
    )
    parts = 2 if chips == 4 else 1
    out_grad_type = jax.ShapeDtypeStruct((shards, chips, 2, parts, rep_unit // parts, width), bf16)
    grad_got, _, result, base, vector_grads, out_grad = run(
        6,
        "grads",
        sizes,
        [AllToAll(sizes, slot_type, REP, late=True, source=0).at(0)],
        Compute(
            grads_body,
            [
                parts_got,
                hidden,
                attn_branch,
                grad_out,
                branch_scale,
                logit_scale,
                gain_two[None],
                full_router[None],
                out_rows,
                attn_out_t,
            ],
            [
                slot_type,
                tokens_type,
                jax.ShapeDtypeStruct((rows, width), f32),
                jax.ShapeDtypeStruct((8, width), f32),
                out_grad_type,
            ],
            [pltpu.VMEM((rows, width), bf16)],
        ),
    )
    gate_up_grad = gate_up_grad.reshape(shards, chips, parts, chip_unit // parts, 2 * ff_half)
    down_grad = down_grad.reshape(shards // 2, chips, parts, down_unit // parts, width)
    gate_up_sum, down_sum, out_sum, home_out, heads_home, _ = run(
        7,
        "attend_back",
        sizes,
        [
            Reduce(sizes, gate_up_grad, ("plane", "shard")).at(0, 2),
            Reduce(sizes, down_grad, ("plane",)).at(1),
            Reduce(sizes, out_grad, ("pair", "plane")).at(1),
            AllToAll(sizes, result, ALL),
            Heads(sizes, heads_type, False, 0),
        ],
        Compute(
            backward_body,
            [qkv_got, grad_got, att_keep, lse, info_got],
            [heads_type],
            [
                pltpu.VMEM((rows, rows), f32),
                pltpu.VMEM((reps, slots, HEAD_DIM, rows), f32),
                pltpu.VMEM((reps, slots, rows, HEAD_DIM), bf16),
                pltpu.VMEM((reps, slots, rows, HEAD_DIM), bf16),
                pltpu.VMEM((reps, 8, rows), f32),
            ],
        ),
    )

    qkv_columns = qkv_weights.shape[1]
    qkv_grad_type = jax.ShapeDtypeStruct(
        (shards, chips, 2, parts, rep_unit // parts, qkv_columns), bf16
    )
    vectors_type = jax.ShapeDtypeStruct((shards, 8, shard_rows), f32)
    qkv_home, gate_up_home, down_home, out_home, home_grad, vectors_home = run(
        8,
        "project_back",
        sizes,
        [
            Reduce(sizes, qkv_grad_type, ("pair", "plane", "shard", "spread"), late=True, source=1),
            Reduce(sizes, gate_up_sum, ("spread",)),
            Reduce(sizes, down_sum, ("shard", "spread"), half=True),
            Reduce(sizes, out_sum, ("shard", "spread")),
            AllToAll(sizes, tokens_type, ALL, late=True, source=0).at(0),
            AllToAll(sizes, vectors_type, ALL, by_shard=True, late=True, source=2).at(0),
        ],
        Compute(
            project_back_body,
            [
                heads_home,
                cosines,
                sines,
                qkv_weights,
                hidden,
                first_normalized,
                gain_one[None],
                base,
                vector_grads,
            ],
            [tokens_type, qkv_grad_type, vectors_type],
            [pltpu.VMEM((qkv_columns, rows), bf16)],
        ),
    )[:6]
    totals = finalize(
        gate_up_home.reshape(chips, 2, chip_unit, 2 * ff_half),
        out_home.reshape(chips, chip_unit, width),
        down_home.reshape(chips * down_unit, width),
        qkv_home.reshape(padded, qkv_columns),
        slot_of_row,
        home_out.reshape(rows, width),
        home_grad.reshape(rows, width),
        shard_rows,
        key_matrix.shape[1],
    )
    gate_total, up_total, out_total, query_total, down_total, key_total, value_total = totals[:7]
    vector_total = jnp.sum(vectors_home, axis=0)

    return (
        *totals[7:],
        query_total,
        key_total,
        value_total,
        out_total,
        gate_total,
        up_total,
        down_total,
        vector_total[0],
        vector_total[1],
        vector_total[2],
    )


def solution(mesh):
    reps, shards = mesh.shape["rep"], mesh.shape["shard"]
    sizes = {"chip": reps // 2, "core": 2, "shard": shards}
    split_mesh = Mesh(mesh.devices.reshape(reps // 2, 2, shards), ALL)
    tokens, tokens_1d = P(ALL, None), P(ALL)
    weight, vector = P("shard", None), P("shard")
    return jax.shard_map(
        functools.partial(local, sizes),
        mesh=split_mesh,
        in_specs=(tokens, tokens, tokens_1d, weight, tokens_1d) + (weight,) * 7 + (vector,) * 3,
        out_specs=(tokens, tokens) + (weight,) * 7 + (vector,) * 3,
        check_vma=False,
    )
```

```python
import functools
import types

import jax
import jax.numpy as jnp
from jax import lax
from jax.experimental import pallas as pl
from jax.experimental.pallas import tpu as pltpu
from jax.sharding import Mesh
from jax.sharding import PartitionSpec as P

QUERY_HEADS = 15
KEY_VALUE_HEADS = 5
HEAD_DIM = 64
GROUP = QUERY_HEADS // KEY_VALUE_HEADS
EPSILON = 1e-05
NEGATIVE_HUGE = -1e30
ROPE_BASE = 10000.0
FF_CHUNK = 256
bf16 = jnp.bfloat16
f32 = jnp.float32
MESH = pl.DeviceIdType.MESH
REP = ("chip", "core")
ALL = ("chip", "core", "shard")
VMEM_SPEC = pl.BlockSpec(memory_space=pltpu.VMEM)
HBM_SPEC = pl.BlockSpec(memory_space=pl.ANY)


def dot(a, b, ca=1, cb=0):
    return lax.dot_general(a, b, (((ca,), (cb,)), ((), ())), preferred_element_type=f32)


def axes_size(sizes, axes):
    total = 1
    for name in axes:
        total *= sizes[name]
    return total


def peer_coords(index, axes, sizes):
    coords = {}
    for name in reversed(axes):
        coords[name] = lax.rem(index, sizes[name])
        index = index // sizes[name]
    return coords


def partner(k, axes, sizes, back=False):
    if axes == ALL:
        reps = axes_size(sizes, REP)
        offsets = {"chip": lax.rem(k, reps) // 2, "core": lax.rem(k, 2), "shard": k // reps}
    elif axes == REP:
        offsets = {"chip": k // 2, "core": lax.rem(k, 2)}
    else:
        offsets = {axes[0]: k}
    coords, index = {}, 0
    for name in axes:
        me, count, offset = lax.axis_index(name), sizes[name], offsets[name]
        if name == "chip" and count == 4:
            x = lax.rem(lax.rem(me, 2) + lax.rem(offset, 2), 2)
            coords[name] = 2 * lax.rem(me // 2 + offset // 2, 2) + x
        else:
            coords[name] = lax.rem(me + (count - offset if back else offset), count)
        index = index * count + coords[name]
    return index, coords


def remote(src, dst, send_sem, recv_sem, coords):
    return pltpu.make_async_remote_copy(
        src_ref=src,
        dst_ref=dst,
        send_sem=send_sem,
        recv_sem=recv_sem,
        device_id=coords,
        device_id_type=MESH,
    )


def each(start, stop, body):
    def step(k, carry):
        body(k)
        return carry

    lax.fori_loop(start, stop, step, 0)


class Item:
    late = False
    final = False
    aliased = False
    pre = 0
    hooks = ()

    def at(self, *hooks):
        self.hooks = hooks
        return self

    def steps(self, ins, outs, scratch):
        yield


class AllToAll(Item):
    final = True

    def __init__(self, sizes, array, axes, spread=False, by_shard=False, late=False, source=None):
        self.sizes, self.axes, self.spread, self.late = sizes, axes, spread, late
        self.by_shard = by_shard
        self.count = axes_size(sizes, axes)
        self.source = source
        self.inputs = [] if source is not None else [array]
        piece = tuple(array.shape) if spread else tuple(array.shape[1:])
        self.in_specs = [VMEM_SPEC] * len(self.inputs)
        self.out_shapes = [jax.ShapeDtypeStruct((self.count,) + piece, array.dtype)]
        self.out_specs = [VMEM_SPEC]
        self.scratch = [
            pltpu.SemaphoreType.DMA((self.count,)),
            pltpu.SemaphoreType.DMA((self.count,)),
        ]

    def index(self, peer):
        return lax.rem(peer, self.sizes["shard"]) if self.by_shard else peer

    def copy(self, k, ins, outs, scratch):
        me = lax.axis_index(self.axes)
        peer, coords = partner(k, self.axes, self.sizes)
        return remote(
            ins[0] if self.spread else ins[0].at[self.index(peer)],
            outs[0].at[me],
            scratch[0].at[k],
            scratch[1].at[k],
            coords,
        )

    def steps(self, ins, outs, scratch):
        each(1, self.count, lambda k: self.copy(k, ins, outs, scratch).start())
        me = lax.axis_index(self.axes)
        outs[0][me] = ins[0][...] if self.spread else ins[0][self.index(me)]
        yield
        each(1, self.count, lambda k: self.copy(k, ins, outs, scratch).wait())


class Swap(AllToAll):
    def __init__(self, sizes, array):
        super().__init__(sizes, array, ("core",), spread=True, late=True)
        self.inputs, self.in_specs = [], []

    def steps(self, ins, outs, scratch):
        core = lax.axis_index("core")

        def copy():
            here = outs[0].at[core]
            return remote(here, here, scratch[0].at[1], scratch[1].at[1], {"core": 1 - core})

        copy().start()
        yield
        copy().wait()


class Stepwise(AllToAll):
    def __init__(self, sizes, array, source):
        super().__init__(sizes, array, REP, source=source)

    def copy_to(self, peer):
        me = lax.axis_index(REP)
        return remote(
            self.src.at[peer],
            self.dst.at[me],
            self.sems[0].at[peer],
            self.sems[1].at[me],
            peer_coords(peer, REP, self.sizes),
        )

    def send(self, peer):
        pl.when(peer != lax.axis_index(REP))(lambda: self.copy_to(peer).start())

    def steps(self, ins, outs, scratch):
        self.src, self.dst, self.sems = ins[0], outs[0], scratch
        yield
        me = lax.axis_index(REP)
        outs[0][me] = ins[0][me]

        def wait(k):
            peer = lax.rem(me + k, self.count)
            remote(
                self.src.at[me],
                self.dst.at[peer],
                self.sems[0].at[peer],
                self.sems[1].at[peer],
                peer_coords(peer, REP, self.sizes),
            ).wait_recv()
            self.copy_to(peer).wait_send()

        each(1, self.count, wait)


class Heads(Item):
    final = True
    late = True

    def __init__(self, sizes, array, to, source):
        self.sizes, self.to, self.source = sizes, to, source
        self.count = axes_size(sizes, REP)
        self.slots = array.shape[1] // 3
        self.main = array.shape[1] if self.slots != 2 else 4
        self.units = array.shape[1]
        self.inputs, self.in_specs = [], []
        self.out_shapes = [jax.ShapeDtypeStruct(array.shape, array.dtype)]
        self.out_specs = [VMEM_SPEC]
        dma = pltpu.SemaphoreType.DMA
        self.scratch = [dma((3, self.count)), dma((3, self.count))]
        self.bounds = (0, self.slots, self.main, self.units)

    def copy(self, k, ins, outs, scratch, part, sending):
        me = lax.axis_index(REP)
        peer, coords = partner(k, REP, self.sizes, not sending)
        units = pl.ds(self.bounds[part], self.bounds[part + 1] - self.bounds[part])
        return peer, remote(
            ins[0].at[peer, units],
            outs[0].at[me if sending else peer, units],
            scratch[0].at[part, k],
            scratch[1].at[part, k],
            coords,
        )

    def every(self, ins, outs, scratch, sending, act, parts=(0, 1, 2)):
        def main(k, part):
            act(self.copy(k, ins, outs, scratch, part, sending)[1])

        def extra(k):
            peer, copy = self.copy(k, ins, outs, scratch, 2, sending)
            owner = peer if sending == self.to else lax.axis_index(REP)
            pl.when(apart(owner) == 1)(lambda: act(copy))

        for part in parts:
            if part < 2:
                each(1, self.count, lambda k: main(k, part))
            elif self.units > self.main:
                each(1, self.count, extra)

    def steps(self, ins, outs, scratch):
        self.every(ins, outs, scratch, True, lambda copy: copy.start(), (0,))
        if self.hooks:
            yield
        self.every(ins, outs, scratch, True, lambda copy: copy.start(), (1, 2))
        me = lax.axis_index(REP)
        outs[0][me] = ins[0][me]
        yield
        self.every(ins, outs, scratch, False, lambda copy: copy.wait_recv())
        self.every(ins, outs, scratch, True, lambda copy: copy.wait_send())


def apart(rep):
    last = KEY_VALUE_HEADS - 1
    return jnp.minimum((2 * rep + 1) // GROUP, last) - jnp.minimum((2 * rep) // GROUP, last)


def key_slots(slots):
    return [0, apart(lax.axis_index(REP))] if slots == 2 else list(range(slots))


def key_unit(slots, slot):
    return slots + 2 * slot


def value_unit(slots, slot):
    return slots + 2 * slot + 1


def flipped(chip, k):
    x, y = lax.rem(chip, 2), chip // 2
    x = 1 - x if k in (1, 3) else x
    y = 1 - y if k in (2, 3) else y
    return 2 * y + x


class Plane:
    def __init__(self, sizes, pair, lo, hi):
        self.pair, self.lo, self.hi, self.chips = pair, lo, hi, sizes["chip"]
        self.relay = self.chips == 4
        self.near = (1, 2) if self.relay else tuple(range(1, self.chips))
        self.scratch = [pltpu.SemaphoreType.DMA((self.chips, hi))] * (4 if pair else 2)

    def bind(self, region, path, guard, other, sems):
        self.region, self.path, self.guard, self.other, self.sems = region, path, guard, other, sems
        self.chip, self.core = lax.axis_index("chip"), lax.axis_index("core")

    def peer(self, k):
        return flipped(self.chip, k) if self.relay else lax.rem(self.chip + k, self.chips)

    def owner(self, k):
        if self.relay:
            return flipped(self.chip, k)
        return lax.rem(self.chip + self.chips - k, self.chips)

    def copy(self, t, k, owner, to):
        ref = self.region(t, owner, self.core)
        return remote(ref, ref, self.sems[0].at[k, t], self.sems[1].at[k, t], {"chip": to})

    def relayed(self, t, k):
        return self.copy(t, 3, self.owner(k), self.peer(3 - k))

    def pass_on(self, t, owner, core=None):
        ref = self.region(t, owner, self.core if core is None else core)
        return remote(
            ref, ref, self.sems[2].at[owner, t], self.sems[3].at[owner, t], {"core": 1 - self.core}
        )

    def parts(self, body, guard=None, span=None):
        lo, hi = span or (self.lo, self.hi)
        each(lo, hi, lambda t: (guard or self.guard)(t, lambda: body(t)))

    def start(self):
        def part(t):
            for k in self.near:
                self.copy(t, k, self.chip, self.peer(k)).start()
            if self.pair:
                self.pass_on(t, self.chip).start()

        self.parts(part)

    def arrived(self, t, k):
        self.copy(t, k, self.owner(k), self.chip).wait_recv()
        if self.pair:
            self.pass_on(t, self.owner(k)).start()

    def forward(self, span=None):
        def part(t):
            for k in self.near:
                self.arrived(t, k)
                if self.relay:
                    pl.when(self.path(t) == k - 1)(lambda: self.relayed(t, k).start())

        self.parts(part, span=span)

    def forwarded(self, span=None):
        if self.relay:
            self.parts(lambda t: self.arrived(t, 3), span=span)

    def finish(self):
        def sent(t):
            for k in self.near:
                self.copy(t, k, self.chip, self.peer(k)).wait_send()
                if self.relay:
                    pl.when(self.path(t) == k - 1)(lambda: self.relayed(t, k).wait_send())
            if self.pair:
                each(0, self.chips, lambda c: self.pass_on(t, c).wait_send())

        self.parts(sent)
        if self.pair:
            self.parts(
                lambda t: each(
                    0, self.chips, lambda c: self.pass_on(t, c, 1 - self.core).wait_recv()
                ),
                self.other,
            )


def always(t, body):
    body()


class Gather(Item):
    def __init__(self, sizes, array, split_axes, stages, half=False):
        self.sizes, self.split_axes, self.stages, self.half = sizes, split_axes, stages, half
        self.shards = sizes["shard"]
        self.slots = self.shards // 2 if half else self.shards
        self.pair = len(split_axes) == 2
        both = stages == "both"
        self.pre = 0 if stages == "plane" or half else 1
        self.inputs = [array]
        self.in_specs = [VMEM_SPEC if both else HBM_SPEC]
        if stages == "plane":
            shape, self.aliased = tuple(array.shape), True
        else:
            shape = (self.slots,) + tuple(array.shape)
        self.out_shapes = [jax.ShapeDtypeStruct(shape, array.dtype)]
        self.out_specs = [VMEM_SPEC if both else HBM_SPEC]
        dma = pltpu.SemaphoreType.DMA
        self.scratch = []
        if stages != "plane":
            self.scratch += [dma((self.shards,)), dma((self.shards,))]
        if stages == "z":
            self.scratch += [pltpu.VMEM(array.shape, array.dtype), dma((2,))]
        else:
            self.plane = Plane(sizes, self.pair, 1, self.shards)
            self.scratch += self.plane.scratch

    def guarded(self, z, body):
        if self.half:
            pl.when(z // self.slots == lax.axis_index("core"))(body)
        else:
            body()

    def slot(self, z):
        return lax.rem(z, self.slots) if self.half else z

    def z_copy(self, k, src, full, scratch, sending):
        me = lax.axis_index("shard")
        mine = lax.axis_index(self.split_axes)
        peer = lax.rem(me + k, self.shards) if sending else lax.rem(me + self.shards - k, self.shards)
        source = me if sending else peer
        dst = full.at[self.slot(source), mine]
        return remote(
            src.at[mine] if sending else dst,
            dst,
            scratch[0].at[k],
            scratch[1].at[k],
            {"shard": peer},
        )

    def z_start(self, src, full, scratch):
        self.guarded(
            lax.axis_index("shard"),
            lambda: each(1, self.shards, lambda k: self.z_copy(k, src, full, scratch, True).start()),
        )

    def z_finish(self, src, full, scratch):
        me = lax.axis_index("shard")

        def receive(k):
            peer = lax.rem(me + self.shards - k, self.shards)
            self.guarded(
                peer, lambda: self.z_copy(k, src, full, scratch, False).wait_recv()
            )

        each(1, self.shards, receive)

        def sent():
            each(1, self.shards, lambda k: self.z_copy(k, src, full, scratch, True).wait_send())

        self.guarded(me, sent)

    def steps(self, ins, outs, scratch):
        me = lax.axis_index("shard")
        src, full = ins[0], outs[0]
        if self.stages == "z":
            self.z_start(src, full, scratch)
            load = pltpu.make_async_copy(src, scratch[2], scratch[3].at[0])
            store = pltpu.make_async_copy(scratch[2], full.at[self.slot(me)], scratch[3].at[1])
            self.guarded(me, load.start)
            yield

            def both():
                load.wait()
                store.start()

            self.guarded(me, both)
            yield
            self.guarded(me, store.wait)
            self.z_finish(src, full, scratch)
            return

        def shard_of(t):
            return lax.rem(me + t, self.shards)

        def region(t, chip, core):
            return full.at[self.slot(shard_of(t)), 2 * chip + core if self.pair else chip]

        guard = (lambda t, body: self.guarded(shard_of(t), body)) if self.half else always
        if self.stages == "both":
            self.z_start(src, full, scratch)

            def keep():
                full[self.slot(me)] = src[...]

            self.guarded(me, keep)
        self.plane.bind(
            region, lambda t: lax.rem(shard_of(t), 2), guard, always, scratch[-len(self.plane.scratch) :]
        )
        if self.stages == "both":
            yield
            self.z_finish(src, full, scratch)
        self.plane.start()
        yield
        self.plane.forward()
        yield
        self.plane.forwarded()
        yield
        self.plane.finish()


class ChunkGather(Item):
    aliased = True
    final = True

    def __init__(self, sizes, array):
        self.shards, self.chunks = sizes["shard"], array.shape[2]
        self.each = self.shards - 1
        self.inputs, self.in_specs = [array], [HBM_SPEC]
        self.out_shapes = [jax.ShapeDtypeStruct(array.shape, array.dtype)]
        self.out_specs = [HBM_SPEC]
        self.plane = Plane(sizes, False, 0, self.chunks * self.each)
        self.scratch = self.plane.scratch

    def span(self, c):
        return (c * self.each, (c + 1) * self.each)

    def forward(self, c):
        self.plane.forward(self.span(c))

    def arrived(self, c):
        self.plane.forwarded(self.span(c))

    def steps(self, ins, outs, scratch):
        me = lax.axis_index("shard")

        def shard_of(t):
            return lax.rem(me + 1 + lax.rem(t, self.each), self.shards)

        self.plane.bind(
            lambda t, chip, core: outs[0].at[shard_of(t), chip, t // self.each],
            lambda t: lax.rem(shard_of(t), 2),
            always,
            always,
            scratch,
        )
        self.plane.start()
        yield
        self.plane.finish()


class Reduce(Item):
    def __init__(self, sizes, array, stages, half=False, late=False, source=None):
        self.stages, self.half, self.late, self.source = stages, half, late, source
        self.pre = int(stages[0] == "pair" and not late)
        self.chips, self.shards = sizes["chip"], sizes["shard"]
        self.slots = self.shards // 2
        lead = {"pair": 3, "plane": 2, "shard": 1, "spread": 0}[stages[0]]
        unit = tuple(array.shape[lead:])
        self.zs = array.shape[0]
        zs, chips, dtype = self.zs, self.chips, array.dtype
        self.inputs = [] if source is not None else [array]
        self.from_hbm = source is None and stages[0] == "plane"
        self.relay = chips == 4 and not late and "plane" in stages
        self.in_specs = [HBM_SPEC if self.from_hbm else VMEM_SPEC] * len(self.inputs)
        self.names, self.scratch = [], []

        def add(name, buffer):
            self.names.append(name)
            self.scratch.append(buffer)

        dma = pltpu.SemaphoreType.DMA
        if "pair" in stages:
            add("pair_got", pltpu.VMEM((zs, chips) + unit, dtype))
            add("pair_sum", pltpu.VMEM((zs, chips) + unit, dtype))
            add("pair_sems", dma((2,)))
        if self.relay:
            half_unit = (zs,) + unit[1:]
            add("near_got", pltpu.VMEM((2, 2) + half_unit, dtype))
            add("relay_sum", pltpu.VMEM((2,) + half_unit, dtype))
            add("relay_got", pltpu.VMEM((2,) + half_unit, dtype))
            add("near_sent", dma((2, 2)))
            add("near_arrived", dma((2, 2)))
            add("relay_sent", dma((2,)))
            add("relay_arrived", dma((2,)))
            if self.from_hbm:
                add("plane_own", pltpu.VMEM((zs,) + unit, dtype))
                add("far_own", pltpu.VMEM((2,) + half_unit, dtype))
                add("own_sems", dma((3,)))
            if stages[-1] != "plane":
                add("plane_sum", pltpu.VMEM((zs,) + unit, dtype))
        elif "plane" in stages:
            add("plane_got", pltpu.VMEM((chips - 1, zs) + unit, dtype))
            add("plane_sent", dma((chips,)))
            add("plane_arrived", dma((chips,)))
            if self.from_hbm:
                add("plane_own", pltpu.VMEM((zs,) + unit, dtype))
                add("own_sems", dma((1,)))
            if stages[-1] != "plane":
                add("plane_sum", pltpu.VMEM((zs,) + unit, dtype))
        if "shard" in stages:
            add("shard_got", pltpu.VMEM((self.shards - 1,) + unit, dtype))
            add("shard_sent", dma((self.shards,)))
            add("shard_arrived", dma((self.shards,)))
        shape = (zs,) + unit if stages[-1] == "plane" else unit
        if stages[-1] == "spread":
            shape = (chips,) + (() if half else (2,)) + unit
            self.plane = Plane(sizes, True, 0, unit[0])
            for index, buffer in enumerate(self.plane.scratch):
                add("spread%d" % index, buffer)
        self.out_shapes = [jax.ShapeDtypeStruct(shape, dtype)]
        self.out_specs = [VMEM_SPEC]

    def steps(self, ins, outs, scratch):
        buf = types.SimpleNamespace(**dict(zip(self.names, scratch)))
        chip, core, shard = (lax.axis_index(name) for name in ALL)
        now, out, last, sent = ins[0], outs[0], self.stages[-1], []
        mine = out.at[chip] if self.half else out.at[chip, core]

        def carrying(index):
            return index // self.slots == core

        def guard(t, body):
            if self.half:
                pl.when(carrying(shard))(body)
            else:
                body()

        def other(t, body):
            if self.half:
                pl.when(jnp.logical_not(carrying(shard)))(body)
            else:
                body()

        if "pair" in self.stages:
            pair = remote(
                now.at[:, :, 1 - core],
                buf.pair_got,
                buf.pair_sems.at[0],
                buf.pair_sems.at[1],
                {"core": 1 - core},
            )
            pair.start()
            yield
            pair.wait()
            given = now

            def add_pair(index):
                z, c = index // self.chips, lax.rem(index, self.chips)
                total = given[z, c, core].astype(f32) + buf.pair_got[z, c].astype(f32)
                buf.pair_sum[z, c] = total.astype(bf16)

            each(0, self.zs * self.chips, add_pair)
            now = buf.pair_sum
        if self.relay:
            source, target = now, out if last == "plane" else buf.plane_sum

            def near_copy(part, dest):
                near = flipped(chip, part + 1)
                return remote(
                    source.at[:, near if dest == 0 else flipped(chip, 3), part],
                    buf.near_got.at[part, dest],
                    buf.near_sent.at[part, dest],
                    buf.near_arrived.at[part, dest],
                    {"chip": near},
                )

            def relay_copy(part):
                return remote(
                    buf.relay_sum.at[part],
                    buf.relay_got.at[part],
                    buf.relay_sent.at[part],
                    buf.relay_arrived.at[part],
                    {"chip": flipped(chip, 2 - part)},
                )

            def own_copies():
                copies = [(source.at[:, chip], buf.plane_own)]
                for part in range(2):
                    far = flipped(chip, 2 - part)
                    copies.append((source.at[:, far, part], buf.far_own.at[part]))
                return [
                    pltpu.make_async_copy(src, dst, buf.own_sems.at[index])
                    for index, (src, dst) in enumerate(copies)
                ]

            for dest in (1, 0):
                for part in range(2):
                    near_copy(part, dest).start()
            if self.from_hbm:
                for copy in own_copies():
                    copy.start()
            yield
            if self.from_hbm:
                for copy in own_copies():
                    copy.wait()
            for part in range(2):
                near_copy(part, 1).wait_recv()
                far = flipped(chip, 2 - part)

                def add_far(z):
                    own = buf.far_own[part, z] if self.from_hbm else source[z, far, part]
                    total = own.astype(f32) + buf.near_got[part, 1, z].astype(f32)
                    buf.relay_sum[part, z] = total.astype(bf16)

                each(0, self.zs, add_far)
                relay_copy(part).start()
            yield
            for part in range(2):
                near_copy(part, 0).wait_recv()
                relay_copy(part).wait_recv()

                def add_near(z):
                    own = buf.plane_own[z, part] if self.from_hbm else source[z, chip, part]
                    total = own.astype(f32) + buf.near_got[part, 0, z].astype(f32)
                    target[z, part] = (total + buf.relay_got[part, z].astype(f32)).astype(bf16)

                each(0, self.zs, add_near)

            def relay_sent():
                for part in range(2):
                    relay_copy(part).wait_send()
                    for dest in range(2):
                        near_copy(part, dest).wait_send()

            sent.append(relay_sent)
            now = target
        elif "plane" in self.stages:
            partial = now

            def plane_copy(k):
                peer = lax.rem(chip + k, self.chips)
                return remote(
                    partial.at[:, peer],
                    buf.plane_got.at[k - 1],
                    buf.plane_sent.at[k],
                    buf.plane_arrived.at[k],
                    {"chip": peer},
                )

            each(1, self.chips, lambda k: plane_copy(k).start())
            if self.from_hbm:
                own = pltpu.make_async_copy(
                    partial.at[:, chip], buf.plane_own, buf.own_sems.at[0]
                )
                own.start()
            yield
            each(1, self.chips, lambda k: plane_copy(k).wait_recv())
            if self.from_hbm:
                own.wait()
            target = out if last == "plane" else buf.plane_sum

            def add_plane(z):
                total = (buf.plane_own[z] if self.from_hbm else partial[z, chip]).astype(f32)
                for k in range(self.chips - 1):
                    total = total + buf.plane_got[k, z].astype(f32)
                target[z] = total.astype(bf16)

            each(0, self.zs, add_plane)
            sent.append(lambda: each(1, self.chips, lambda k: plane_copy(k).wait_send()))
            now = target
        if "shard" in self.stages:
            summed = now

            def slot(index):
                return lax.rem(index, self.slots) if self.half else index

            def shard_copy(k):
                peer = lax.rem(shard + k, self.shards)
                return peer, remote(
                    summed.at[slot(peer)],
                    buf.shard_got.at[k - 1],
                    buf.shard_sent.at[k],
                    buf.shard_arrived.at[k],
                    {"shard": peer},
                )

            def shard_each(act):
                def one(k):
                    peer, copy = shard_copy(k)
                    if self.half:
                        pl.when(carrying(peer))(lambda: act(copy))
                    else:
                        act(copy)

                each(1, self.shards, one)

            shard_each(lambda copy: copy.start())
            yield

            def add_shard():
                each(1, self.shards, lambda k: shard_copy(k)[1].wait_recv())
                target = mine if last == "spread" else out
                for part in range(target.shape[0]):
                    total = summed[slot(shard), part].astype(f32)
                    for k in range(self.shards - 1):
                        total = total + buf.shard_got[k, part].astype(f32)
                    target[part] = total.astype(bf16)

            guard(0, add_shard)
            sent.append(lambda: shard_each(lambda copy: copy.wait_send()))
        if last == "spread":
            if "shard" not in self.stages:

                def keep():
                    mine[...] = now[...]

                guard(0, keep)
            self.plane.bind(
                lambda t, c, k: out.at[c, t] if self.half else out.at[c, k, t],
                lambda t: lax.rem(t, 2),
                guard,
                other,
                scratch[-4:],
            )
            self.plane.start()
            yield
            self.plane.forward()
            yield
            self.plane.forwarded()
            yield
            self.plane.finish()
        for wait in sent:
            wait()


class Compute:
    def __init__(self, body, inputs, out_shapes, scratch=()):
        self.body, self.inputs, self.out_shapes = body, list(inputs), list(out_shapes)
        self.scratch = list(scratch)


def greet_all(sizes, wide):
    barrier = pltpu.get_barrier_semaphore()
    groups = [ALL] if wide else [REP, ("shard",)]
    total = 0
    for axes in groups:
        count, me = axes_size(sizes, axes), lax.axis_index(axes)
        total += count - 1

        def greet(k):
            peer = peer_coords(lax.rem(me + k, count), axes, sizes)
            pl.semaphore_signal(barrier, inc=1, device_id=peer, device_id_type=MESH)

        each(1, count, greet)
    pl.semaphore_wait(barrier, total)


DONE = object()


def run(collective_id, name, sizes, items, compute=None, vmem=None):
    wide = any(getattr(item, "axes", ()) == ALL for item in items)
    compute = compute or Compute(None, [], [])
    inputs, in_specs, out_shapes, out_specs, scratch, aliases = [], [], [], [], [], {}
    spans = []
    for item in items:
        if item.aliased:
            aliases[len(inputs)] = len(out_shapes)
        spans.append((len(inputs), len(out_shapes), len(scratch)))
        inputs += item.inputs
        in_specs += item.in_specs
        out_shapes += item.out_shapes
        out_specs += item.out_specs
        scratch += item.scratch
    own = (len(inputs), len(out_shapes), len(scratch))
    inputs += compute.inputs
    in_specs += [VMEM_SPEC] * len(compute.inputs)
    out_shapes += compute.out_shapes
    out_specs += [VMEM_SPEC] * len(compute.out_shapes)
    scratch += compute.scratch
    n_in, n_out = len(inputs), len(out_shapes)

    def kernel(*refs):
        ins, outs, tmp = refs[:n_in], refs[n_in : n_in + n_out], refs[n_in + n_out :]

        def parts(index):
            item, (a, b, c) = items[index], spans[index]
            item_ins = ins[a : a + len(item.inputs)]
            if getattr(item, "source", None) is not None:
                item_ins = [outs[own[1] + item.source]]
            return (
                item_ins,
                outs[b : b + len(item.out_shapes)],
                tmp[c : c + len(item.scratch)],
            )

        greet_all(sizes, wide)
        going = {}
        for index, item in enumerate(items):
            if not item.late:
                going[index] = item.steps(*parts(index))
                next(going[index])
        for index, item in enumerate(items):
            if not item.late:
                for _ in range(item.pre):
                    next(going[index])
        def hook(n):
            for index, item in enumerate(items):
                if n in item.hooks:
                    if index not in going:
                        going[index] = item.steps(*parts(index))
                    next(going[index], DONE)

        hook.outs = [parts(index)[1] for index in range(len(items))]
        if compute.body is not None:
            compute.body(ins[own[0] :], outs[own[1] :], tmp[own[2] :], hook)
        for index, item in enumerate(items):
            if index not in going:
                going[index] = item.steps(*parts(index))
                next(going[index])
        for final in (False, True):
            left = [index for index, item in enumerate(items) if item.final == final]
            while left:
                left = [index for index in left if next(going[index], DONE) is not DONE]

    return pl.pallas_call(
        kernel,
        out_shape=out_shapes,
        in_specs=in_specs,
        out_specs=out_specs,
        scratch_shapes=scratch,
        input_output_aliases=aliases,
        compiler_params=pltpu.CompilerParams(
            collective_id=collective_id, has_side_effects=True, vmem_limit_bytes=vmem
        ),
        name=name,
    )(*inputs)


def mask_rows(code_row):
    index = lax.broadcasted_iota(jnp.int32, (16, code_row.shape[1]), 0)
    return jnp.where(index == code_row, 0.0, NEGATIVE_HUGE).astype(bf16)


def segment_rows(segment_row):
    index = lax.broadcasted_iota(jnp.int32, (16, segment_row.shape[1]), 0)
    return jnp.where(index == segment_row, 1.0, 0.0).astype(bf16)


def as_column(row):
    return jnp.transpose(jnp.broadcast_to(row, (128, row.shape[1])))[:, :1]


def diagonal_bias(info):
    code, place = as_column(info[0:1]), as_column(info[2:3])
    allowed = (place == info[2:3]) | ((code == info[1:2]) & (place <= info[2:3]))
    return jnp.where(allowed, 0.0, NEGATIVE_HUGE)


def forward_body(home, ins, outs, tmp, hook):
    qkv_ref, info_ref = ins
    out_ref, keep_ref, lse_ref = outs
    bias, acc, stat = tmp
    blocks, slots = qkv_ref.shape[0], qkv_ref.shape[1] // 3
    source = key_slots(slots)
    key = [key_unit(slots, source[m]) for m in range(slots)]
    value = [value_unit(slots, source[m]) for m in range(slots)]

    @pl.loop(0, blocks)
    def _(turn):
        i = lax.rem(lax.axis_index(REP) + turn, blocks)
        for n, step in enumerate((blocks // 2, blocks - 2, blocks - 1)):
            pl.when(turn == step)(lambda: hook(n))
        bias[...] = diagonal_bias(info_ref[i])
        seg = segment_rows(info_ref[i, 1:2])
        qa = [jnp.concatenate([qkv_ref[i, m], seg], axis=0) for m in range(slots)]
        for m in range(slots):
            s = dot(jnp.transpose(qkv_ref[i, key[m]]), qkv_ref[i, m]) + bias[...]
            top = jnp.max(s, axis=0, keepdims=True)
            p = jnp.exp(s - top)
            stat[2 * m : 2 * m + 1] = top
            stat[2 * m + 1 : 2 * m + 2] = jnp.sum(p, axis=0, keepdims=True)
            acc[m] = dot(qkv_ref[i, value[m]], p.astype(bf16))

        @pl.loop(0, i)
        def _(j):
            mask = mask_rows(info_ref[j, 0:1])
            for m in range(slots):
                ka = jnp.transpose(jnp.concatenate([qkv_ref[j, key[m]], mask], axis=0))
                s = dot(ka, qa[m])
                old = stat[2 * m : 2 * m + 1]
                top = jnp.maximum(old, jnp.max(s, axis=0, keepdims=True))
                p = jnp.exp(s - top)
                factor = jnp.exp(old - top)
                stat[2 * m : 2 * m + 1] = top
                stat[2 * m + 1 : 2 * m + 2] = stat[2 * m + 1 : 2 * m + 2] * factor + jnp.sum(
                    p, axis=0, keepdims=True
                )
                acc[m] = acc[m] * factor + dot(qkv_ref[j, value[m]], p.astype(bf16))

        for m in range(slots):
            total = stat[2 * m + 1 : 2 * m + 2]
            result = acc[m] / total
            out_ref[i, m] = result.astype(bf16)
            keep_ref[i, m] = result
            lse_ref[i, m : m + 1] = stat[2 * m : 2 * m + 1] + jnp.log(total)
        home.send(i)


def backward_body(ins, outs, tmp, hook):
    qkv_ref, do_ref, keep_ref, lse_ref, info_ref = ins
    (out_ref,) = outs
    bias, dq, qn, don, delta = tmp
    blocks, slots = qkv_ref.shape[0], qkv_ref.shape[1] // 3
    source = key_slots(slots)
    key = [key_unit(slots, source[m]) for m in range(slots)]
    value = [value_unit(slots, source[m]) for m in range(slots)]

    @pl.loop(0, blocks)
    def _(i):
        for m in range(slots):
            qn[i, m] = jnp.transpose(qkv_ref[i, m])
            don[i, m] = jnp.transpose(do_ref[i, m])
            delta[i, m : m + 1] = jnp.sum(
                do_ref[i, m].astype(f32) * keep_ref[i, m], axis=0, keepdims=True
            )
            dq[i, m] = jnp.zeros_like(dq[i, m])

    @pl.loop(0, blocks)
    def _(j):
        for n, step in enumerate((blocks // 2, blocks // 2 + 1, blocks - 1)):
            pl.when(j == step)(lambda: hook(n))
        bias[...] = diagonal_bias(info_ref[j])
        mask = mask_rows(info_ref[j, 0:1])
        kn = [jnp.transpose(qkv_ref[j, key[m]]) for m in range(slots)]
        ka = [
            jnp.transpose(jnp.concatenate([qkv_ref[j, key[m]], mask], axis=0)) for m in range(slots)
        ]
        vn = [jnp.transpose(qkv_ref[j, value[m]]) for m in range(slots)]

        def tile(i, m, s):
            p = jnp.exp(s - lse_ref[i, m : m + 1])
            dp = dot(vn[m], do_ref[i, m])
            ds = (p * (dp - delta[i, m : m + 1])).astype(bf16)
            dq[i, m] += dot(qkv_ref[j, key[m]], ds)
            return dot(ds, qn[i, m]), dot(p.astype(bf16), don[i, m])

        start = []
        for m in range(slots):
            start += list(tile(j, m, dot(kn[m], qkv_ref[j, m]) + bias[...]))

        def later(i, carry):
            seg = segment_rows(info_ref[i, 1:2])
            new = []
            for m in range(slots):
                qa = jnp.concatenate([qkv_ref[i, m], seg], axis=0)
                a, b = tile(i, m, dot(ka[m], qa))
                new += [carry[2 * m] + a, carry[2 * m + 1] + b]
            return tuple(new)

        done = lax.fori_loop(j + 1, blocks, later, tuple(start))
        done = [jnp.transpose(value) for value in done]
        if slots == 2:
            shared = (1 - source[1]).astype(f32)
            done[0] = done[0] + done[2] * shared
            done[1] = done[1] + done[3] * shared
        for m in range(slots):
            out_ref[j, key_unit(slots, m)] = done[2 * m].astype(bf16)
            out_ref[j, value_unit(slots, m)] = done[2 * m + 1].astype(bf16)

    @pl.loop(0, blocks)
    def _(i):
        for m in range(slots):
            out_ref[i, m] = (dq[i, m] * HEAD_DIM ** (-0.5)).astype(bf16)


def ffn_body(late, ins, outs, tmp, hook):
    first_ref, down_ref, attn_ref, out_ref, hidden_ref, grad_ref, scale_ref, gain_ref = ins
    gu_grad_ref, down_grad_ref, part_ref, branch_ref = outs
    raw, weight, ffn, dx, sem = tmp
    (x_ref,), (gf_ref,), (late_ref,) = hook.outs[:3]
    cores, rows, width = x_ref.shape
    core = lax.axis_index("core")
    shards, filled = raw.shape[0], width // raw.shape[0]
    columns = weight.shape[1]
    half = columns // 2
    padded = raw.shape[1] * raw.shape[2]

    @pl.loop(0, rows // 128)
    def _(block):
        at = pl.ds(pl.multiple_of(block * 128, 128), 128)
        branch = dot(attn_ref[:filled, at], out_ref[0, :filled], 0, 0)
        for z in range(1, shards):
            here = attn_ref[z * filled : (z + 1) * filled, at]
            branch = branch + dot(here, out_ref[z, :filled], 0, 0)
        branch_ref[at] = branch
        x_ref[core, at] = rms_scale(hidden_ref[at].astype(f32) + branch, gain_ref[...]).astype(bf16)
        gf_ref[core, at] = (scale_ref[at] * grad_ref[at].astype(f32)).astype(bf16)

    hook(0)

    def compact(get):
        for z in range(shards):
            weight[z * filled : (z + 1) * filled] = get(z)[:filled]

    compact(lambda z: first_ref[z].reshape(padded, columns))
    hook(1)
    x = x_ref[...].reshape(cores * rows, width)
    gf = gf_ref[...].reshape(cores * rows, width)

    @pl.loop(0, late.chunks + 1)
    def _(k):
        at = pl.multiple_of(k * columns, columns)
        down = down_ref[pl.ds(pl.multiple_of(k * half, half), half)]

        @pl.when(k < late.chunks)
        def _():
            late.forward(k)

        both = dot(x, weight[...])
        gate, up = both[:, :half], both[:, half:]
        sig = 1.0 / (1.0 + jnp.exp(-gate))
        act = gate * sig
        hidden = (act * up).astype(bf16)
        grad_hidden = dot(gf, down, 1, 1)
        grad_gate = (grad_hidden * up * (sig * (1.0 + gate * (1.0 - sig)))).astype(bf16)
        grad_up = (grad_hidden * act).astype(bf16)
        grads = jnp.concatenate([grad_gate, grad_up], axis=1)
        ffn_now = dot(hidden, down)
        dx_now = dot(grads, weight[...], 1, 1)

        @pl.when(k == 0)
        def _():
            ffn[...] = ffn_now
            dx[...] = dx_now

        @pl.when(k > 0)
        def _():
            ffn[...] += ffn_now
            dx[...] += dx_now

        @pl.when(k == late.chunks)
        def _():
            for c in range(cores):
                part_ref[c, 0] = dx[c * rows : (c + 1) * rows].astype(bf16)
                part_ref[c, 1] = ffn[c * rows : (c + 1) * rows].astype(bf16)
            hook(2)

        load = pltpu.make_async_copy(late_ref.at[:, :, jnp.minimum(k, late.chunks - 1)], raw, sem.at[0])

        @pl.when(k < late.chunks)
        def _():
            late.arrived(k)
            load.start()

        gu_grad = dot(x, grads, 0, 0)
        for z in range(shards):
            gu_grad_ref[z, :filled, pl.ds(at, columns)] = gu_grad[
                z * filled : (z + 1) * filled
            ].astype(bf16)
            if padded > filled:
                gu_grad_ref[z, filled:, pl.ds(at, columns)] = jnp.zeros(
                    (padded - filled, columns), bf16
                )
        down_grad_ref[pl.ds(pl.multiple_of(k * half, half), half)] = dot(hidden, gf, 0, 0).astype(
            bf16
        )

        @pl.when(k < late.chunks)
        def _():
            load.wait()
            compact(lambda z: raw[z].reshape(padded, columns))


def rms_scale(rows, gain):
    return rows * lax.rsqrt(jnp.mean(rows * rows, axis=-1, keepdims=True) + EPSILON) * gain


def norm_back(rows, gain, grad):
    r = lax.rsqrt(jnp.mean(rows * rows, axis=-1, keepdims=True) + EPSILON)
    scaled = gain * grad
    back = r * scaled - rows * (r * r * r) * jnp.mean(scaled * rows, axis=-1, keepdims=True)
    return back, jnp.sum(grad * rows * r, axis=0)


def line_layout(lengths_row, positions):
    seq_ends = jnp.cumsum(lengths_row, dtype=jnp.int32)
    reached = seq_ends[None, :] <= positions[:, None]
    segment = jnp.sum(reached.astype(jnp.int32), axis=1)
    starts = jnp.max(jnp.where(reached, seq_ends[None, :], 0), axis=1)
    return segment, positions - starts, positions < seq_ends[-1]


def project_body(ins, outs, tmp, hook):
    hidden_ref, weight_ref, gain_ref, cos_ref, sin_ref = ins
    sent_ref, normed_ref, full_ref = outs
    reps, units, _, rows = sent_ref.shape
    slots, filled = units // 3, full_ref.shape[0] // weight_ref.shape[0]
    for z in range(weight_ref.shape[0]):
        full_ref[z * filled : (z + 1) * filled] = weight_ref[z, :filled]
    hidden = hidden_ref[...].astype(f32)
    normed = rms_scale(hidden, gain_ref[...]).astype(bf16)
    normed_ref[...] = normed
    cosines, sines = cos_ref[...], sin_ref[...]
    half, columns = HEAD_DIM // 2, full_ref.shape[1]

    def put(kind, head, value):
        slot = head % slots
        unit = (slot, key_unit(slots, slot), value_unit(slots, slot))[kind]
        sent_ref[head // slots, unit] = value

    for head in range(QUERY_HEADS, reps * slots):
        for kind in range(3):
            put(kind, head, jnp.zeros((HEAD_DIM, rows), bf16))
    for start in range(0, columns, 256):
        stop = min(start + 256, columns)
        block = jnp.transpose(dot(normed, full_ref[:, start:stop]))
        for head in range(start // HEAD_DIM, stop // HEAD_DIM):
            at = head * HEAD_DIM - start
            a, b = block[at : at + half], block[at + half : at + HEAD_DIM]
            if head < QUERY_HEADS:
                scale = HEAD_DIM ** (-0.5)
                put(
                    0,
                    head,
                    (
                        jnp.concatenate(
                            [a * cosines - b * sines, b * cosines + a * sines], axis=0
                        )
                        * scale
                    ).astype(bf16),
                )
            elif head < QUERY_HEADS + KEY_VALUE_HEADS:
                value = jnp.concatenate(
                    [a * cosines - b * sines, b * cosines + a * sines], axis=0
                ).astype(bf16)
                for m in range(GROUP):
                    put(1, (head - QUERY_HEADS) * GROUP + m, value)
            else:
                value = block[at : at + HEAD_DIM].astype(bf16)
                for m in range(GROUP):
                    put(2, (head - QUERY_HEADS - KEY_VALUE_HEADS) * GROUP + m, value)
        if start < QUERY_HEADS * HEAD_DIM <= stop:
            hook(0)
    hook(1)


def project_back_body(ins, outs, tmp, hook):
    (grads_ref, cos_ref, sin_ref, weight_ref, hidden_ref, normed_ref, gain_ref, base_ref) = ins[:8]
    vectors_ref = ins[8]
    sent_ref, weight_grad_ref, vectors_grad_ref = outs
    (dt,) = tmp
    slots, half = grads_ref.shape[1] // 3, HEAD_DIM // 2
    cosines, sines = cos_ref[...], sin_ref[...]

    def get(kind, head):
        slot = head % slots
        unit = (slot, key_unit(slots, slot), value_unit(slots, slot))[kind]
        return grads_ref[head // slots, unit].astype(f32)

    def back(value):
        a, b = value[:half], value[half:]
        return jnp.concatenate([a * cosines + b * sines, b * cosines - a * sines], axis=0)

    for head in range(QUERY_HEADS):
        dt[head * HEAD_DIM : (head + 1) * HEAD_DIM] = back(get(0, head)).astype(bf16)
    for group in range(KEY_VALUE_HEADS):
        for kind in (1, 2):
            value = get(kind, group * GROUP)
            for head in range(group * GROUP + 1, (group + 1) * GROUP):
                if slots != 2 or head % 2 == 0:
                    value = value + get(kind, head)
            if kind == 1:
                value = back(value)
            at = (QUERY_HEADS + (kind - 1) * KEY_VALUE_HEADS + group) * HEAD_DIM
            dt[at : at + HEAD_DIM] = value.astype(bf16)
    grad = dot(dt[...], weight_ref[...], 0, 1)
    norm_grad, gain_grad = norm_back(hidden_ref[...].astype(f32), gain_ref[...], grad)
    index = lax.broadcasted_iota(jnp.int32, vectors_ref.shape, 0)
    vectors = jnp.where(index == 0, gain_grad[None], vectors_ref[...])
    piece = vectors_grad_ref.shape[2]
    for z in range(vectors_grad_ref.shape[0]):
        vectors_grad_ref[z] = vectors[:, z * piece : (z + 1) * piece]
    total = (base_ref[...] + norm_grad).astype(bf16)
    devices, per_pair = sent_ref.shape[:2]
    sent_ref[...] = total.reshape(sent_ref.shape)
    hook(0)
    shards, chips, cores, parts, unit, columns = weight_grad_ref.shape
    filled = normed_ref.shape[1] // shards
    places = [(c, k, p) for c in range(chips) for k in range(cores) for p in range(parts)]
    for start in range(0, columns, 256):
        stop = min(start + 256, columns)
        block = dot(normed_ref[...], dt[start:stop], 0, 1)
        for z in range(shards):
            for r, place in enumerate(places):
                size = max(0, min(unit, filled - r * unit))
                at = z * filled + r * unit
                here = weight_grad_ref.at[z, *place]
                if size:
                    here[:size, start:stop] = block[at : at + size].astype(bf16)
                if size < unit:
                    here[size:, start:stop] = jnp.zeros((unit - size, stop - start), bf16)


def prepare_body(ins, outs, tmp, hook):
    to_slot_ref, cotangent_ref, gate_ref, up_ref, down_ref = ins
    slots_ref, first_ref, late_ref, down_rows_ref = outs
    hook(0)
    sent = dot(to_slot_ref[...], cotangent_ref[...], 1, 1).astype(bf16)
    slots_ref[...] = sent.reshape(slots_ref.shape)
    chips, unit = first_ref.shape[:2]
    filled, half = gate_ref.shape[0], gate_ref.shape[1] // 2
    for chip in range(chips):
        size = max(0, min(unit, filled - chip * unit))
        for chunk in range(late_ref.shape[1] + 1):
            target = late_ref.at[chip, chunk - 1] if chunk else first_ref.at[chip]
            at = pl.multiple_of(lax.axis_index("core") * half + chunk * FF_CHUNK, FF_CHUNK)
            for which, source in enumerate((gate_ref, up_ref)):
                columns = pl.ds(which * FF_CHUNK, FF_CHUNK)
                if size:
                    rows = pl.ds(chip * unit, size)
                    target[:size, columns] = source[rows, pl.ds(at, FF_CHUNK)]
                if size < unit:
                    target[size:, columns] = jnp.zeros((unit - size, FF_CHUNK), bf16)
    count = down_rows_ref.shape[0]
    for start in range(0, count, 128):
        stop = min(start + 128, count)
        down_rows_ref[start:stop] = jnp.transpose(down_ref[:, start:stop])


def grads_body(ins, outs, tmp, hook):
    (parts_ref, hidden_ref, branch_ref, grad_ref, scale_ref, logit_ref, gain_ref, router_ref) = ins[:8]
    out_weight_ref, attn_ref = ins[8:]
    sent_ref, result_ref, base_ref, vectors_ref, out_grad_ref = outs
    (grad_attn,) = tmp
    rows, width = hidden_ref.shape
    group = 64 // result_ref.shape[1]

    def block(b, carry):
        at = pl.ds(pl.multiple_of(b * 64, 64), 64)
        hidden, branch = hidden_ref[at].astype(f32), branch_ref[at]
        grad, scale = grad_ref[at].astype(f32), scale_ref[at]
        grad_normed = parts_ref[0, 0, at].astype(f32) + parts_ref[1, 0, at].astype(f32)
        ffn = parts_ref[0, 1, at].astype(f32) + parts_ref[1, 1, at].astype(f32)
        total = branch + ffn
        result = (hidden + scale * total).astype(bf16)
        result_ref[pl.ds(b * group, group)] = result.reshape(group, *result_ref.shape[1:])
        grad_logit = logit_ref[at] * jnp.sum(grad * total, axis=1, keepdims=True)
        grad_middle, gain_grad = norm_back(hidden + branch, gain_ref[...], grad_normed)
        grad_attn[at] = (scale * grad + grad_middle).astype(bf16)
        base_ref[at] = grad + grad_middle + grad_logit * router_ref[...]
        router_grad = jnp.sum(grad_logit * hidden, axis=0)
        return carry[0] + gain_grad[None], carry[1] + router_grad[None]

    zero = jnp.zeros((1, width), f32)
    gain_grad, router_grad = lax.fori_loop(0, rows // 64, block, (zero, zero))
    index = lax.broadcasted_iota(jnp.int32, vectors_ref.shape, 0)
    vectors_ref[...] = jnp.where(index == 1, gain_grad, jnp.where(index == 2, router_grad, 0.0))
    reps, slots = sent_ref.shape[:2]
    shards, filled = out_weight_ref.shape[0], width // out_weight_ref.shape[0]
    for z in range(shards):
        piece = dot(out_weight_ref[z, :filled], grad_attn[...], 1, 1).astype(bf16)
        start = z * filled
        while start < (z + 1) * filled:
            head = start // HEAD_DIM
            stop = min((head + 1) * HEAD_DIM, (z + 1) * filled)
            rows_of_head = pl.ds(start - head * HEAD_DIM, stop - start)
            sent_ref[head // slots, head % slots, rows_of_head] = piece[
                start - z * filled : stop - z * filled
            ]
            start = stop
    for head in range(width // HEAD_DIM, reps * slots):
        sent_ref[head // slots, head % slots] = jnp.zeros(sent_ref.shape[2:], bf16)
    hook(0)
    _, chips, cores, parts, unit, _ = out_grad_ref.shape
    places = [(c, k, p) for c in range(chips) for k in range(cores) for p in range(parts)]
    for z in range(shards):
        piece = dot(attn_ref[z * filled : (z + 1) * filled], grad_attn[...])
        for r, place in enumerate(places):
            size = max(0, min(unit, filled - r * unit))
            here = out_grad_ref.at[z, *place]
            if size:
                here[:size] = piece[r * unit : r * unit + size].astype(bf16)
            if size < unit:
                here[size:] = jnp.zeros((unit - size, width), bf16)


def finalize_kernel(*refs):
    gate_up_ref, out_ref, down_ref, qkv_ref, slot_ref, result_ref, grad_ref = refs[:7]
    gate, up, out, query, down, key, value, result, grad = refs[7:]
    cores, rows, columns = gate_up_ref.shape[1:]
    query_end = query.shape[1]

    @pl.when(pl.program_id(0) == 0)
    def _():
        slots = lax.broadcasted_iota(jnp.int32, (result_ref.shape[0], slot_ref.shape[1]), 0)
        to_slot = jnp.where(slots == slot_ref[...], 1.0, 0.0).astype(bf16)
        result[...] = dot(result_ref[...], to_slot, 0, 0).astype(bf16)
        grad[...] = dot(grad_ref[...], to_slot, 0, 0).astype(bf16)
        down[...] = jnp.transpose(down_ref[...]).astype(f32)
        heads = jnp.transpose(qkv_ref[:, query_end:])[:, : key.shape[1]].astype(f32)
        key[...] = heads[: key.shape[0]]
        value[...] = heads[key.shape[0] :]

    half = columns // 2
    for core in range(cores):
        for start in range(0, columns, 2 * FF_CHUNK):
            at = core * half + start // 2
            middle = start + FF_CHUNK
            gate[:, at : at + FF_CHUNK] = gate_up_ref[0, core, :, start:middle].astype(f32)
            up[:, at : at + FF_CHUNK] = gate_up_ref[0, core, :, middle : middle + FF_CHUNK].astype(f32)
    out[...] = out_ref[0].astype(f32)
    at = pl.ds(pl.multiple_of(pl.program_id(0) * rows, rows), rows)
    query[...] = qkv_ref[at, :query_end].astype(f32)


def finalize(gate_up, out, down, qkv, slot_of_row, result, grad, shard_rows, key_width):
    chips, rows = gate_up.shape[0], gate_up.shape[2]
    width, hidden = out.shape[2], gate_up.shape[3]
    by_chip = [(shard_rows, hidden), (shard_rows, hidden), (shard_rows, width), (shard_rows, width)]
    whole = [((width, down.shape[0]), f32)] + [((key_width, shard_rows), f32)] * 2
    whole += [((width, result.shape[0]), bf16)] * 2

    def full(shape):
        return pl.BlockSpec(tuple(shape), lambda c: (0,) * len(shape))

    slots = slot_of_row[None]
    totals = pl.pallas_call(
        finalize_kernel,
        grid=(chips,),
        in_specs=[
            pl.BlockSpec((1, 2, rows, hidden), lambda c: (c, 0, 0, 0)),
            pl.BlockSpec((1, rows, width), lambda c: (c, 0, 0)),
        ]
        + [full(array.shape) for array in (down, qkv, slots, result, grad)],
        out_specs=[pl.BlockSpec((rows, shape[1]), lambda c: (c, 0)) for shape in by_chip]
        + [full(shape) for shape, _ in whole],
        out_shape=[jax.ShapeDtypeStruct(shape, f32) for shape in by_chip]
        + [jax.ShapeDtypeStruct(shape, dtype) for shape, dtype in whole],
        name="finalize",
    )(gate_up, out, down, qkv, slots, result, grad)
    return list(totals[:4]) + [jnp.transpose(total) for total in totals[4:]]


def rounded_up(value, unit):
    return -(-value // unit) * unit


def local(
    sizes,
    hidden_in,
    cotangent,
    destination,
    seq_lengths,
    gate_mask,
    query_weight,
    key_matrix,
    value_matrix,
    out_weight,
    gate_weight,
    up_weight,
    down_weight,
    attn_gain,
    ffn_gain,
    router_weight,
):
    rows, width = hidden_in.shape
    chips, shards = sizes["chip"], sizes["shard"]
    reps = 2 * chips
    devices = reps * shards
    per_pair = rows // devices
    slots = -(-QUERY_HEADS // reps)
    padded_heads = slots * reps
    chip, core, shard = lax.axis_index("chip"), lax.axis_index("core"), lax.axis_index("shard")
    rep = lax.axis_index(REP)
    shard_rows = query_weight.shape[0]
    rep_unit = rounded_up(-(-shard_rows // reps), 8)
    padded = rep_unit * reps
    chip_unit = padded // chips
    ff_half = gate_weight.shape[1] // 2
    chunks = ff_half // FF_CHUNK

    def padded_rows(array):
        return jnp.pad(array, ((0, padded - shard_rows), (0, 0)))

    qkv_shard = padded_rows(jnp.concatenate([query_weight, key_matrix, value_matrix], axis=1))
    qkv_shard = qkv_shard.reshape(reps, rep_unit, -1)
    out_shard = padded_rows(out_weight).reshape(reps, rep_unit, width)
    down_unit = down_weight.shape[0] // chips
    vectors = jnp.stack([attn_gain, ffn_gain, router_weight]).astype(f32)
    vectors = jnp.pad(vectors, ((0, 5), (0, 0)))

    row_index = jnp.arange(rows, dtype=jnp.int32)
    target = destination // rows
    earlier = (target[None, :] == target[:, None]) & (row_index[None, :] < row_index[:, None])
    slot_of_row = target * per_pair + jnp.sum(earlier.astype(jnp.int32), axis=1)
    to_slot = slot_of_row[None, :] == row_index[:, None]
    to_slot_b = to_slot.astype(bf16)
    place_sent = jnp.sum(jnp.where(to_slot, (destination % rows)[None, :], 0), axis=1)
    place_sent = place_sent.reshape(devices, 1, per_pair)
    place_sent = jnp.pad(place_sent, ((0, 0), (0, 0), (0, 128 - per_pair)))

    def by_slot(tokens):
        tokens = jnp.dot(to_slot_b, tokens, preferred_element_type=f32).astype(bf16)
        return tokens.reshape(devices, per_pair, width)

    first_type = jax.ShapeDtypeStruct((chips, chip_unit, 2 * FF_CHUNK), bf16)
    late_type = jax.ShapeDtypeStruct((chips, chunks - 1, chip_unit, 2 * FF_CHUNK), bf16)
    tokens_type = jax.ShapeDtypeStruct((devices, per_pair, width), bf16)
    got_hidden, got_place, vectors_got, qkv_full, grad_slots, first_shard, late_shard, down_shard = run(
        1,
        "first",
        sizes,
        [
            AllToAll(sizes, by_slot(hidden_in), ALL, late=True).at(0),
            AllToAll(sizes, place_sent, ALL, late=True).at(0),
            AllToAll(sizes, vectors, ("shard",), spread=True),
            Gather(sizes, qkv_shard, REP, "both"),
        ],
        Compute(
            prepare_body,
            [
                to_slot_b,
                jnp.transpose(cotangent),
                gate_weight,
                up_weight,
                jnp.transpose(down_weight),
            ],
            [
                tokens_type,
                first_type,
                late_type,
                jax.ShapeDtypeStruct(down_weight.shape, bf16),
            ],
        ),
    )
    down_shard = down_shard.reshape(chips, down_unit, width)
    hidden = got_hidden.reshape(rows, width)
    place = got_place[:, 0, :per_pair].reshape(rows)
    qkv_full = qkv_full.reshape(shards, padded, -1)
    vectors_full = jnp.transpose(vectors_got[:, :3], (1, 0, 2)).reshape(3, width)
    gain_one, gain_two, full_router = vectors_full[0], vectors_full[1], vectors_full[2]
    router_logit = jnp.sum(hidden.astype(f32) * full_router, axis=1)
    gate_value = jax.nn.sigmoid(router_logit)

    positions = rep * rows + place
    segment, within, is_valid = line_layout(seq_lengths[0], positions)
    here = place[:, None] == row_index[None, :]
    gate_here = jnp.sum(jnp.where(here, gate_mask[None, :], 0), axis=1)
    active = is_valid & (gate_here == 1)
    key_code = jnp.where(active, segment, -1)
    active_f = active.astype(f32)
    branch_scale = (active_f * gate_value)[:, None]
    logit_scale = branch_scale * (1.0 - gate_value)[:, None]
    info = jnp.pad(jnp.stack([key_code, segment, place]), ((0, 5), (0, 0)))
    steps = jnp.arange(HEAD_DIM // 2).astype(f32)
    frequency = jnp.power(ROPE_BASE, -2.0 * steps / HEAD_DIM)
    angles = frequency[:, None] * within.astype(f32)[None, :]
    cosines, sines = jnp.cos(angles), jnp.sin(angles)

    heads_shape = (reps, 3 * slots, HEAD_DIM, rows)
    heads_type = jax.ShapeDtypeStruct(heads_shape, bf16)
    first_z, late_z, out_z, info_got, qkv_got, _, first_normalized, qkv_weights = run(
        2,
        "project",
        sizes,
        [
            Gather(sizes, first_shard, ("chip",), "z"),
            Gather(sizes, late_shard, ("chip",), "z"),
            Gather(sizes, out_shard, REP, "z"),
            AllToAll(sizes, info, REP, spread=True),
            Heads(sizes, heads_type, True, 0).at(0, 1),
        ],
        Compute(
            project_body,
            [hidden, qkv_full, gain_one[None], cosines, sines],
            [
                heads_type,
                jax.ShapeDtypeStruct((rows, width), bf16),
                jax.ShapeDtypeStruct((width, qkv_full.shape[2]), bf16),
            ],
        ),
    )
    slot_type = jax.ShapeDtypeStruct((reps, slots, HEAD_DIM, rows), bf16)
    home = Stepwise(sizes, slot_type, 0)
    first_full, down_full, out_full, got_grad, att_home, _, att_keep, lse = run(
        3,
        "attend",
        sizes,
        [
            Gather(sizes, first_z, ("chip",), "plane").at(1),
            Gather(sizes, down_shard, ("chip",), "both", half=True).at(0, 2),
            Gather(sizes, out_z, REP, "plane").at(1),
            AllToAll(sizes, grad_slots, ALL),
            home,
        ],
        Compute(
            functools.partial(forward_body, home),
            [qkv_got, info_got],
            [
                slot_type,
                jax.ShapeDtypeStruct(slot_type.shape, f32),
                jax.ShapeDtypeStruct((reps, 8, rows), f32),
            ],
            [
                pltpu.VMEM((rows, rows), f32),
                pltpu.VMEM((slots, HEAD_DIM, rows), f32),
                pltpu.VMEM((8, rows), f32),
            ],
        ),
    )
    attn_out_t = att_home.reshape(padded_heads * HEAD_DIM, rows)
    out_rows = out_full.reshape(shards, padded, width)
    down = down_full.reshape(ff_half, width)
    grad_out = got_grad.reshape(rows, width)
    late = ChunkGather(sizes, late_z)
    parts_type = jax.ShapeDtypeStruct((2, 2, rows, width), bf16)
    own_type = jax.ShapeDtypeStruct((rows, width), bf16)
    _, _, _, parts_got, gate_up_grad, down_grad, _, attn_branch = run(
        4,
        "feed_forward",
        sizes,
        [
            Swap(sizes, own_type).at(0, 1),
            Swap(sizes, own_type).at(0, 1),
            late,
            AllToAll(sizes, parts_type, ("core",), late=True, source=2).at(2),
        ],
        Compute(
            functools.partial(ffn_body, late),
            [
                first_full,
                down,
                attn_out_t,
                out_rows,
                hidden,
                grad_out,
                branch_scale,
                gain_two[None],
            ],
            [
                jax.ShapeDtypeStruct((shards, padded, 2 * ff_half), bf16),
                jax.ShapeDtypeStruct(down.shape, bf16),
                parts_type,
                jax.ShapeDtypeStruct((rows, width), f32),
            ],
            [
                pltpu.VMEM((shards, chips, chip_unit, 2 * FF_CHUNK), bf16),
                pltpu.VMEM((width, 2 * FF_CHUNK), bf16),
                pltpu.VMEM((2 * rows, width), f32),
                pltpu.VMEM((2 * rows, width), f32),
                pltpu.SemaphoreType.DMA((1,)),
            ],
        ),
        vmem=67_000_000,
    )
    parts = 2 if chips == 4 else 1
    out_grad_type = jax.ShapeDtypeStruct((shards, chips, 2, parts, rep_unit // parts, width), bf16)
    grad_got, _, result, base, vector_grads, out_grad = run(
        6,
        "grads",
        sizes,
        [AllToAll(sizes, slot_type, REP, late=True, source=0).at(0)],
        Compute(
            grads_body,
            [
                parts_got,
                hidden,
                attn_branch,
                grad_out,
                branch_scale,
                logit_scale,
                gain_two[None],
                full_router[None],
                out_rows,
                attn_out_t,
            ],
            [
                slot_type,
                tokens_type,
                jax.ShapeDtypeStruct((rows, width), f32),
                jax.ShapeDtypeStruct((8, width), f32),
                out_grad_type,
            ],
            [pltpu.VMEM((rows, width), bf16)],
        ),
    )
    gate_up_grad = gate_up_grad.reshape(shards, chips, parts, chip_unit // parts, 2 * ff_half)
    down_grad = down_grad.reshape(shards // 2, chips, parts, down_unit // parts, width)
    gate_up_sum, down_sum, out_sum, home_out, heads_home, _ = run(
        7,
        "attend_back",
        sizes,
        [
            Reduce(sizes, gate_up_grad, ("plane", "shard")).at(0, 2),
            Reduce(sizes, down_grad, ("plane",)).at(1),
            Reduce(sizes, out_grad, ("pair", "plane")).at(1),
            AllToAll(sizes, result, ALL),
            Heads(sizes, heads_type, False, 0),
        ],
        Compute(
            backward_body,
            [qkv_got, grad_got, att_keep, lse, info_got],
            [heads_type],
            [
                pltpu.VMEM((rows, rows), f32),
                pltpu.VMEM((reps, slots, HEAD_DIM, rows), f32),
                pltpu.VMEM((reps, slots, rows, HEAD_DIM), bf16),
                pltpu.VMEM((reps, slots, rows, HEAD_DIM), bf16),
                pltpu.VMEM((reps, 8, rows), f32),
            ],
        ),
    )

    qkv_columns = qkv_weights.shape[1]
    qkv_grad_type = jax.ShapeDtypeStruct(
        (shards, chips, 2, parts, rep_unit // parts, qkv_columns), bf16
    )
    vectors_type = jax.ShapeDtypeStruct((shards, 8, shard_rows), f32)
    qkv_home, gate_up_home, down_home, out_home, home_grad, vectors_home = run(
        8,
        "project_back",
        sizes,
        [
            Reduce(sizes, qkv_grad_type, ("pair", "plane", "shard", "spread"), late=True, source=1),
            Reduce(sizes, gate_up_sum, ("spread",)),
            Reduce(sizes, down_sum, ("shard", "spread"), half=True),
            Reduce(sizes, out_sum, ("shard", "spread")),
            AllToAll(sizes, tokens_type, ALL, late=True, source=0).at(0),
            AllToAll(sizes, vectors_type, ALL, by_shard=True, late=True, source=2).at(0),
        ],
        Compute(
            project_back_body,
            [
                heads_home,
                cosines,
                sines,
                qkv_weights,
                hidden,
                first_normalized,
                gain_one[None],
                base,
                vector_grads,
            ],
            [tokens_type, qkv_grad_type, vectors_type],
            [pltpu.VMEM((qkv_columns, rows), bf16)],
        ),
    )[:6]
    totals = finalize(
        gate_up_home.reshape(chips, 2, chip_unit, 2 * ff_half),
        out_home.reshape(chips, chip_unit, width),
        down_home.reshape(chips * down_unit, width),
        qkv_home.reshape(padded, qkv_columns),
        slot_of_row,
        home_out.reshape(rows, width),
        home_grad.reshape(rows, width),
        shard_rows,
        key_matrix.shape[1],
    )
    gate_total, up_total, out_total, query_total, down_total, key_total, value_total = totals[:7]
    vector_total = jnp.sum(vectors_home, axis=0)

    return (
        *totals[7:],
        query_total,
        key_total,
        value_total,
        out_total,
        gate_total,
        up_total,
        down_total,
        vector_total[0],
        vector_total[1],
        vector_total[2],
    )


def solution(mesh):
    reps, shards = mesh.shape["rep"], mesh.shape["shard"]
    sizes = {"chip": reps // 2, "core": 2, "shard": shards}
    split_mesh = Mesh(mesh.devices.reshape(reps // 2, 2, shards), ALL)
    tokens, tokens_1d = P(ALL, None), P(ALL)
    weight, vector = P("shard", None), P("shard")
    return jax.shard_map(
        functools.partial(local, sizes),
        mesh=split_mesh,
        in_specs=(tokens, tokens, tokens_1d, weight, tokens_1d) + (weight,) * 7 + (vector,) * 3,
        out_specs=(tokens, tokens) + (weight,) * 7 + (vector,) * 3,
        check_vma=False,
    )
```
